32 devices in a mesh: row: 4 (over x, core), col: 8 (over z, y).
Axes of the slice: x: 2, y: 2, z: 4, core: 2. Of those that a mesh axis runs over, the one named last changes fastest.
Arguments:
- object_slices: float32 [2, 2, 1024, 2048], P(None, None, 'row', 'col'), may hold values from -5 to 5
- probe: float32 [2, 128, 128], replicated, may hold values from -6 to 6
- amplitudes: float32 [4, 8, 16, 128, 128], P('row', 'col'), may hold values from 0.3 to 3
- scan_pos: int32 [2, 4, 8, 16], P(None, 'row', 'col'), may hold values from 0 to 2047, as said below
- scan_count: int32 [4, 8], P('row', 'col'), may hold values from 0 to 16, as said below
Outputs:
- object_new: float32 [2, 2, 1024, 2048], P(None, None, 'row', 'col')
The draws below stay inside these ranges and needn't reach their ends.
Inputs may be any that keep to these rules, and one draw needn't show every extreme that they name: `scan_pos`: entry [0, i, j, k] is the pixel row and [1, i, j, k] the pixel column of the centre of slot k of tile (i, j); the centre lies within that tile's 256 x 256 pixels, also for slots that are not live. The live scans of a tile are its first scan_count slots; in every tile row the counts of its 8 tiles sum to exactly 64, and some tile of every row holds 16 scans.
All inputs are finite; a program needn't handle non-finite values.
Results may differ from the reference program's by a relative error of at most 0.00029.
Values sent between devices are 32-bit elements; how exact they have to be, the bound alone decides.
No kernel may reach another device: no remote copies, remote signals or barrier semaphores. Data moves between devices by JAX's collectives and lax.ppermute only.
A program may use at most 128 MiB of HBM per device.

```python
import math
import jax
import jax.numpy as jnp
from jax import lax

P_SIZE = 128
SLICES = 2
ITERS = 2
TR = 256
TC = 256
OWN_CAP = 16
GRID_R = 4
GRID_C = 8
NR = 1024
NC = 2048


def draw_scan_count(key, part):

    def one_row(row_key):
        key_order, key_first = jax.random.split(row_key)
        column_order = jax.random.permutation(key_order, GRID_C)
        first_half = jax.random.randint(key_first, (GRID_C // 2,), 0, OWN_CAP + 1)
        first_half = first_half.at[0].set(OWN_CAP)
        paired = jnp.stack([first_half, OWN_CAP - first_half], axis=1).reshape(GRID_C)
        return jnp.zeros((GRID_C,), jnp.int32).at[column_order].set(paired.astype(jnp.int32))
    return jax.vmap(one_row)(jax.random.split(jax.random.fold_in(key, 11), GRID_R))


def draw_scan_pos(key, part):
    key_rows, key_cols = jax.random.split(jax.random.fold_in(key, 23))
    offset_rows = jax.random.randint(key_rows, (GRID_R, GRID_C, OWN_CAP), 0, TR)
    offset_cols = jax.random.randint(key_cols, (GRID_R, GRID_C, OWN_CAP), 0, TC)
    offset_rows = offset_rows.at[GRID_R - 1, GRID_C - 1, 0].set(TR - 1).at[0, 0, 1].set(0)
    offset_cols = offset_cols.at[GRID_R - 1, GRID_C - 1, 0].set(TC - 1).at[0, 0, 1].set(0)
    start_rows = (jnp.arange(GRID_R, dtype=jnp.int32) * TR)[:, None, None]
    start_cols = (jnp.arange(GRID_C, dtype=jnp.int32) * TC)[None, :, None]
    return jnp.stack([offset_rows + start_rows, offset_cols + start_cols]).astype(jnp.int32)


def block_scale(stream_key, shape, shards, smallest, high):
    factor_of, own = 1.0, jax.random.fold_in(stream_key, 6)
    for dim, shards_of in shards:
        steps = jnp.exp(jax.random.uniform(jax.random.fold_in(own, dim), (shards_of,), jnp.float32, smallest / len(shards), high / len(shards)))
        factor_of = factor_of * jnp.repeat(steps, shape[dim] // shards_of).reshape([-1 if axis == dim else 1 for axis in range(len(shape))])
    return factor_of


def centred(rng, extent, width, most, pieces=(), kind=jnp.bfloat16):
    drawn = width * jax.random.normal(rng, extent, jnp.float32)
    if pieces:
        drawn = drawn * block_scale(rng, extent, pieces, -0.22, 0.18)
    return jnp.clip(drawn, -most, most).astype(kind)


def setup_inputs(seed: int = 0) -> dict:
    keys = jax.random.split(jax.random.key(seed), 6)
    object_slices = centred(keys[0], (SLICES, 2, NR, NC), 0.7, 5.0, ((2, 4), (3, 8)), jnp.float32)
    probe = centred(keys[1], (2, P_SIZE, P_SIZE), 1.0, 6.0, (), jnp.float32)
    amplitudes = jnp.clip(jnp.exp(math.log(3.0) - 2.3025851 * jax.random.uniform(keys[2], (GRID_R, GRID_C, OWN_CAP, P_SIZE, P_SIZE), jnp.float32) ** block_scale(keys[2], (GRID_R, GRID_C, OWN_CAP, P_SIZE, P_SIZE), ((0, 4), (1, 8)), -0.2, 0.2)), 0.3, 3.0)
    scan_pos = draw_scan_pos(jax.random.fold_in(keys[5], 71), 0)
    scan_count = draw_scan_count(jax.random.fold_in(keys[5], 71), 0)
    return {"object_slices": object_slices, "probe": probe, "amplitudes": amplitudes, "scan_pos": scan_pos, "scan_count": scan_count}


modulus_offset = 0.5
fresnel_scale = 0.9

def propagator(frame_size, dtype):
    positions = jnp.arange(frame_size, dtype=jnp.int32)
    frequency = jnp.where(positions < frame_size // 2, positions, positions - frame_size).astype(dtype)
    phase = math.pi * fresnel_scale * (frequency[:, None] ** 2 + frequency[None, :] ** 2) / frame_size
    return jnp.cos(phase) + 1j * jnp.sin(phase)

def slot_gradients(patches, local_amps, probe_c, prop):
    layers = patches.shape[1]
    objects = [patches[:, layer_id, 0] + 1j * patches[:, layer_id, 1] for layer_id in range(layers)]
    incident = [jnp.broadcast_to(probe_c, objects[0].shape)]
    for layer_id in range(layers - 1):
        exit_wave = incident[layer_id] * objects[layer_id]
        spectrum = jnp.fft.fft2(exit_wave, norm='ortho')
        incident.append(jnp.fft.ifft2(prop * spectrum, norm='ortho'))
    psi = jnp.fft.fft2(incident[-1] * objects[-1], norm='ortho')
    modulus = jnp.sqrt(jnp.real(psi) ** 2 + jnp.imag(psi) ** 2 + modulus_offset)
    residual = psi * (1.0 - local_amps / modulus)
    back_wave = jnp.fft.ifft2(residual, norm='ortho')
    gradients = [None] * layers
    for layer_id in reversed(range(layers)):
        grad_c = jnp.conj(incident[layer_id]) * back_wave
        gradients[layer_id] = jnp.stack([jnp.real(grad_c), jnp.imag(grad_c)], axis=1)
        if layer_id > 0:
            adjoint = jnp.conj(objects[layer_id]) * back_wave
            spectrum = jnp.fft.fft2(adjoint, norm='ortho')
            back_wave = jnp.fft.ifft2(jnp.conj(prop) * spectrum, norm='ortho')
    return jnp.stack(gradients, axis=1)

def reference(object_slices, probe, amplitudes, scan_pos, scan_count):
    frame_size = probe.shape[-1]
    half_frame = frame_size // 2
    probe_c = probe[0] + 1j * probe[1]
    prop = propagator(frame_size, probe.dtype)
    tiles = GRID_R * GRID_C
    centre_rows = scan_pos[0].reshape(tiles, OWN_CAP).astype(jnp.int32)
    centre_cols = scan_pos[1].reshape(tiles, OWN_CAP).astype(jnp.int32)
    amps_all = amplitudes.reshape(tiles, OWN_CAP, frame_size, frame_size)
    counts = scan_count.reshape(tiles).astype(jnp.int32)
    slot_ids = jnp.arange(OWN_CAP, dtype=jnp.int32)
    zero_index = jnp.zeros((), jnp.int32)
    current = object_slices
    for iteration in range(ITERS):
        padded = jnp.pad(current, ((0, 0), (0, 0), (half_frame, half_frame), (half_frame, half_frame)))

        def tile_step(tile_id, accumulator):
            rows_here = centre_rows[tile_id]
            cols_here = centre_cols[tile_id]
            patches = jax.vmap(lambda row_at, col_at: lax.dynamic_slice(padded, (zero_index, zero_index, row_at, col_at), (SLICES, 2, frame_size, frame_size)))(rows_here, cols_here)
            live_mask = (slot_ids < counts[tile_id]).astype(padded.dtype)
            gradients = slot_gradients(patches, amps_all[tile_id], probe_c, prop) * live_mask[:, None, None, None, None]

            def add_one(item, inner):
                corner = (zero_index, zero_index, rows_here[item], cols_here[item])
                current_block = lax.dynamic_slice(inner, corner, (SLICES, 2, frame_size, frame_size))
                return lax.dynamic_update_slice(inner, current_block + gradients[item], corner)
            return lax.fori_loop(0, OWN_CAP, add_one, accumulator)
        accumulator = lax.fori_loop(0, tiles, tile_step, jnp.zeros_like(padded))
        current = current - accumulator[:, :, half_frame:half_frame + NR, half_frame:half_frame + NC]
    return current
```

```python
import functools
import math

import jax
import jax.numpy as jnp
import ml_dtypes
import numpy as np
from jax import lax
from jax.experimental import pallas as pl
from jax.experimental.pallas import tpu as pltpu
from jax.sharding import PartitionSpec as P

ITERS = 2
LANES = 128
GROUP = 4

modulus_offset = 0.5
fresnel_scale = 0.9


def split_table(table):
    high = table.astype(np.float32).astype(ml_dtypes.bfloat16)
    low = (table - high.astype(np.float64)).astype(np.float32).astype(ml_dtypes.bfloat16)
    return high, low


def transform_tables(frame_size):
    positions = np.arange(frame_size)
    dft = np.exp(-2j * math.pi * (positions[:, None] * positions[None, :] % frame_size) / frame_size)
    dft = dft / math.sqrt(frame_size)
    frequency = np.where(positions < frame_size // 2, positions, positions - frame_size)
    phase = np.exp(1j * math.pi * fresnel_scale * frequency.astype(np.float64) ** 2 / frame_size)
    hop = (np.conj(dft) * phase[None, :]) @ dft
    tables = []
    for matrix in (dft, hop):
        re, im = matrix.real, matrix.imag
        right = np.block([[re, im], [-im, re]])
        left = np.block([[re, -im], [im, re]])
        for table in (right, left):
            tables.extend(split_table(table))
    return np.stack(tables)


DFT_RIGHT, DFT_LEFT, HOP_RIGHT, HOP_LEFT = 0, 2, 4, 6


def neighbour(values, axis, step):
    count = lax.axis_size(axis)
    pairs = [(i, i + step) for i in range(count) if 0 <= i + step < count]
    return lax.ppermute(values, axis, pairs)


def lane_ids(shape):
    return lax.broadcasted_iota(jnp.int32, shape, len(shape) - 1)


def swap_halves(values):
    return pltpu.roll(values, LANES // 2, values.ndim - 1)


def vmem():
    return pl.BlockSpec(memory_space=pltpu.VMEM)


def smem():
    return pl.BlockSpec(memory_space=pltpu.SMEM)


def split(values):
    high = values.astype(jnp.bfloat16)
    return high, (values - high.astype(jnp.float32)).astype(jnp.bfloat16)


def dot(a, b):
    return jnp.dot(a, b, preferred_element_type=jnp.float32)


def pack_kernel(object_ref, left_ref, right_ref, up_ref, down_ref):
    planes, rows, cols = object_ref.shape
    half = rows // 2
    low = lane_ids((half, LANES)) < LANES // 2
    for plane in range(planes):
        first = object_ref[plane, :, 0:LANES]
        last = object_ref[plane, :, cols - LANES : cols]
        left_ref[plane] = jnp.where(low, first[half:], swap_halves(first[:half]))
        right_ref[plane] = jnp.where(low, swap_halves(last[:half]), last[half:])
        up_ref[plane] = object_ref[plane, 0:64, :]
        down_ref[plane] = object_ref[plane, rows - 64 : rows, :]


def gradients(pos_ref, amps_ref, probe_ref, tables_ref, field_ref, grad_ref, work):
    frame = probe_ref.shape[-1]
    o0, o1, inc, wave = work
    count = pos_ref[2, 0]
    lanes = lane_ids((frame, LANES))

    grad_ref[...] = jnp.zeros_like(grad_ref)

    def right(source, index):
        table_high, table_low = tables_ref[index], tables_ref[index + 1]
        high, low = split(source)
        return dot(high, table_high) + (dot(low, table_high) + dot(high, table_low))

    def left(source, index):
        table_high, table_low = tables_ref[index], tables_ref[index + 1]
        high, low = split(source)
        return dot(table_high, high) + (dot(table_high, low) + dot(table_low, high))

    def two_sided(zs, right_index, left_index):
        rows = jnp.concatenate([jnp.concatenate(z, axis=1) for z in zs], axis=0)
        out = right(rows, right_index)
        result = []
        for pair in range(0, len(zs), 2):
            re = jnp.concatenate(
                [out[(pair + k) * frame : (pair + k + 1) * frame, :frame] for k in range(2)], axis=1
            )
            im = jnp.concatenate(
                [out[(pair + k) * frame : (pair + k + 1) * frame, frame:] for k in range(2)], axis=1
            )
            mixed = left(jnp.concatenate([re, im], axis=0), left_index)
            for k in range(2):
                cols = slice(k * frame, (k + 1) * frame)
                result.append((mixed[:frame, cols], mixed[frame:, cols]))
        return result

    def group_step(group, carry):
        base = group * GROUP
        where = []
        for k in range(GROUP):
            row_at, col_at = pos_ref[0, base + k], pos_ref[1, base + k]
            block = lax.shift_right_logical(col_at, 7)
            shift = jnp.bitwise_and(col_at, LANES - 1)
            where.append((pl.ds(row_at, frame), block, shift))
            for plane in range(4):
                near = field_ref[plane, block, pl.ds(row_at, frame), :]
                far = field_ref[plane, block + 1, pl.ds(row_at, frame), :]
                joined = jnp.where(lanes >= shift, near, far)
                target = o0 if plane < 2 else o1
                target[k, plane % 2] = pltpu.roll(
                    joined, jnp.bitwise_and(LANES - shift, LANES - 1), 1
                )
        probe_re, probe_im = probe_ref[0], probe_ref[1]
        zs = []
        for k in range(GROUP):
            a, b = o0[k, 0], o0[k, 1]
            zs.append((probe_re * a - probe_im * b, probe_re * b + probe_im * a))
        for k, (re, im) in enumerate(two_sided(zs, HOP_RIGHT, HOP_LEFT)):
            inc[k, 0] = re
            inc[k, 1] = im
        zs = []
        for k in range(GROUP):
            a, b, c, d = inc[k, 0], inc[k, 1], o1[k, 0], o1[k, 1]
            zs.append((a * c - b * d, a * d + b * c))
        for k, (re, im) in enumerate(two_sided(zs, DFT_RIGHT, DFT_LEFT)):
            live = jnp.where(base + k < count, 1.0, 0.0)
            factor = (1.0 - amps_ref[base + k] * lax.rsqrt(re * re + im * im + modulus_offset)) * live
            wave[k, 0] = re * factor
            wave[k, 1] = im * factor
        zs = [(wave[k, 0], wave[k, 1]) for k in range(GROUP)]

        def place(k, first_plane, values):
            rows, block, shift = where[k]
            for part in range(2):
                moved = pltpu.roll(values[part], shift, 1)
                near = jnp.where(lanes >= shift, moved, 0.0)
                far = jnp.where(lanes >= shift, 0.0, moved)
                grad_ref[first_plane + part, block, rows, :] += near
                grad_ref[first_plane + part, block + 1, rows, :] += far

        for k, (re, im) in enumerate(two_sided(zs, DFT_LEFT, DFT_RIGHT)):
            wave[k, 0] = re
            wave[k, 1] = im
        zs = []
        for k in range(GROUP):
            re, im = wave[k, 0], wave[k, 1]
            a, b, c, d = inc[k, 0], inc[k, 1], o1[k, 0], o1[k, 1]
            place(k, 2, (a * re + b * im, a * im - b * re))
            zs.append((c * re + d * im, c * im - d * re))
        for k, (re, im) in enumerate(two_sided(zs, HOP_LEFT, HOP_RIGHT)):
            place(k, 0, (probe_re * re + probe_im * im, probe_re * im - probe_im * re))
        return carry

    lax.fori_loop(0, (count + GROUP - 1) // GROUP, group_step, 0)


def write_grad(grad_ref, top_ref, own_ref, bottom_ref):
    rim = top_ref.shape[2]
    rows = own_ref.shape[2]
    top_ref[...] = grad_ref[:, :, 0:rim, :]
    own_ref[...] = grad_ref[:, :, rim : rim + rows, :]
    bottom_ref[...] = grad_ref[:, :, rim + rows : rim + rows + rim, :]


def first_kernel(
    pos_ref, object_ref, from_left, from_right, from_up, from_down, corner_up, corner_down,
    amps_ref, probe_ref, tables_ref,
    field_ref, top_ref, own_ref, bottom_ref,
    grad_ref, *work,
):
    planes, rows, cols = object_ref.shape
    rim = from_up.shape[1]
    half = rows // 2
    blocks = cols // LANES

    def lay(plane, row_at, tiles, left, right):
        low = lane_ids(tiles[0].shape) < LANES // 2
        turned = [left] + [swap_halves(tile) for tile in tiles] + [right]
        for block in range(blocks + 1):
            field_ref[plane, block, row_at : row_at + tiles[0].shape[0], :] = jnp.where(
                low, turned[block], turned[block + 1]
            )

    def tiles_of(ref, plane, lo, hi):
        return [ref[plane, lo:hi, b * LANES : (b + 1) * LANES] for b in range(blocks)]

    for plane in range(planes):
        corner = corner_up[plane]
        turned = swap_halves(corner)
        lay(plane, 0, tiles_of(from_up, plane, 0, rim), turned, turned)
        lay(plane, rim, tiles_of(object_ref, plane, 0, half), from_left[plane], from_right[plane])
        lay(
            plane, rim + half, tiles_of(object_ref, plane, half, rows),
            swap_halves(from_left[plane]), swap_halves(from_right[plane]),
        )
        corner = corner_down[plane]
        lay(plane, rim + rows, tiles_of(from_down, plane, 0, rim), corner, corner)
    gradients(pos_ref, amps_ref, probe_ref, tables_ref, field_ref, grad_ref, work)
    write_grad(grad_ref, top_ref, own_ref, bottom_ref)


def fold_rows(own_ref, from_up, from_down, block, plane):
    rim = from_up.shape[2]
    rows = own_ref.shape[2]
    return [
        (0, rim, own_ref[plane, block, 0:rim, :] + from_up[plane, block]),
        (rim, rows - rim, own_ref[plane, block, rim : rows - rim, :]),
        (rows - rim, rows, own_ref[plane, block, rows - rim : rows, :] + from_down[plane, block]),
    ]


def fold_kernel(own_ref, from_up, from_down, left_ref, mid_ref, right_ref):
    planes, blocks = own_ref.shape[:2]
    for plane in range(planes):
        for block in range(blocks):
            for lo, hi, values in fold_rows(own_ref, from_up, from_down, block, plane):
                if block == 0:
                    left_ref[plane, lo:hi, :] = values
                elif block == blocks - 1:
                    right_ref[plane, lo:hi, :] = values
                else:
                    mid_ref[plane, block - 1, lo:hi, :] = values


def total_kernel(left_ref, mid_ref, right_ref, from_left, from_right, own_ref, up_ref, down_ref):
    planes, blocks, rows, _ = own_ref.shape
    rim = up_ref.shape[2]
    for plane in range(planes):
        for block in range(blocks):
            if block == 0:
                values = left_ref[plane] + from_left[plane]
            elif block == blocks - 1:
                values = right_ref[plane] + from_right[plane]
            else:
                values = mid_ref[plane, block - 1]
            own_ref[plane, block] = values
            up_ref[plane, block] = values[0:rim]
            down_ref[plane, block] = values[rows - rim : rows]


def next_kernel(
    pos_ref, old_ref, total_ref, from_up, from_down, amps_ref, probe_ref, tables_ref,
    field_ref, top_ref, own_ref, bottom_ref,
    grad_ref, *work,
):
    planes, blocks, rows, _ = total_ref.shape
    rim = from_up.shape[2]
    for block in range(blocks):
        lane = lane_ids((1, 1, LANES))
        inside = lane >= 0
        if block == 0:
            inside = lane >= pos_ref[2, 1] * (LANES // 2)
        if block == blocks - 1:
            inside = lane < LANES - pos_ref[2, 2] * (LANES // 2)
        for lo, hi, values in (
            (0, rim, from_up[:, block]),
            (rim, rim + rows, total_ref[:, block]),
            (rim + rows, rows + 2 * rim, from_down[:, block]),
        ):
            updated = old_ref[:, block, lo:hi, :] - values
            field_ref[:, block, lo:hi, :] = jnp.where(inside, updated, 0.0)
    gradients(pos_ref, amps_ref, probe_ref, tables_ref, field_ref, grad_ref, work)
    write_grad(grad_ref, top_ref, own_ref, bottom_ref)


def last_fold_kernel(own_ref, from_up, from_down, folded_ref, left_ref, right_ref):
    planes, blocks, rows, _ = own_ref.shape
    half = rows // 2
    low = lane_ids((half, LANES)) < LANES // 2
    for plane in range(planes):
        for block in range(blocks):
            for lo, hi, values in fold_rows(own_ref, from_up, from_down, block, plane):
                folded_ref[plane, block, lo:hi, :] = values
        first = folded_ref[plane, 0]
        left_ref[plane] = jnp.where(low, first[:half], swap_halves(first[half:]))
        last = folded_ref[plane, blocks - 1]
        right_ref[plane] = jnp.where(low, swap_halves(last[half:]), last[:half])


def finish_kernel(field_ref, folded_ref, from_left, from_right, out_ref):
    planes, blocks, rows, _ = folded_ref.shape
    rim = (field_ref.shape[2] - rows) // 2
    half = rows // 2
    low = lane_ids((half, LANES)) < LANES // 2
    for plane in range(planes):
        for part in range(2):
            turned = []
            for block in range(blocks):
                values = folded_ref[plane, block, part * half : (part + 1) * half, :]
                if block == 0:
                    extra = from_left[plane]
                    values += extra if part == 0 else swap_halves(extra)
                if block == blocks - 1:
                    extra = from_right[plane]
                    values += extra if part == 0 else swap_halves(extra)
                old = field_ref[plane, block, rim + part * half : rim + (part + 1) * half, :]
                turned.append(swap_halves(old - values))
            for block in range(blocks - 1):
                out_ref[
                    plane, part * half : (part + 1) * half, block * LANES : (block + 1) * LANES
                ] = jnp.where(low, turned[block], turned[block + 1])


def f32(*shape):
    return jax.ShapeDtypeStruct(shape, jnp.float32)


def body(object_slices, probe, amplitudes, scan_pos, scan_count):
    layers, _, tile_r, tile_c = object_slices.shape
    planes = layers * 2
    frame = probe.shape[-1]
    rim = frame // 2
    blocks = tile_c // LANES + 1
    slots = amplitudes.shape[2]
    row_id, col_id = lax.axis_index("row"), lax.axis_index("col")
    amps = amplitudes[0, 0]
    flags = jnp.stack(
        [
            scan_count[0, 0],
            (col_id == 0).astype(jnp.int32),
            (col_id == lax.axis_size("col") - 1).astype(jnp.int32),
        ]
    )
    pos = jnp.stack(
        [
            scan_pos[0, 0, 0] - row_id * tile_r,
            scan_pos[1, 0, 0] - col_id * tile_c,
            jnp.pad(flags, (0, slots - 3)),
        ]
    )
    tables = jnp.asarray(transform_tables(frame))
    tile = object_slices.reshape(planes, tile_r, tile_c)

    left, right, up, down = pl.pallas_call(
        pack_kernel,
        out_shape=[f32(planes, tile_r // 2, LANES)] * 2 + [f32(planes, rim, tile_c)] * 2,
        in_specs=[vmem()],
        out_specs=[vmem()] * 4,
    )(tile)
    from_left = neighbour(right, "col", 1)
    from_right = neighbour(left, "col", -1)
    from_up = neighbour(down, "row", 1)
    from_down = neighbour(up, "row", -1)
    low = lane_ids((1, 1, LANES)) < LANES // 2
    lower, upper = slice(0, rim), slice(tile_r // 2 - rim, tile_r // 2)
    corner_down = neighbour(jnp.where(low, from_left[:, lower], from_right[:, lower]), "row", -1)
    corner_up = neighbour(jnp.where(low, from_right[:, upper], from_left[:, upper]), "row", 1)

    work = [pltpu.VMEM((planes, blocks, tile_r + frame, LANES), jnp.float32)] + [
        pltpu.VMEM((GROUP, 2, frame, frame), jnp.float32)
    ] * 4
    outs = [
        f32(planes, blocks, tile_r + frame, LANES),
        f32(planes, blocks, rim, LANES),
        f32(planes, blocks, tile_r, LANES),
        f32(planes, blocks, rim, LANES),
    ]
    field, top, own, bottom = pl.pallas_call(
        first_kernel,
        out_shape=outs,
        in_specs=[smem()] + [vmem()] * 10,
        out_specs=[vmem()] * 4,
        scratch_shapes=work,
    )(pos, tile, from_left, from_right, from_up, from_down, corner_up, corner_down, amps, probe, tables)

    for iteration in range(1, ITERS):
        from_up = neighbour(bottom, "row", 1)
        from_down = neighbour(top, "row", -1)
        left, mid, right = pl.pallas_call(
            fold_kernel,
            out_shape=[
                f32(planes, tile_r, LANES),
                f32(planes, blocks - 2, tile_r, LANES),
                f32(planes, tile_r, LANES),
            ],
            in_specs=[vmem()] * 3,
            out_specs=[vmem()] * 3,
        )(own, from_up, from_down)
        from_left = neighbour(right, "col", 1)
        from_right = neighbour(left, "col", -1)
        total, up, down = pl.pallas_call(
            total_kernel,
            out_shape=[
                f32(planes, blocks, tile_r, LANES),
                f32(planes, blocks, rim, LANES),
                f32(planes, blocks, rim, LANES),
            ],
            in_specs=[vmem()] * 5,
            out_specs=[vmem()] * 3,
        )(left, mid, right, from_left, from_right)
        from_up = neighbour(down, "row", 1)
        from_down = neighbour(up, "row", -1)
        field, top, own, bottom = pl.pallas_call(
            next_kernel,
            out_shape=outs,
            in_specs=[smem()] + [vmem()] * 7,
            out_specs=[vmem()] * 4,
            scratch_shapes=work,
        )(pos, field, total, from_up, from_down, amps, probe, tables)

    from_up = neighbour(bottom, "row", 1)
    from_down = neighbour(top, "row", -1)
    folded, left, right = pl.pallas_call(
        last_fold_kernel,
        out_shape=[
            f32(planes, blocks, tile_r, LANES),
            f32(planes, tile_r // 2, LANES),
            f32(planes, tile_r // 2, LANES),
        ],
        in_specs=[vmem()] * 3,
        out_specs=[vmem()] * 3,
    )(own, from_up, from_down)
    from_left = neighbour(right, "col", 1)
    from_right = neighbour(left, "col", -1)
    out = pl.pallas_call(
        finish_kernel,
        out_shape=f32(planes, tile_r, tile_c),
        in_specs=[vmem()] * 4,
        out_specs=vmem(),
    )(field, folded, from_left, from_right)
    return out.reshape(object_slices.shape)


def solution(mesh):
    in_specs = (
        P(None, None, "row", "col"),
        P(),
        P("row", "col", None, None, None),
        P(None, "row", "col", None),
        P("row", "col"),
    )
    out_specs = P(None, None, "row", "col")
    return jax.shard_map(body, mesh=mesh, in_specs=in_specs, out_specs=out_specs, check_vma=False)
```

```python
import functools
import math

import jax
import jax.numpy as jnp
import ml_dtypes
import numpy as np
from jax import lax
from jax.experimental import pallas as pl
from jax.experimental.pallas import tpu as pltpu
from jax.sharding import PartitionSpec as P

ITERS = 2
LANES = 128
GROUP = 4

modulus_offset = 0.5
fresnel_scale = 0.9


def split_table(table):
    high = table.astype(np.float32).astype(ml_dtypes.bfloat16)
    low = (table - high.astype(np.float64)).astype(np.float32).astype(ml_dtypes.bfloat16)
    return high, low


def transform_tables(frame_size):
    positions = np.arange(frame_size)
    dft = np.exp(-2j * math.pi * (positions[:, None] * positions[None, :] % frame_size) / frame_size)
    dft = dft / math.sqrt(frame_size)
    frequency = np.where(positions < frame_size // 2, positions, positions - frame_size)
    phase = np.exp(1j * math.pi * fresnel_scale * frequency.astype(np.float64) ** 2 / frame_size)
    hop = (np.conj(dft) * phase[None, :]) @ dft
    tables = []
    for matrix in (dft, hop):
        re, im = matrix.real, matrix.imag
        right = np.block([[re, im], [-im, re]])
        left = np.block([[re, -im], [im, re]])
        for table in (right, left):
            tables.extend(split_table(table))
    return np.stack(tables)


DFT_RIGHT, DFT_LEFT, HOP_RIGHT, HOP_LEFT = 0, 2, 4, 6


def neighbour(values, axis, step):
    count = lax.axis_size(axis)
    pairs = [(i, i + step) for i in range(count) if 0 <= i + step < count]
    return lax.ppermute(values, axis, pairs)


def lane_ids(shape):
    return lax.broadcasted_iota(jnp.int32, shape, len(shape) - 1)


def swap_halves(values):
    return pltpu.roll(values, LANES // 2, values.ndim - 1)


def vmem():
    return pl.BlockSpec(memory_space=pltpu.VMEM)


def smem():
    return pl.BlockSpec(memory_space=pltpu.SMEM)


def split(values):
    high = values.astype(jnp.bfloat16)
    return high, (values - high.astype(jnp.float32)).astype(jnp.bfloat16)


def dot(a, b):
    return jnp.dot(a, b, preferred_element_type=jnp.float32)


def pack_kernel(object_ref, left_ref, right_ref, up_ref, down_ref):
    planes, rows, cols = object_ref.shape
    half = rows // 2
    low = lane_ids((half, LANES)) < LANES // 2
    for plane in range(planes):
        first = object_ref[plane, :, 0:LANES]
        last = object_ref[plane, :, cols - LANES : cols]
        left_ref[plane] = jnp.where(low, first[half:], swap_halves(first[:half]))
        right_ref[plane] = jnp.where(low, swap_halves(last[:half]), last[half:])
        up_ref[plane] = object_ref[plane, 0:64, :]
        down_ref[plane] = object_ref[plane, rows - 64 : rows, :]


def gradients(pos_ref, amps_ref, probe_ref, tables_ref, field_ref, grad_ref, work):
    frame = probe_ref.shape[-1]
    o0, o1, inc, wave = work
    count = pos_ref[2, 0]
    lanes = lane_ids((frame, LANES))

    grad_ref[...] = jnp.zeros_like(grad_ref)

    def right(source, index):
        table_high, table_low = tables_ref[index], tables_ref[index + 1]
        high, low = split(source)
        return dot(high, table_high) + (dot(low, table_high) + dot(high, table_low))

    def left(source, index):
        table_high, table_low = tables_ref[index], tables_ref[index + 1]
        high, low = split(source)
        return dot(table_high, high) + (dot(table_high, low) + dot(table_low, high))

    def two_sided(zs, right_index, left_index):
        rows = jnp.concatenate([jnp.concatenate(z, axis=1) for z in zs], axis=0)
        out = right(rows, right_index)
        result = []
        for pair in range(0, len(zs), 2):
            re = jnp.concatenate(
                [out[(pair + k) * frame : (pair + k + 1) * frame, :frame] for k in range(2)], axis=1
            )
            im = jnp.concatenate(
                [out[(pair + k) * frame : (pair + k + 1) * frame, frame:] for k in range(2)], axis=1
            )
            mixed = left(jnp.concatenate([re, im], axis=0), left_index)
            for k in range(2):
                cols = slice(k * frame, (k + 1) * frame)
                result.append((mixed[:frame, cols], mixed[frame:, cols]))
        return result

    def group_step(group, carry):
        base = group * GROUP
        where = []
        for k in range(GROUP):
            row_at, col_at = pos_ref[0, base + k], pos_ref[1, base + k]
            block = lax.shift_right_logical(col_at, 7)
            shift = jnp.bitwise_and(col_at, LANES - 1)
            where.append((pl.ds(row_at, frame), block, shift))
            for plane in range(4):
                near = field_ref[plane, block, pl.ds(row_at, frame), :]
                far = field_ref[plane, block + 1, pl.ds(row_at, frame), :]
                joined = jnp.where(lanes >= shift, near, far)
                target = o0 if plane < 2 else o1
                target[k, plane % 2] = pltpu.roll(
                    joined, jnp.bitwise_and(LANES - shift, LANES - 1), 1
                )
        probe_re, probe_im = probe_ref[0], probe_ref[1]
        zs = []
        for k in range(GROUP):
            a, b = o0[k, 0], o0[k, 1]
            zs.append((probe_re * a - probe_im * b, probe_re * b + probe_im * a))
        for k, (re, im) in enumerate(two_sided(zs, HOP_RIGHT, HOP_LEFT)):
            inc[k, 0] = re
            inc[k, 1] = im
        zs = []
        for k in range(GROUP):
            a, b, c, d = inc[k, 0], inc[k, 1], o1[k, 0], o1[k, 1]
            zs.append((a * c - b * d, a * d + b * c))
        for k, (re, im) in enumerate(two_sided(zs, DFT_RIGHT, DFT_LEFT)):
            live = jnp.where(base + k < count, 1.0, 0.0)
            factor = (1.0 - amps_ref[base + k] * lax.rsqrt(re * re + im * im + modulus_offset)) * live
            wave[k, 0] = re * factor
            wave[k, 1] = im * factor
        zs = [(wave[k, 0], wave[k, 1]) for k in range(GROUP)]

        def place(k, first_plane, values):
            rows, block, shift = where[k]
            for part in range(2):
                moved = pltpu.roll(values[part], shift, 1)
                near = jnp.where(lanes >= shift, moved, 0.0)
                far = jnp.where(lanes >= shift, 0.0, moved)
                grad_ref[first_plane + part, block, rows, :] += near
                grad_ref[first_plane + part, block + 1, rows, :] += far

        for k, (re, im) in enumerate(two_sided(zs, DFT_LEFT, DFT_RIGHT)):
            wave[k, 0] = re
            wave[k, 1] = im
        zs = []
        for k in range(GROUP):
            re, im = wave[k, 0], wave[k, 1]
            a, b, c, d = inc[k, 0], inc[k, 1], o1[k, 0], o1[k, 1]
            place(k, 2, (a * re + b * im, a * im - b * re))
            zs.append((c * re + d * im, c * im - d * re))
        for k, (re, im) in enumerate(two_sided(zs, HOP_LEFT, HOP_RIGHT)):
            place(k, 0, (probe_re * re + probe_im * im, probe_re * im - probe_im * re))
        return carry

    lax.fori_loop(0, (count + GROUP - 1) // GROUP, group_step, 0)


def write_grad(grad_ref, top_ref, own_ref, bottom_ref):
    rim = top_ref.shape[2]
    rows = own_ref.shape[2]
    top_ref[...] = grad_ref[:, :, 0:rim, :]
    own_ref[...] = grad_ref[:, :, rim : rim + rows, :]
    bottom_ref[...] = grad_ref[:, :, rim + rows : rim + rows + rim, :]


def first_kernel(
    pos_ref, object_ref, from_left, from_right, from_up, from_down, corner_up, corner_down,
    amps_ref, probe_ref, tables_ref,
    field_ref, top_ref, own_ref, bottom_ref,
    grad_ref, *work,
):
    planes, rows, cols = object_ref.shape
    rim = from_up.shape[1]
    half = rows // 2
    blocks = cols // LANES

    def lay(plane, row_at, tiles, left, right):
        low = lane_ids(tiles[0].shape) < LANES // 2
        turned = [left] + [swap_halves(tile) for tile in tiles] + [right]
        for block in range(blocks + 1):
            field_ref[plane, block, row_at : row_at + tiles[0].shape[0], :] = jnp.where(
                low, turned[block], turned[block + 1]
            )

    def tiles_of(ref, plane, lo, hi):
        return [ref[plane, lo:hi, b * LANES : (b + 1) * LANES] for b in range(blocks)]

    for plane in range(planes):
        corner = corner_up[plane]
        turned = swap_halves(corner)
        lay(plane, 0, tiles_of(from_up, plane, 0, rim), turned, turned)
        lay(plane, rim, tiles_of(object_ref, plane, 0, half), from_left[plane], from_right[plane])
        lay(
            plane, rim + half, tiles_of(object_ref, plane, half, rows),
            swap_halves(from_left[plane]), swap_halves(from_right[plane]),
        )
        corner = corner_down[plane]
        lay(plane, rim + rows, tiles_of(from_down, plane, 0, rim), corner, corner)
    gradients(pos_ref, amps_ref, probe_ref, tables_ref, field_ref, grad_ref, work)
    write_grad(grad_ref, top_ref, own_ref, bottom_ref)


def fold_rows(own_ref, from_up, from_down, block, plane):
    rim = from_up.shape[2]
    rows = own_ref.shape[2]
    return [
        (0, rim, own_ref[plane, block, 0:rim, :] + from_up[plane, block]),
        (rim, rows - rim, own_ref[plane, block, rim : rows - rim, :]),
        (rows - rim, rows, own_ref[plane, block, rows - rim : rows, :] + from_down[plane, block]),
    ]


def fold_kernel(own_ref, from_up, from_down, left_ref, mid_ref, right_ref):
    planes, blocks = own_ref.shape[:2]
    for plane in range(planes):
        for block in range(blocks):
            for lo, hi, values in fold_rows(own_ref, from_up, from_down, block, plane):
                if block == 0:
                    left_ref[plane, lo:hi, :] = values
                elif block == blocks - 1:
                    right_ref[plane, lo:hi, :] = values
                else:
                    mid_ref[plane, block - 1, lo:hi, :] = values


def total_kernel(left_ref, mid_ref, right_ref, from_left, from_right, own_ref, up_ref, down_ref):
    planes, blocks, rows, _ = own_ref.shape
    rim = up_ref.shape[2]
    for plane in range(planes):
        for block in range(blocks):
            if block == 0:
                values = left_ref[plane] + from_left[plane]
            elif block == blocks - 1:
                values = right_ref[plane] + from_right[plane]
            else:
                values = mid_ref[plane, block - 1]
            own_ref[plane, block] = values
            up_ref[plane, block] = values[0:rim]
            down_ref[plane, block] = values[rows - rim : rows]


def next_kernel(
    pos_ref, old_ref, total_ref, from_up, from_down, amps_ref, probe_ref, tables_ref,
    field_ref, top_ref, own_ref, bottom_ref,
    grad_ref, *work,
):
    planes, blocks, rows, _ = total_ref.shape
    rim = from_up.shape[2]
    for block in range(blocks):
        lane = lane_ids((1, 1, LANES))
        inside = lane >= 0
        if block == 0:
            inside = lane >= pos_ref[2, 1] * (LANES // 2)
        if block == blocks - 1:
            inside = lane < LANES - pos_ref[2, 2] * (LANES // 2)
        for lo, hi, values in (
            (0, rim, from_up[:, block]),
            (rim, rim + rows, total_ref[:, block]),
            (rim + rows, rows + 2 * rim, from_down[:, block]),
        ):
            updated = old_ref[:, block, lo:hi, :] - values
            field_ref[:, block, lo:hi, :] = jnp.where(inside, updated, 0.0)
    gradients(pos_ref, amps_ref, probe_ref, tables_ref, field_ref, grad_ref, work)
    write_grad(grad_ref, top_ref, own_ref, bottom_ref)


def last_fold_kernel(own_ref, from_up, from_down, folded_ref, left_ref, right_ref):
    planes, blocks, rows, _ = own_ref.shape
    half = rows // 2
    low = lane_ids((half, LANES)) < LANES // 2
    for plane in range(planes):
        for block in range(blocks):
            for lo, hi, values in fold_rows(own_ref, from_up, from_down, block, plane):
                folded_ref[plane, block, lo:hi, :] = values
        first = folded_ref[plane, 0]
        left_ref[plane] = jnp.where(low, first[:half], swap_halves(first[half:]))
        last = folded_ref[plane, blocks - 1]
        right_ref[plane] = jnp.where(low, swap_halves(last[half:]), last[:half])


def finish_kernel(field_ref, folded_ref, from_left, from_right, out_ref):
    planes, blocks, rows, _ = folded_ref.shape
    rim = (field_ref.shape[2] - rows) // 2
    half = rows // 2
    low = lane_ids((half, LANES)) < LANES // 2
    for plane in range(planes):
        for part in range(2):
            turned = []
            for block in range(blocks):
                values = folded_ref[plane, block, part * half : (part + 1) * half, :]
                if block == 0:
                    extra = from_left[plane]
                    values += extra if part == 0 else swap_halves(extra)
                if block == blocks - 1:
                    extra = from_right[plane]
                    values += extra if part == 0 else swap_halves(extra)
                old = field_ref[plane, block, rim + part * half : rim + (part + 1) * half, :]
                turned.append(swap_halves(old - values))
            for block in range(blocks - 1):
                out_ref[
                    plane, part * half : (part + 1) * half, block * LANES : (block + 1) * LANES
                ] = jnp.where(low, turned[block], turned[block + 1])


def f32(*shape):
    return pltpu.VMEM(shape, jnp.float32)


def on_chip(*arrays):
    return [pltpu.with_memory_space_constraint(array, pltpu.VMEM) for array in arrays]


def limit(mib):
    return pltpu.CompilerParams(vmem_limit_bytes=mib << 20)


def body(object_slices, probe, amplitudes, scan_pos, scan_count):
    layers, _, tile_r, tile_c = object_slices.shape
    planes = layers * 2
    frame = probe.shape[-1]
    rim = frame // 2
    blocks = tile_c // LANES + 1
    slots = amplitudes.shape[2]
    row_id, col_id = lax.axis_index("row"), lax.axis_index("col")
    amps = amplitudes[0, 0]
    flags = jnp.stack(
        [
            scan_count[0, 0],
            (col_id == 0).astype(jnp.int32),
            (col_id == lax.axis_size("col") - 1).astype(jnp.int32),
        ]
    )
    pos = jnp.stack(
        [
            scan_pos[0, 0, 0] - row_id * tile_r,
            scan_pos[1, 0, 0] - col_id * tile_c,
            jnp.pad(flags, (0, slots - 3)),
        ]
    )
    tables = jnp.asarray(transform_tables(frame))
    tile = object_slices.reshape(planes, tile_r, tile_c)

    left, right, up, down = pl.pallas_call(
        pack_kernel,
        out_shape=[f32(planes, tile_r // 2, LANES)] * 2 + [f32(planes, rim, tile_c)] * 2,
        in_specs=[vmem()],
        out_specs=[vmem()] * 4,
        compiler_params=limit(4),
    )(*on_chip(tile))
    from_left = neighbour(right, "col", 1)
    from_right = neighbour(left, "col", -1)
    from_up = neighbour(down, "row", 1)
    from_down = neighbour(up, "row", -1)
    low = lane_ids((1, 1, LANES)) < LANES // 2
    lower, upper = slice(0, rim), slice(tile_r // 2 - rim, tile_r // 2)
    corner_down = neighbour(jnp.where(low, from_left[:, lower], from_right[:, lower]), "row", -1)
    corner_up = neighbour(jnp.where(low, from_right[:, upper], from_left[:, upper]), "row", 1)

    work = [pltpu.VMEM((planes, blocks, tile_r + frame, LANES), jnp.float32)] + [
        pltpu.VMEM((GROUP, 2, frame, frame), jnp.float32)
    ] * 4
    outs = [
        f32(planes, blocks, tile_r + frame, LANES),
        f32(planes, blocks, rim, LANES),
        f32(planes, blocks, tile_r, LANES),
        f32(planes, blocks, rim, LANES),
    ]
    field, top, own, bottom = pl.pallas_call(
        first_kernel,
        out_shape=outs,
        in_specs=[smem()] + [vmem()] * 10,
        out_specs=[vmem()] * 4,
        scratch_shapes=work,
        compiler_params=limit(20),
    )(
        pos,
        *on_chip(
            tile, from_left, from_right, from_up, from_down, corner_up, corner_down,
            amps, probe, tables,
        ),
    )

    for iteration in range(1, ITERS):
        from_up = neighbour(bottom, "row", 1)
        from_down = neighbour(top, "row", -1)
        left, mid, right = pl.pallas_call(
            fold_kernel,
            out_shape=[
                f32(planes, tile_r, LANES),
                f32(planes, blocks - 2, tile_r, LANES),
                f32(planes, tile_r, LANES),
            ],
            in_specs=[vmem()] * 3,
            out_specs=[vmem()] * 3,
            compiler_params=limit(4),
        )(*on_chip(own, from_up, from_down))
        from_left = neighbour(right, "col", 1)
        from_right = neighbour(left, "col", -1)
        total, up, down = pl.pallas_call(
            total_kernel,
            out_shape=[
                f32(planes, blocks, tile_r, LANES),
                f32(planes, blocks, rim, LANES),
                f32(planes, blocks, rim, LANES),
            ],
            in_specs=[vmem()] * 5,
            out_specs=[vmem()] * 3,
            compiler_params=limit(4),
        )(*on_chip(left, mid, right, from_left, from_right))
        from_up = neighbour(down, "row", 1)
        from_down = neighbour(up, "row", -1)
        field, top, own, bottom = pl.pallas_call(
            next_kernel,
            out_shape=outs,
            in_specs=[smem()] + [vmem()] * 7,
            out_specs=[vmem()] * 4,
            scratch_shapes=work,
            compiler_params=limit(20),
        )(pos, *on_chip(field, total, from_up, from_down, amps, probe, tables))

    from_up = neighbour(bottom, "row", 1)
    from_down = neighbour(top, "row", -1)
    folded, left, right = pl.pallas_call(
        last_fold_kernel,
        out_shape=[
            f32(planes, blocks, tile_r, LANES),
            f32(planes, tile_r // 2, LANES),
            f32(planes, tile_r // 2, LANES),
        ],
        in_specs=[vmem()] * 3,
        out_specs=[vmem()] * 3,
            compiler_params=limit(4),
    )(*on_chip(own, from_up, from_down))
    from_left = neighbour(right, "col", 1)
    from_right = neighbour(left, "col", -1)
    out = pl.pallas_call(
        finish_kernel,
        out_shape=jax.ShapeDtypeStruct((planes, tile_r, tile_c), jnp.float32),
        in_specs=[vmem()] * 4,
        out_specs=vmem(),
        compiler_params=limit(8),
    )(*on_chip(field, folded, from_left, from_right))
    return out.reshape(object_slices.shape)


def solution(mesh):
    in_specs = (
        P(None, None, "row", "col"),
        P(),
        P("row", "col", None, None, None),
        P(None, "row", "col", None),
        P("row", "col"),
    )
    out_specs = P(None, None, "row", "col")
    return jax.shard_map(body, mesh=mesh, in_specs=in_specs, out_specs=out_specs, check_vma=False)
```

```python
import math

import jax
import jax.numpy as jnp
import ml_dtypes
import numpy as np
from jax import lax
from jax.experimental import pallas as pl
from jax.experimental.pallas import tpu as pltpu
from jax.sharding import PartitionSpec as P

ITERS = 2
LANES = 128
GROUP = 4

modulus_offset = 0.5
fresnel_scale = 0.9


def split_table(table):
    high = table.astype(np.float32).astype(ml_dtypes.bfloat16)
    low = (table - high.astype(np.float64)).astype(np.float32).astype(ml_dtypes.bfloat16)
    return high, low


def transform_tables(frame_size):
    positions = np.arange(frame_size)
    dft = np.exp(-2j * math.pi * (positions[:, None] * positions[None, :] % frame_size) / frame_size)
    dft = dft / math.sqrt(frame_size)
    frequency = np.where(positions < frame_size // 2, positions, positions - frame_size)
    phase = np.exp(1j * math.pi * fresnel_scale * frequency.astype(np.float64) ** 2 / frame_size)
    hop = (np.conj(dft) * phase[None, :]) @ dft
    tables = []
    for matrix in (dft, hop):
        re, im = matrix.real, matrix.imag
        right = np.block([[re, im], [-im, re]])
        left = np.block([[re, -im], [im, re]])
        for table in (right, left):
            tables.extend(split_table(table))
    return np.stack(tables)


DFT_RIGHT, DFT_LEFT, HOP_RIGHT, HOP_LEFT = 0, 2, 4, 6


def neighbour(values, axis, step):
    count = lax.axis_size(axis)
    pairs = [(i, i + step) for i in range(count) if 0 <= i + step < count]
    return lax.ppermute(values, axis, pairs)


def lane_ids(shape):
    return lax.broadcasted_iota(jnp.int32, shape, len(shape) - 1)


def swap_halves(values):
    return pltpu.roll(values, LANES // 2, values.ndim - 1)


def vmem():
    return pl.BlockSpec(memory_space=pltpu.VMEM)


def smem():
    return pl.BlockSpec(memory_space=pltpu.SMEM)


def split(values):
    high = values.astype(jnp.bfloat16)
    return high, (values - high.astype(jnp.float32)).astype(jnp.bfloat16)


def dot(a, b):
    return jnp.dot(a, b, preferred_element_type=jnp.float32)


def blend(first, second):
    return jnp.where(lane_ids(first.shape) < LANES // 2, first, second)


def segments(rows, rim):
    half = rows // 2
    return ((slice(0, rim), slice(rows - rim, rows)), (slice(rim, half), slice(half, rows - rim)))


def pack_kernel(object_ref, turned_ref, left_edge, right_edge, left_mid, right_mid):
    planes, rows, cols = object_ref.shape
    tiles = cols // LANES
    pieces = segments(rows, left_edge.shape[1])
    for plane in range(planes):
        for (upper, lower), left_ref, right_ref in zip(
            pieces, (left_edge, left_mid), (right_edge, right_mid)
        ):
            left_ref[plane] = blend(
                object_ref[plane, lower, 0:LANES], swap_halves(object_ref[plane, upper, 0:LANES])
            )
            right_ref[plane] = blend(
                swap_halves(object_ref[plane, upper, cols - LANES : cols]),
                object_ref[plane, lower, cols - LANES : cols],
            )
    for plane in range(planes):
        for tile in range(tiles):
            turned_ref[plane, tile] = swap_halves(
                object_ref[plane, :, tile * LANES : (tile + 1) * LANES]
            )


def lay(turned_ref, plane, rows, left, right, put):
    tiles = turned_ref.shape[1]
    parts = [left] + [turned_ref[plane, tile, rows, :] for tile in range(tiles)] + [right]
    for block in range(tiles + 1):
        put(block, blend(parts[block], parts[block + 1]))


def rows_kernel(turned_ref, from_left, from_right, tables_hbm, up_ref, down_ref, tables_ref, sem):
    copy = pltpu.make_async_copy(tables_hbm, tables_ref, sem)
    copy.start()
    planes, _, rows, _ = turned_ref.shape
    rim = up_ref.shape[2]
    (upper, lower), _ = segments(rows, rim)
    for plane in range(planes):

        def put_up(block, values):
            up_ref[plane, block] = values

        def put_down(block, values):
            down_ref[plane, block] = values

        left, right = from_left[plane], from_right[plane]
        lay(turned_ref, plane, upper, left, right, put_up)
        lay(turned_ref, plane, lower, swap_halves(left), swap_halves(right), put_down)
    copy.wait()


def gradients(pos_ref, amps_ref, probe_ref, tables_ref, field_ref, grad_ref, work):
    frame = probe_ref.shape[-1]
    o0, o1, inc, wave = work
    count = pos_ref[2, 0]
    lanes = lane_ids((frame, LANES))

    grad_ref[...] = jnp.zeros_like(grad_ref)

    def right(source, index):
        table_high, table_low = tables_ref[index], tables_ref[index + 1]
        high, low = split(source)
        return dot(high, table_high) + (dot(low, table_high) + dot(high, table_low))

    def left(source, index):
        table_high, table_low = tables_ref[index], tables_ref[index + 1]
        high, low = split(source)
        return dot(table_high, high) + (dot(table_high, low) + dot(table_low, high))

    def two_sided(zs, right_index, left_index):
        result = []
        for pair in range(0, len(zs), 2):
            rows = jnp.concatenate([jnp.concatenate(z, axis=1) for z in zs[pair : pair + 2]], axis=0)
            out = right(rows, right_index)
            mixed = left(
                jnp.concatenate(
                    [
                        jnp.concatenate([out[:frame, :frame], out[frame:, :frame]], axis=1),
                        jnp.concatenate([out[:frame, frame:], out[frame:, frame:]], axis=1),
                    ],
                    axis=0,
                ),
                left_index,
            )
            for k in range(2):
                cols = slice(k * frame, (k + 1) * frame)
                result.append((mixed[:frame, cols], mixed[frame:, cols]))
        return result

    def group_step(group, carry):
        base = group * GROUP
        where = []
        for k in range(GROUP):
            row_at, col_at = pos_ref[0, base + k], pos_ref[1, base + k]
            block = lax.shift_right_logical(col_at, 7)
            shift = jnp.bitwise_and(col_at, LANES - 1)
            where.append((pl.ds(row_at, frame), block, shift))
            for plane in range(4):
                near = field_ref[plane, block, pl.ds(row_at, frame), :]
                far = field_ref[plane, block + 1, pl.ds(row_at, frame), :]
                joined = jnp.where(lanes >= shift, near, far)
                target = o0 if plane < 2 else o1
                target[k, plane % 2] = pltpu.roll(
                    joined, jnp.bitwise_and(LANES - shift, LANES - 1), 1
                )
        probe_re, probe_im = probe_ref[0], probe_ref[1]
        zs = []
        for k in range(GROUP):
            a, b = o0[k, 0], o0[k, 1]
            zs.append((probe_re * a - probe_im * b, probe_re * b + probe_im * a))
        for k, (re, im) in enumerate(two_sided(zs, HOP_RIGHT, HOP_LEFT)):
            inc[k, 0] = re
            inc[k, 1] = im
        zs = []
        for k in range(GROUP):
            a, b, c, d = inc[k, 0], inc[k, 1], o1[k, 0], o1[k, 1]
            zs.append((a * c - b * d, a * d + b * c))
        for k, (re, im) in enumerate(two_sided(zs, DFT_RIGHT, DFT_LEFT)):
            live = jnp.where(base + k < count, 1.0, 0.0)
            factor = (1.0 - amps_ref[base + k] * lax.rsqrt(re * re + im * im + modulus_offset)) * live
            wave[k, 0] = re * factor
            wave[k, 1] = im * factor
        zs = [(wave[k, 0], wave[k, 1]) for k in range(GROUP)]

        def place(k, first_plane, values):
            rows, block, shift = where[k]
            for part in range(2):
                moved = pltpu.roll(values[part], shift, 1)
                near = jnp.where(lanes >= shift, moved, 0.0)
                far = jnp.where(lanes >= shift, 0.0, moved)
                grad_ref[first_plane + part, block, rows, :] += near
                grad_ref[first_plane + part, block + 1, rows, :] += far

        for k, (re, im) in enumerate(two_sided(zs, DFT_LEFT, DFT_RIGHT)):
            wave[k, 0] = re
            wave[k, 1] = im
        zs = []
        for k in range(GROUP):
            re, im = wave[k, 0], wave[k, 1]
            a, b, c, d = inc[k, 0], inc[k, 1], o1[k, 0], o1[k, 1]
            place(k, 2, (a * re + b * im, a * im - b * re))
            zs.append((c * re + d * im, c * im - d * re))
        for k, (re, im) in enumerate(two_sided(zs, HOP_LEFT, HOP_RIGHT)):
            place(k, 0, (probe_re * re + probe_im * im, probe_re * im - probe_im * re))
        return carry

    lax.fori_loop(0, (count + GROUP - 1) // GROUP, group_step, 0)


def write_grad(grad_ref, pieces, packed):
    top, bottom, edges, left, mid, right = pieces
    _, blocks, all_rows, _ = grad_ref.shape
    rim = top.shape[2]
    rows = all_rows - 2 * rim
    top[...] = grad_ref[:, :, 0:rim, :]
    bottom[...] = grad_ref[:, :, rim + rows : all_rows, :]
    edges[:, :, 0:rim, :] = grad_ref[:, :, rim : 2 * rim, :]
    edges[:, :, rim : 2 * rim, :] = grad_ref[:, :, rows : rim + rows, :]
    left[...] = grad_ref[:, 0, 2 * rim : rows, :]
    mid[...] = grad_ref[:, 1 : blocks - 1, 2 * rim : rows, :]
    right[...] = grad_ref[:, blocks - 1, 2 * rim : rows, :]
    if packed:
        half = (rows - 2 * rim) // 2
        upper, lower = slice(2 * rim, 2 * rim + half), slice(2 * rim + half, rows)
        pack_bands(grad_ref, packed, upper, lower)


def pack_bands(ref, packed, upper, lower):
    blocks = ref.shape[1]
    for plane in range(ref.shape[0]):
        packed[0][plane] = blend(ref[plane, 0, upper, :], swap_halves(ref[plane, 0, lower, :]))
        packed[1][plane] = blend(
            swap_halves(ref[plane, blocks - 1, lower, :]), ref[plane, blocks - 1, upper, :]
        )


def first_kernel(
    pos_ref, turned_ref, up_ref, down_ref, from_left, from_right, from_up, from_down,
    amps_ref, probe_ref, tables_ref, field_ref, *rest,
):
    pieces, (grad_ref, *work) = rest[:-5], rest[-5:]
    planes, _, rows, _ = turned_ref.shape
    rim = up_ref.shape[2]
    _, (upper, lower) = segments(rows, rim)
    field_ref[:, :, 0:rim, :] = from_up[...]
    field_ref[:, :, rim : 2 * rim, :] = up_ref[...]
    field_ref[:, :, rows : rows + rim, :] = down_ref[...]
    field_ref[:, :, rows + rim : rows + 2 * rim, :] = from_down[...]
    for plane in range(planes):

        def put_upper(block, values):
            field_ref[plane, block, rim + upper.start : rim + upper.stop, :] = values

        def put_lower(block, values):
            field_ref[plane, block, rim + lower.start : rim + lower.stop, :] = values

        left, right = from_left[plane], from_right[plane]
        lay(turned_ref, plane, upper, left, right, put_upper)
        lay(turned_ref, plane, lower, swap_halves(left), swap_halves(right), put_lower)
    gradients(pos_ref, amps_ref, probe_ref, tables_ref, field_ref, grad_ref, work)
    write_grad(grad_ref, pieces[:6], pieces[6:])


def folded(edges, from_up, from_down, plane, block):
    rim = from_up.shape[2]
    return (
        edges[plane, block, 0:rim, :] + from_up[plane, block],
        edges[plane, block, rim : 2 * rim, :] + from_down[plane, block],
    )


def fold_kernel(edges, from_up, from_down, left_ref, mid_ref, right_ref):
    planes, blocks = edges.shape[:2]
    rim = from_up.shape[2]
    for plane in range(planes):
        for block in range(blocks):
            upper, lower = folded(edges, from_up, from_down, plane, block)
            target = mid_ref.at[plane, block - 1]
            if block == 0:
                target = left_ref.at[plane]
            elif block == blocks - 1:
                target = right_ref.at[plane]
            target[0:rim, :] = upper
            target[rim : 2 * rim, :] = lower


def total_kernel(left_ref, mid_ref, right_ref, from_left, from_right, up_ref, down_ref):
    planes, blocks, rim, _ = up_ref.shape
    for plane in range(planes):
        for block in range(blocks):
            if block == 0:
                values = left_ref[plane] + from_left[plane]
            elif block == blocks - 1:
                values = right_ref[plane] + from_right[plane]
            else:
                values = mid_ref[plane, block - 1]
            up_ref[plane, block] = values[0:rim]
            down_ref[plane, block] = values[rim : 2 * rim]


def next_kernel(
    pos_ref, old_ref, up_ref, down_ref, left_ref, mid_ref, right_ref,
    from_left, from_right, from_up, from_down, amps_ref, probe_ref, tables_ref, field_ref, *rest,
):
    pieces, (grad_ref, *work) = rest[:-5], rest[-5:]
    _, blocks, all_rows, _ = old_ref.shape
    rim = up_ref.shape[2]
    rows = all_rows - 2 * rim
    for block in range(blocks):
        lane = lane_ids((1, 1, LANES))
        inside = lane >= 0
        middle = mid_ref[:, block - 1] if 0 < block < blocks - 1 else None
        if block == 0:
            inside = lane >= pos_ref[2, 1] * (LANES // 2)
            middle = left_ref[...] + from_left[...]
        if block == blocks - 1:
            inside = lane < LANES - pos_ref[2, 2] * (LANES // 2)
            middle = right_ref[...] + from_right[...]
        for lo, hi, values in (
            (0, rim, from_up[:, block]),
            (rim, 2 * rim, up_ref[:, block]),
            (2 * rim, rows, middle),
            (rows, rows + rim, down_ref[:, block]),
            (rows + rim, all_rows, from_down[:, block]),
        ):
            updated = old_ref[:, block, lo:hi, :] - values
            field_ref[:, block, lo:hi, :] = jnp.where(inside, updated, 0.0)
    gradients(pos_ref, amps_ref, probe_ref, tables_ref, field_ref, grad_ref, work)
    write_grad(grad_ref, pieces[:6], pieces[6:])


def last_fold_kernel(edges, from_up, from_down, folded_ref, left_ref, right_ref):
    planes, blocks = edges.shape[:2]
    rim = from_up.shape[2]
    for plane in range(planes):
        for block in range(blocks):
            upper, lower = folded(edges, from_up, from_down, plane, block)
            folded_ref[plane, block, 0:rim, :] = upper
            folded_ref[plane, block, rim : 2 * rim, :] = lower
    pack_bands(folded_ref, (left_ref, right_ref), slice(0, rim), slice(rim, 2 * rim))


def finish_kernel(
    field_ref, edges, left_ref, mid_ref, right_ref,
    mid_left, mid_right, edge_left, edge_right, out_ref,
):
    planes, blocks, _, _ = field_ref.shape
    rows = out_ref.shape[1]
    rim = edge_left.shape[1]
    (first, last), (upper, lower) = segments(rows, rim)
    half = upper.stop - upper.start

    def whole(plane, part, edge):
        size = rim if edge else half
        at = slice(part * size, (part + 1) * size)
        values = [
            edges[plane, block, at, :] if edge
            else left_ref[plane, at, :] if block == 0
            else right_ref[plane, at, :] if block == blocks - 1
            else mid_ref[plane, block - 1, at, :]
            for block in range(blocks)
        ]
        extras = [edge_left[plane], edge_right[plane]] if edge else [mid_left[plane], mid_right[plane]]
        if part == 1:
            extras = [swap_halves(extra) for extra in extras]
        values[0] += extras[0]
        values[-1] += extras[1]
        return values

    for plane in range(planes):
        for part, edge, at in ((0, True, first), (0, False, upper), (1, False, lower), (1, True, last)):
            values = whole(plane, part, edge)
            turned = [
                swap_halves(field_ref[plane, block, rim + at.start : rim + at.stop, :] - values[block])
                for block in range(blocks)
            ]
            for block in range(blocks - 1):
                out_ref[plane, at, block * LANES : (block + 1) * LANES] = blend(
                    turned[block], turned[block + 1]
                )


def f32(*shape):
    return pltpu.VMEM(shape, jnp.float32)


def on_chip(*arrays):
    return [pltpu.with_memory_space_constraint(array, pltpu.VMEM) for array in arrays]


def body(object_slices, probe, amplitudes, scan_pos, scan_count):
    layers, _, tile_r, tile_c = object_slices.shape
    planes = layers * 2
    frame = probe.shape[-1]
    rim = frame // 2
    blocks = tile_c // LANES + 1
    slots = amplitudes.shape[2]
    row_id, col_id = lax.axis_index("row"), lax.axis_index("col")
    amps = amplitudes[0, 0]
    flags = jnp.stack(
        [
            scan_count[0, 0],
            (col_id == 0).astype(jnp.int32),
            (col_id == lax.axis_size("col") - 1).astype(jnp.int32),
        ]
    )
    pos = jnp.stack(
        [
            scan_pos[0, 0, 0] - row_id * tile_r,
            scan_pos[1, 0, 0] - col_id * tile_c,
            jnp.pad(flags, (0, slots - 3)),
        ]
    )
    tables = jnp.asarray(transform_tables(frame))
    tile = object_slices.reshape(planes, tile_r, tile_c)

    band = tile_r - 2 * rim

    def call(kernel, outs, mib, scratch=(), scalars=(), raw=()):
        def run(*arrays):
            return pl.pallas_call(
                kernel,
                out_shape=outs,
                in_specs=[smem()] * len(scalars) + [vmem()] * len(arrays)
                + [pl.BlockSpec(memory_space=pltpu.HBM)] * len(raw),
                out_specs=[vmem()] * len(outs),
                scratch_shapes=list(scratch),
                compiler_params=pltpu.CompilerParams(vmem_limit_bytes=mib << 20),
            )(
                *scalars,
                *on_chip(*arrays),
                *[pltpu.with_memory_space_constraint(array, pltpu.HBM) for array in raw],
            )

        return run

    strip = f32(planes, blocks, rim, LANES)
    packed_edge = f32(planes, rim, LANES)
    packed_mid = f32(planes, band // 2, LANES)
    turned, left_edge, right_edge, left_mid, right_mid = call(
        pack_kernel,
        [f32(planes, blocks - 1, tile_r, LANES)] + [packed_edge] * 2 + [packed_mid] * 2,
        4,
    )(tile)
    from_left = neighbour(right_edge, "col", 1)
    from_right = neighbour(left_edge, "col", -1)
    mid_left = neighbour(right_mid, "col", 1)
    mid_right = neighbour(left_mid, "col", -1)
    up, down, tables = call(
        rows_kernel,
        [strip, strip, pltpu.VMEM(tables.shape, tables.dtype)],
        4,
        scratch=[pltpu.SemaphoreType.DMA(())],
        raw=[tables],
    )(turned, from_left, from_right)
    from_up = neighbour(down, "row", 1)
    from_down = neighbour(up, "row", -1)

    field_shape = f32(planes, blocks, tile_r + frame, LANES)
    work = [field_shape] + [pltpu.VMEM((GROUP, 2, frame, frame), jnp.float32)] * 4
    pieces = [
        strip,
        strip,
        f32(planes, blocks, 2 * rim, LANES),
        f32(planes, band, LANES),
        f32(planes, blocks - 2, band, LANES),
        f32(planes, band, LANES),
    ]
    field, top, bottom, edges, left, mid, right = call(
        first_kernel, [field_shape] + pieces, 20, scratch=work, scalars=[pos]
    )(turned, up, down, mid_left, mid_right, from_up, from_down, amps, probe, tables)

    for iteration in range(1, ITERS):
        mid_left = neighbour(right, "col", 1)
        mid_right = neighbour(left, "col", -1)
        from_up = neighbour(bottom, "row", 1)
        from_down = neighbour(top, "row", -1)
        edge_parts = call(
            fold_kernel,
            [
                f32(planes, 2 * rim, LANES),
                f32(planes, blocks - 2, 2 * rim, LANES),
                f32(planes, 2 * rim, LANES),
            ],
            4,
        )(edges, from_up, from_down)
        from_left = neighbour(edge_parts[2], "col", 1)
        from_right = neighbour(edge_parts[0], "col", -1)
        up, down = call(total_kernel, [strip, strip], 4)(*edge_parts, from_left, from_right)
        from_up = neighbour(down, "row", 1)
        from_down = neighbour(up, "row", -1)
        last = iteration == ITERS - 1
        field, top, bottom, edges, left, mid, right, *packed = call(
            next_kernel,
            [field_shape] + pieces + [packed_mid] * (2 * last),
            20,
            scratch=work,
            scalars=[pos],
        )(
            field, up, down, left, mid, right, mid_left, mid_right, from_up, from_down,
            amps, probe, tables,
        )

    mid_left = neighbour(packed[1], "col", 1)
    mid_right = neighbour(packed[0], "col", -1)
    from_up = neighbour(bottom, "row", 1)
    from_down = neighbour(top, "row", -1)
    edges, edge_left, edge_right = call(
        last_fold_kernel, [f32(planes, blocks, 2 * rim, LANES)] + [packed_edge] * 2, 4
    )(edges, from_up, from_down)
    edge_left, edge_right = neighbour(edge_right, "col", 1), neighbour(edge_left, "col", -1)
    (out,) = call(finish_kernel, [jax.ShapeDtypeStruct((planes, tile_r, tile_c), jnp.float32)], 8)(
        field, edges, left, mid, right, mid_left, mid_right, edge_left, edge_right
    )
    return out.reshape(object_slices.shape)


def solution(mesh):
    in_specs = (
        P(None, None, "row", "col"),
        P(),
        P("row", "col", None, None, None),
        P(None, "row", "col", None),
        P("row", "col"),
    )
    out_specs = P(None, None, "row", "col")

    return jax.shard_map(body, mesh=mesh, in_specs=in_specs, out_specs=out_specs, check_vma=False)
```

```python
import math

import jax
import jax.numpy as jnp
import ml_dtypes
import numpy as np
from jax import lax
from jax.experimental import pallas as pl
from jax.experimental.pallas import tpu as pltpu
from jax.sharding import PartitionSpec as P

ITERS = 2
LANES = 128
GROUP = 4

modulus_offset = 0.5
fresnel_scale = 0.9


def split_table(table):
    high = table.astype(np.float32).astype(ml_dtypes.bfloat16)
    low = (table - high.astype(np.float64)).astype(np.float32).astype(ml_dtypes.bfloat16)
    return high, low


def transform_tables(frame_size):
    positions = np.arange(frame_size)
    dft = np.exp(-2j * math.pi * (positions[:, None] * positions[None, :] % frame_size) / frame_size)
    dft = dft / math.sqrt(frame_size)
    frequency = np.where(positions < frame_size // 2, positions, positions - frame_size)
    phase = np.exp(1j * math.pi * fresnel_scale * frequency.astype(np.float64) ** 2 / frame_size)
    hop = (np.conj(dft) * phase[None, :]) @ dft
    tables = []
    for matrix in (dft, hop):
        re, im = matrix.real, matrix.imag
        right = np.block([[re, im], [-im, re]])
        left = np.block([[re, -im], [im, re]])
        for table in (right, left):
            tables.extend(split_table(table))
    return np.stack(tables)


DFT_RIGHT, DFT_LEFT, HOP_RIGHT, HOP_LEFT = 0, 2, 4, 6


def exchange(odd_values, even_values, axis):
    count = lax.axis_size(axis)
    received = []
    for values, first in ((odd_values, 1), (even_values, 0)):
        lower = range(first, count - 1, 2)
        pairs = [(i, i + 1) for i in lower] + [(i + 1, i) for i in lower]
        received.append(lax.ppermute(values, axis, pairs))
    return received


def paired(axis, before, after):
    even = lax.rem(lax.axis_index(axis), 2) == 0
    return jnp.where(even, before, after), jnp.where(even, after, before)


def lane_ids(shape):
    return lax.broadcasted_iota(jnp.int32, shape, len(shape) - 1)


def swap_halves(values):
    return pltpu.roll(values, LANES // 2, values.ndim - 1)


def vmem():
    return pl.BlockSpec(memory_space=pltpu.VMEM)


def smem():
    return pl.BlockSpec(memory_space=pltpu.SMEM)


def split(values):
    high = values.astype(jnp.bfloat16)
    return high, (values - high.astype(jnp.float32)).astype(jnp.bfloat16)


def dot(a, b):
    return jnp.dot(a, b, preferred_element_type=jnp.float32)


def blend(first, second):
    return jnp.where(lane_ids(first.shape) < LANES // 2, first, second)


def segments(rows, rim):
    half = rows // 2
    return ((slice(0, rim), slice(rows - rim, rows)), (slice(rim, half), slice(half, rows - rim)))


def pack_kernel(object_ref, turned_ref, odd_edge, even_edge, odd_mid, even_mid):
    planes, rows, cols = object_ref.shape
    tiles = cols // LANES
    pieces = segments(rows, odd_edge.shape[1])
    for plane in range(planes):
        for (upper, lower), odd_ref, even_ref in zip(
            pieces, (odd_edge, odd_mid), (even_edge, even_mid)
        ):
            left = blend(
                object_ref[plane, lower, 0:LANES], swap_halves(object_ref[plane, upper, 0:LANES])
            )
            right = blend(
                swap_halves(object_ref[plane, upper, cols - LANES : cols]),
                object_ref[plane, lower, cols - LANES : cols],
            )
            odd_ref[plane], even_ref[plane] = paired("col", left, right)
    for plane in range(planes):
        for tile in range(tiles):
            turned_ref[plane, tile] = swap_halves(
                object_ref[plane, :, tile * LANES : (tile + 1) * LANES]
            )


def lay(turned_ref, plane, rows, left, right, put):
    tiles = turned_ref.shape[1]
    parts = [left] + [turned_ref[plane, tile, rows, :] for tile in range(tiles)] + [right]
    for block in range(tiles + 1):
        put(block, blend(parts[block], parts[block + 1]))


def rows_kernel(
    turned_ref, from_odd, from_even, tables_hbm, up_ref, down_ref, odd_ref, even_ref, tables_ref, sem
):
    copy = pltpu.make_async_copy(tables_hbm, tables_ref, sem)
    copy.start()
    planes, _, rows, _ = turned_ref.shape
    rim = up_ref.shape[2]
    (upper, lower), _ = segments(rows, rim)
    for plane in range(planes):

        def put_up(block, values):
            up_ref[plane, block] = values

        def put_down(block, values):
            down_ref[plane, block] = values

        left, right = paired("col", from_odd[plane], from_even[plane])
        lay(turned_ref, plane, upper, left, right, put_up)
        lay(turned_ref, plane, lower, swap_halves(left), swap_halves(right), put_down)
    odd_ref[...], even_ref[...] = paired("row", up_ref[...], down_ref[...])
    copy.wait()


def gradients(pos_ref, amps_ref, probe_ref, tables_ref, field_ref, grad_ref, work):
    frame = probe_ref.shape[-1]
    o0, o1, inc, wave = work
    count = pos_ref[2, 0]
    lanes = lane_ids((frame, LANES))

    grad_ref[...] = jnp.zeros_like(grad_ref)

    def right(source, index):
        table_high, table_low = tables_ref[index], tables_ref[index + 1]
        high, low = split(source)
        return dot(high, table_high) + (dot(low, table_high) + dot(high, table_low))

    def left(source, index):
        table_high, table_low = tables_ref[index], tables_ref[index + 1]
        high, low = split(source)
        return dot(table_high, high) + (dot(table_high, low) + dot(table_low, high))

    def two_sided(zs, right_index, left_index):
        result = []
        for pair in range(0, len(zs), 2):
            rows = jnp.concatenate([jnp.concatenate(z, axis=1) for z in zs[pair : pair + 2]], axis=0)
            out = right(rows, right_index)
            mixed = left(
                jnp.concatenate(
                    [
                        jnp.concatenate([out[:frame, :frame], out[frame:, :frame]], axis=1),
                        jnp.concatenate([out[:frame, frame:], out[frame:, frame:]], axis=1),
                    ],
                    axis=0,
                ),
                left_index,
            )
            for k in range(2):
                cols = slice(k * frame, (k + 1) * frame)
                result.append((mixed[:frame, cols], mixed[frame:, cols]))
        return result

    def group_step(group, carry):
        base = group * GROUP
        where = []
        for k in range(GROUP):
            row_at, col_at = pos_ref[0, base + k], pos_ref[1, base + k]
            block = lax.shift_right_logical(col_at, 7)
            shift = jnp.bitwise_and(col_at, LANES - 1)
            where.append((pl.ds(row_at, frame), block, shift))
            for plane in range(4):
                near = field_ref[plane, block, pl.ds(row_at, frame), :]
                far = field_ref[plane, block + 1, pl.ds(row_at, frame), :]
                joined = jnp.where(lanes >= shift, near, far)
                target = o0 if plane < 2 else o1
                target[k, plane % 2] = pltpu.roll(
                    joined, jnp.bitwise_and(LANES - shift, LANES - 1), 1
                )
        probe_re, probe_im = probe_ref[0], probe_ref[1]
        zs = []
        for k in range(GROUP):
            a, b = o0[k, 0], o0[k, 1]
            zs.append((probe_re * a - probe_im * b, probe_re * b + probe_im * a))
        for k, (re, im) in enumerate(two_sided(zs, HOP_RIGHT, HOP_LEFT)):
            inc[k, 0] = re
            inc[k, 1] = im
        zs = []
        for k in range(GROUP):
            a, b, c, d = inc[k, 0], inc[k, 1], o1[k, 0], o1[k, 1]
            zs.append((a * c - b * d, a * d + b * c))
        for k, (re, im) in enumerate(two_sided(zs, DFT_RIGHT, DFT_LEFT)):
            live = jnp.where(base + k < count, 1.0, 0.0)
            factor = (1.0 - amps_ref[base + k] * lax.rsqrt(re * re + im * im + modulus_offset)) * live
            wave[k, 0] = re * factor
            wave[k, 1] = im * factor
        zs = [(wave[k, 0], wave[k, 1]) for k in range(GROUP)]

        def place(k, first_plane, values):
            rows, block, shift = where[k]
            for part in range(2):
                moved = pltpu.roll(values[part], shift, 1)
                near = jnp.where(lanes >= shift, moved, 0.0)
                far = jnp.where(lanes >= shift, 0.0, moved)
                grad_ref[first_plane + part, block, rows, :] += near
                grad_ref[first_plane + part, block + 1, rows, :] += far

        for k, (re, im) in enumerate(two_sided(zs, DFT_LEFT, DFT_RIGHT)):
            wave[k, 0] = re
            wave[k, 1] = im
        zs = []
        for k in range(GROUP):
            re, im = wave[k, 0], wave[k, 1]
            a, b, c, d = inc[k, 0], inc[k, 1], o1[k, 0], o1[k, 1]
            place(k, 2, (a * re + b * im, a * im - b * re))
            zs.append((c * re + d * im, c * im - d * re))
        for k, (re, im) in enumerate(two_sided(zs, HOP_LEFT, HOP_RIGHT)):
            place(k, 0, (probe_re * re + probe_im * im, probe_re * im - probe_im * re))
        return carry

    lax.fori_loop(0, (count + GROUP - 1) // GROUP, group_step, 0)


def write_grad(grad_ref, pieces):
    row_odd, row_even, edges, left, mid, right, band_odd, band_even = pieces
    _, blocks, all_rows, _ = grad_ref.shape
    rim = row_odd.shape[2]
    rows = all_rows - 2 * rim
    row_odd[...], row_even[...] = paired(
        "row", grad_ref[:, :, 0:rim, :], grad_ref[:, :, rim + rows : all_rows, :]
    )
    edges[:, :, 0:rim, :] = grad_ref[:, :, rim : 2 * rim, :]
    edges[:, :, rim : 2 * rim, :] = grad_ref[:, :, rows : rim + rows, :]
    left[...] = grad_ref[:, 0, 2 * rim : rows, :]
    mid[...] = grad_ref[:, 1 : blocks - 1, 2 * rim : rows, :]
    right[...] = grad_ref[:, blocks - 1, 2 * rim : rows, :]
    if band_odd.shape[1] == rows - 2 * rim:
        band_odd[...], band_even[...] = paired("col", left[...], right[...])
    else:
        half = (rows - 2 * rim) // 2
        upper, lower = slice(2 * rim, 2 * rim + half), slice(2 * rim + half, rows)
        pack_bands(grad_ref, (band_odd, band_even), upper, lower)


def pack_bands(ref, packed, upper, lower):
    last = ref.shape[1] - 1
    for plane in range(ref.shape[0]):
        packed[0][plane], packed[1][plane] = paired(
            "col",
            blend(ref[plane, 0, upper, :], swap_halves(ref[plane, 0, lower, :])),
            blend(swap_halves(ref[plane, last, lower, :]), ref[plane, last, upper, :]),
        )


def first_kernel(
    pos_ref, turned_ref, up_ref, down_ref, from_odd, from_even, row_odd, row_even,
    amps_ref, probe_ref, tables_ref, field_ref, *rest,
):
    pieces, (grad_ref, *work) = rest[:-5], rest[-5:]
    planes, _, rows, _ = turned_ref.shape
    rim = up_ref.shape[2]
    _, (upper, lower) = segments(rows, rim)
    field_ref[:, :, 0:rim, :], field_ref[:, :, rows + rim : rows + 2 * rim, :] = paired(
        "row", row_odd[...], row_even[...]
    )
    field_ref[:, :, rim : 2 * rim, :] = up_ref[...]
    field_ref[:, :, rows : rows + rim, :] = down_ref[...]
    for plane in range(planes):

        def put_upper(block, values):
            field_ref[plane, block, rim + upper.start : rim + upper.stop, :] = values

        def put_lower(block, values):
            field_ref[plane, block, rim + lower.start : rim + lower.stop, :] = values

        left, right = paired("col", from_odd[plane], from_even[plane])
        lay(turned_ref, plane, upper, left, right, put_upper)
        lay(turned_ref, plane, lower, swap_halves(left), swap_halves(right), put_lower)
    gradients(pos_ref, amps_ref, probe_ref, tables_ref, field_ref, grad_ref, work)
    write_grad(grad_ref, pieces)


def folded(edges, row_odd, row_even, plane, block):
    rim = row_odd.shape[2]
    from_up, from_down = paired("row", row_odd[plane, block], row_even[plane, block])
    return (
        edges[plane, block, 0:rim, :] + from_up, edges[plane, block, rim : 2 * rim, :] + from_down
    )


def fold_kernel(edges, row_odd, row_even, folded_ref, odd_ref, even_ref):
    planes, blocks = edges.shape[:2]
    rim = row_odd.shape[2]
    for plane in range(planes):
        for block in range(blocks):
            upper, lower = folded(edges, row_odd, row_even, plane, block)
            folded_ref[plane, block, 0:rim, :] = upper
            folded_ref[plane, block, rim : 2 * rim, :] = lower
    if odd_ref.shape[1] == 2 * rim:
        odd_ref[...], even_ref[...] = paired("col", folded_ref[:, 0], folded_ref[:, blocks - 1])
    else:
        pack_bands(folded_ref, (odd_ref, even_ref), slice(0, rim), slice(rim, 2 * rim))


def total_kernel(folded_ref, from_odd, from_even, up_ref, down_ref, odd_ref, even_ref):
    planes, blocks, rim, _ = up_ref.shape
    for plane in range(planes):
        left, right = paired("col", from_odd[plane], from_even[plane])
        for block in range(blocks):
            values = folded_ref[plane, block]
            if block == 0:
                values += left
            if block == blocks - 1:
                values += right
            up_ref[plane, block] = values[0:rim]
            down_ref[plane, block] = values[rim : 2 * rim]
    odd_ref[...], even_ref[...] = paired("row", up_ref[...], down_ref[...])


def next_kernel(
    pos_ref, old_ref, up_ref, down_ref, left_ref, mid_ref, right_ref,
    from_odd, from_even, row_odd, row_even, amps_ref, probe_ref, tables_ref, field_ref, *rest,
):
    pieces, (grad_ref, *work) = rest[:-5], rest[-5:]
    _, blocks, all_rows, _ = old_ref.shape
    rim = up_ref.shape[2]
    rows = all_rows - 2 * rim
    from_left, from_right = paired("col", from_odd[...], from_even[...])
    for block in range(blocks):
        lane = lane_ids((1, 1, LANES))
        from_up, from_down = paired("row", row_odd[:, block], row_even[:, block])
        inside = lane >= 0
        middle = mid_ref[:, block - 1] if 0 < block < blocks - 1 else None
        if block == 0:
            inside = lane >= pos_ref[2, 1] * (LANES // 2)
            middle = left_ref[...] + from_left
        if block == blocks - 1:
            inside = lane < LANES - pos_ref[2, 2] * (LANES // 2)
            middle = right_ref[...] + from_right
        for lo, hi, values in (
            (0, rim, from_up),
            (rim, 2 * rim, up_ref[:, block]),
            (2 * rim, rows, middle),
            (rows, rows + rim, down_ref[:, block]),
            (rows + rim, all_rows, from_down),
        ):
            updated = old_ref[:, block, lo:hi, :] - values
            field_ref[:, block, lo:hi, :] = jnp.where(inside, updated, 0.0)
    gradients(pos_ref, amps_ref, probe_ref, tables_ref, field_ref, grad_ref, work)
    write_grad(grad_ref, pieces)


def finish_kernel(
    field_ref, edges, left_ref, mid_ref, right_ref,
    mid_odd, mid_even, edge_odd, edge_even, out_ref,
):
    planes, blocks, _, _ = field_ref.shape
    rows = out_ref.shape[1]
    rim = edge_odd.shape[1]
    (first, last), (upper, lower) = segments(rows, rim)
    half = upper.stop - upper.start

    def whole(plane, part, edge):
        size = rim if edge else half
        at = slice(part * size, (part + 1) * size)
        values = [
            edges[plane, block, at, :] if edge
            else left_ref[plane, at, :] if block == 0
            else right_ref[plane, at, :] if block == blocks - 1
            else mid_ref[plane, block - 1, at, :]
            for block in range(blocks)
        ]
        odd, even = (edge_odd, edge_even) if edge else (mid_odd, mid_even)
        extras = paired("col", odd[plane], even[plane])
        if part == 1:
            extras = [swap_halves(extra) for extra in extras]
        values[0] += extras[0]
        values[-1] += extras[1]
        return values

    for plane in range(planes):
        for part, edge, at in ((0, True, first), (0, False, upper), (1, False, lower), (1, True, last)):
            values = whole(plane, part, edge)
            turned = [
                swap_halves(field_ref[plane, block, rim + at.start : rim + at.stop, :] - values[block])
                for block in range(blocks)
            ]
            for block in range(blocks - 1):
                out_ref[plane, at, block * LANES : (block + 1) * LANES] = blend(
                    turned[block], turned[block + 1]
                )


def f32(*shape):
    return pltpu.VMEM(shape, jnp.float32)


def on_chip(*arrays):
    return [pltpu.with_memory_space_constraint(array, pltpu.VMEM) for array in arrays]


def body(object_slices, probe, amplitudes, scan_pos, scan_count):
    layers, _, tile_r, tile_c = object_slices.shape
    planes = layers * 2
    frame = probe.shape[-1]
    rim = frame // 2
    blocks = tile_c // LANES + 1
    slots = amplitudes.shape[2]
    row_id, col_id = lax.axis_index("row"), lax.axis_index("col")
    amps = amplitudes[0, 0]
    flags = jnp.stack(
        [
            scan_count[0, 0],
            (col_id == 0).astype(jnp.int32),
            (col_id == lax.axis_size("col") - 1).astype(jnp.int32),
        ]
    )
    pos = jnp.stack(
        [
            scan_pos[0, 0, 0] - row_id * tile_r,
            scan_pos[1, 0, 0] - col_id * tile_c,
            jnp.pad(flags, (0, slots - 3)),
        ]
    )
    tables = jnp.asarray(transform_tables(frame))
    tile = object_slices.reshape(planes, tile_r, tile_c)

    band = tile_r - 2 * rim

    def call(kernel, outs, mib, scratch=(), scalars=(), raw=()):
        def run(*arrays):
            return pl.pallas_call(
                kernel,
                out_shape=outs,
                in_specs=[smem()] * len(scalars) + [vmem()] * len(arrays)
                + [pl.BlockSpec(memory_space=pltpu.HBM)] * len(raw),
                out_specs=[vmem()] * len(outs),
                scratch_shapes=list(scratch),
                compiler_params=pltpu.CompilerParams(vmem_limit_bytes=mib << 20),
            )(
                *scalars,
                *on_chip(*arrays),
                *[pltpu.with_memory_space_constraint(array, pltpu.HBM) for array in raw],
            )

        return run

    strip = f32(planes, blocks, rim, LANES)
    packed_edge = f32(planes, rim, LANES)
    packed_mid = f32(planes, band // 2, LANES)
    packed_both = [packed_edge] * 2
    turned, odd_edge, even_edge, odd_mid, even_mid = call(
        pack_kernel,
        [f32(planes, blocks - 1, tile_r, LANES)] + packed_both + [packed_mid] * 2,
        4,
    )(tile)
    edge_strips = exchange(odd_edge, even_edge, "col")
    mid_strips = exchange(odd_mid, even_mid, "col")
    up, down, odd, even, tables = call(
        rows_kernel,
        [strip] * 4 + [pltpu.VMEM(tables.shape, tables.dtype)],
        4,
        scratch=[pltpu.SemaphoreType.DMA(())],
        raw=[tables],
    )(turned, *edge_strips)
    row_strips = exchange(odd, even, "row")

    field_shape = f32(planes, blocks, tile_r + frame, LANES)
    work = [field_shape] + [pltpu.VMEM((GROUP, 2, frame, frame), jnp.float32)] * 4
    edge_rows = f32(planes, blocks, 2 * rim, LANES)
    pieces = [
        strip,
        strip,
        edge_rows,
        f32(planes, band, LANES),
        f32(planes, blocks - 2, band, LANES),
        f32(planes, band, LANES),
    ]
    field, *grads = call(
        first_kernel, [field_shape] + pieces + [f32(planes, band, LANES)] * 2, 20,
        scratch=work, scalars=[pos],
    )(turned, up, down, *mid_strips, *row_strips, amps, probe, tables)

    for iteration in range(1, ITERS):
        odd, even, edges, left, mid, right, band_odd, band_even = grads
        row_strips = exchange(odd, even, "row")
        mid_strips = exchange(band_odd, band_even, "col")
        edges, odd, even = call(
            fold_kernel, [edge_rows] + [f32(planes, 2 * rim, LANES)] * 2, 4
        )(edges, *row_strips)
        edge_strips = exchange(odd, even, "col")
        up, down, odd, even = call(total_kernel, [strip] * 4, 4)(edges, *edge_strips)
        row_strips = exchange(odd, even, "row")
        bands = [f32(planes, band, LANES)] * 2 if iteration < ITERS - 1 else [packed_mid] * 2
        field, *grads = call(
            next_kernel, [field_shape] + pieces + bands, 20, scratch=work, scalars=[pos]
        )(field, up, down, left, mid, right, *mid_strips, *row_strips, amps, probe, tables)

    odd, even, edges, left, mid, right, band_odd, band_even = grads
    row_strips = exchange(odd, even, "row")
    mid_strips = exchange(band_odd, band_even, "col")
    edges, odd, even = call(fold_kernel, [edge_rows] + packed_both, 4)(edges, *row_strips)
    edge_strips = exchange(odd, even, "col")
    (out,) = call(finish_kernel, [jax.ShapeDtypeStruct((planes, tile_r, tile_c), jnp.float32)], 8)(
        field, edges, left, mid, right, *mid_strips, *edge_strips
    )
    return out.reshape(object_slices.shape)


def solution(mesh):
    in_specs = (
        P(None, None, "row", "col"),
        P(),
        P("row", "col", None, None, None),
        P(None, "row", "col", None),
        P("row", "col"),
    )
    out_specs = P(None, None, "row", "col")

    return jax.shard_map(body, mesh=mesh, in_specs=in_specs, out_specs=out_specs, check_vma=False)
```

```python
import math

import jax
import jax.numpy as jnp
import ml_dtypes
import numpy as np
from jax import lax
from jax.experimental import pallas as pl
from jax.experimental.pallas import tpu as pltpu
from jax.sharding import PartitionSpec as P

ITERS = 2
LANES = 128
GROUP = 8

modulus_offset = 0.5
fresnel_scale = 0.9


def split_table(table):
    high = table.astype(np.float32).astype(ml_dtypes.bfloat16)
    low = (table - high.astype(np.float64)).astype(np.float32).astype(ml_dtypes.bfloat16)
    return high, low


def transform_tables(frame_size):
    positions = np.arange(frame_size)
    dft = np.exp(-2j * math.pi * (positions[:, None] * positions[None, :] % frame_size) / frame_size)
    dft = dft / math.sqrt(frame_size)
    frequency = np.where(positions < frame_size // 2, positions, positions - frame_size)
    phase = np.exp(1j * math.pi * fresnel_scale * frequency.astype(np.float64) ** 2 / frame_size)
    hop = (np.conj(dft) * phase[None, :]) @ dft
    tables = []
    for matrix in (dft, hop):
        re, im = matrix.real, matrix.imag
        right = np.block([[re, im], [-im, re]])
        left = np.block([[re, -im], [im, re]])
        for table in (right, left):
            tables.extend(split_table(table))
    return np.stack(tables)


DFT_RIGHT, DFT_LEFT, HOP_RIGHT, HOP_LEFT = 0, 2, 4, 6


def exchange(odd_values, even_values, axis):
    count = lax.axis_size(axis)
    received = []
    for values, first in ((odd_values, 1), (even_values, 0)):
        lower = range(first, count - 1, 2)
        pairs = [(i, i + 1) for i in lower] + [(i + 1, i) for i in lower]
        received.append(lax.ppermute(values, axis, pairs))
    return received


def paired(axis, before, after):
    even = lax.rem(lax.axis_index(axis), 2) == 0
    return jnp.where(even, before, after), jnp.where(even, after, before)


def lane_ids(shape):
    return lax.broadcasted_iota(jnp.int32, shape, len(shape) - 1)


def swap_halves(values):
    return pltpu.roll(values, LANES // 2, values.ndim - 1)


def vmem():
    return pl.BlockSpec(memory_space=pltpu.VMEM)


def smem():
    return pl.BlockSpec(memory_space=pltpu.SMEM)


def split(values):
    high = values.astype(jnp.bfloat16)
    return high, (values - high.astype(jnp.float32)).astype(jnp.bfloat16)


def dot(a, b):
    return jnp.dot(a, b, preferred_element_type=jnp.float32)


def blend(first, second):
    return jnp.where(lane_ids(first.shape) < LANES // 2, first, second)


def segments(rows, rim):
    half = rows // 2
    return ((slice(0, rim), slice(rows - rim, rows)), (slice(rim, half), slice(half, rows - rim)))


def pack_kernel(object_ref, turned_ref, odd_edge, even_edge, odd_mid, even_mid):
    planes, rows, cols = object_ref.shape
    tiles = cols // LANES
    pieces = segments(rows, odd_edge.shape[1])
    for plane in range(planes):
        for (upper, lower), odd_ref, even_ref in zip(
            pieces, (odd_edge, odd_mid), (even_edge, even_mid)
        ):
            left = blend(
                object_ref[plane, lower, 0:LANES], swap_halves(object_ref[plane, upper, 0:LANES])
            )
            right = blend(
                swap_halves(object_ref[plane, upper, cols - LANES : cols]),
                object_ref[plane, lower, cols - LANES : cols],
            )
            odd_ref[plane], even_ref[plane] = paired("col", left, right)
    for plane in range(planes):
        for tile in range(tiles):
            turned_ref[plane, tile] = swap_halves(
                object_ref[plane, :, tile * LANES : (tile + 1) * LANES]
            )


def lay(turned_ref, plane, rows, left, right, put):
    tiles = turned_ref.shape[1]
    parts = [left] + [turned_ref[plane, tile, rows, :] for tile in range(tiles)] + [right]
    for block in range(tiles + 1):
        put(block, blend(parts[block], parts[block + 1]))


def load_kernel(source_hbm, target_ref, sem):
    copy = pltpu.make_async_copy(source_hbm, target_ref, sem)
    copy.start()
    copy.wait()


def rows_kernel(turned_ref, from_odd, from_even, up_ref, down_ref, odd_ref, even_ref):
    planes, _, rows, _ = turned_ref.shape
    rim = up_ref.shape[2]
    (upper, lower), _ = segments(rows, rim)
    for plane in range(planes):

        def put_up(block, values):
            up_ref[plane, block] = values

        def put_down(block, values):
            down_ref[plane, block] = values

        left, right = paired("col", from_odd[plane], from_even[plane])
        lay(turned_ref, plane, upper, left, right, put_up)
        lay(turned_ref, plane, lower, swap_halves(left), swap_halves(right), put_down)
    odd_ref[...], even_ref[...] = paired("row", up_ref[...], down_ref[...])


def gradients(pos_ref, amps_ref, probe_ref, tables_ref, field_ref, grad_ref, work):
    frame = probe_ref.shape[-1]
    o0, o1, inc, wave = work
    count = pos_ref[2, 0]
    lanes = lane_ids((frame, LANES))

    grad_ref[...] = jnp.zeros_like(grad_ref)

    def right(source, index):
        table_high, table_low = tables_ref[index], tables_ref[index + 1]
        high, low = split(source)
        return dot(high, table_high) + (dot(low, table_high) + dot(high, table_low))

    def left(source, index):
        table_high, table_low = tables_ref[index], tables_ref[index + 1]
        high, low = split(source)
        return dot(table_high, high) + (dot(table_high, low) + dot(table_low, high))

    def two_sided(zs, right_index, left_index):
        outs = [
            right(
                jnp.concatenate([jnp.concatenate(z, axis=1) for z in zs[pair : pair + 2]], axis=0),
                right_index,
            )
            for pair in range(0, len(zs), 2)
        ]
        mixes = [
            left(
                jnp.concatenate(
                    [
                        jnp.concatenate([out[:frame, :frame], out[frame:, :frame]], axis=1),
                        jnp.concatenate([out[:frame, frame:], out[frame:, frame:]], axis=1),
                    ],
                    axis=0,
                ),
                left_index,
            )
            for out in outs
        ]
        result = []
        for mixed in mixes:
            for k in range(2):
                cols = slice(k * frame, (k + 1) * frame)
                result.append((mixed[:frame, cols], mixed[frame:, cols]))
        return result

    def group_step(group, carry):
        base = group * GROUP
        where = []
        for k in range(GROUP):
            row_at, col_at = pos_ref[0, base + k], pos_ref[1, base + k]
            block = lax.shift_right_logical(col_at, 7)
            shift = jnp.bitwise_and(col_at, LANES - 1)
            where.append((pl.ds(row_at, frame), block, shift))
            for plane in range(4):
                near = field_ref[plane, block, pl.ds(row_at, frame), :]
                far = field_ref[plane, block + 1, pl.ds(row_at, frame), :]
                joined = jnp.where(lanes >= shift, near, far)
                target = o0 if plane < 2 else o1
                target[k, plane % 2] = pltpu.roll(
                    joined, jnp.bitwise_and(LANES - shift, LANES - 1), 1
                )
        probe_re, probe_im = probe_ref[0], probe_ref[1]
        zs = []
        for k in range(GROUP):
            a, b = o0[k, 0], o0[k, 1]
            zs.append((probe_re * a - probe_im * b, probe_re * b + probe_im * a))
        for k, (re, im) in enumerate(two_sided(zs, HOP_RIGHT, HOP_LEFT)):
            inc[k, 0] = re
            inc[k, 1] = im
        zs = []
        for k in range(GROUP):
            a, b, c, d = inc[k, 0], inc[k, 1], o1[k, 0], o1[k, 1]
            zs.append((a * c - b * d, a * d + b * c))
        for k, (re, im) in enumerate(two_sided(zs, DFT_RIGHT, DFT_LEFT)):
            live = jnp.where(base + k < count, 1.0, 0.0)
            factor = (1.0 - amps_ref[base + k] * lax.rsqrt(re * re + im * im + modulus_offset)) * live
            wave[k, 0] = re * factor
            wave[k, 1] = im * factor
        zs = [(wave[k, 0], wave[k, 1]) for k in range(GROUP)]

        def place(k, first_plane, values):
            rows, block, shift = where[k]
            for part in range(2):
                moved = pltpu.roll(values[part], shift, 1)
                near = jnp.where(lanes >= shift, moved, 0.0)
                far = jnp.where(lanes >= shift, 0.0, moved)
                grad_ref[first_plane + part, block, rows, :] += near
                grad_ref[first_plane + part, block + 1, rows, :] += far

        for k, (re, im) in enumerate(two_sided(zs, DFT_LEFT, DFT_RIGHT)):
            wave[k, 0] = re
            wave[k, 1] = im
        zs = []
        for k in range(GROUP):
            re, im = wave[k, 0], wave[k, 1]
            a, b, c, d = inc[k, 0], inc[k, 1], o1[k, 0], o1[k, 1]
            place(k, 2, (a * re + b * im, a * im - b * re))
            zs.append((c * re + d * im, c * im - d * re))
        for k, (re, im) in enumerate(two_sided(zs, HOP_LEFT, HOP_RIGHT)):
            place(k, 0, (probe_re * re + probe_im * im, probe_re * im - probe_im * re))
        return carry

    lax.fori_loop(0, (count + GROUP - 1) // GROUP, group_step, 0)


def write_grad(grad_ref, pieces):
    row_odd, row_even, edges, left, mid, right, band_odd, band_even = pieces
    _, blocks, all_rows, _ = grad_ref.shape
    rim = row_odd.shape[2]
    rows = all_rows - 2 * rim
    row_odd[...], row_even[...] = paired(
        "row", grad_ref[:, :, 0:rim, :], grad_ref[:, :, rim + rows : all_rows, :]
    )
    edges[:, :, 0:rim, :] = grad_ref[:, :, rim : 2 * rim, :]
    edges[:, :, rim : 2 * rim, :] = grad_ref[:, :, rows : rim + rows, :]
    left[...] = grad_ref[:, 0, 2 * rim : rows, :]
    mid[...] = grad_ref[:, 1 : blocks - 1, 2 * rim : rows, :]
    right[...] = grad_ref[:, blocks - 1, 2 * rim : rows, :]
    if band_odd.shape[1] == rows - 2 * rim:
        band_odd[...], band_even[...] = paired("col", left[...], right[...])
    else:
        half = (rows - 2 * rim) // 2
        upper, lower = slice(2 * rim, 2 * rim + half), slice(2 * rim + half, rows)
        pack_bands(grad_ref, (band_odd, band_even), upper, lower)


def pack_bands(ref, packed, upper, lower):
    last = ref.shape[1] - 1
    for plane in range(ref.shape[0]):
        packed[0][plane], packed[1][plane] = paired(
            "col",
            blend(ref[plane, 0, upper, :], swap_halves(ref[plane, 0, lower, :])),
            blend(swap_halves(ref[plane, last, lower, :]), ref[plane, last, upper, :]),
        )


def first_kernel(
    pos_ref, turned_ref, up_ref, down_ref, from_odd, from_even, row_odd, row_even,
    amps_ref, probe_ref, tables_ref, field_ref, *rest,
):
    pieces, (grad_ref, *work) = rest[:-5], rest[-5:]
    planes, _, rows, _ = turned_ref.shape
    rim = up_ref.shape[2]
    _, (upper, lower) = segments(rows, rim)
    field_ref[:, :, 0:rim, :], field_ref[:, :, rows + rim : rows + 2 * rim, :] = paired(
        "row", row_odd[...], row_even[...]
    )
    field_ref[:, :, rim : 2 * rim, :] = up_ref[...]
    field_ref[:, :, rows : rows + rim, :] = down_ref[...]
    for plane in range(planes):

        def put_upper(block, values):
            field_ref[plane, block, rim + upper.start : rim + upper.stop, :] = values

        def put_lower(block, values):
            field_ref[plane, block, rim + lower.start : rim + lower.stop, :] = values

        left, right = paired("col", from_odd[plane], from_even[plane])
        lay(turned_ref, plane, upper, left, right, put_upper)
        lay(turned_ref, plane, lower, swap_halves(left), swap_halves(right), put_lower)
    gradients(pos_ref, amps_ref, probe_ref, tables_ref, field_ref, grad_ref, work)
    write_grad(grad_ref, pieces)


def folded(edges, row_odd, row_even, plane, block):
    rim = row_odd.shape[2]
    from_up, from_down = paired("row", row_odd[plane, block], row_even[plane, block])
    return (
        edges[plane, block, 0:rim, :] + from_up, edges[plane, block, rim : 2 * rim, :] + from_down
    )


def fold_kernel(edges, row_odd, row_even, folded_ref, odd_ref, even_ref):
    planes, blocks = edges.shape[:2]
    rim = row_odd.shape[2]
    for plane in range(planes):
        for block in range(blocks):
            upper, lower = folded(edges, row_odd, row_even, plane, block)
            folded_ref[plane, block, 0:rim, :] = upper
            folded_ref[plane, block, rim : 2 * rim, :] = lower
    if odd_ref.shape[1] == 2 * rim:
        odd_ref[...], even_ref[...] = paired("col", folded_ref[:, 0], folded_ref[:, blocks - 1])
    else:
        pack_bands(folded_ref, (odd_ref, even_ref), slice(0, rim), slice(rim, 2 * rim))


def total_kernel(folded_ref, from_odd, from_even, up_ref, down_ref, odd_ref, even_ref):
    planes, blocks, rim, _ = up_ref.shape
    for plane in range(planes):
        left, right = paired("col", from_odd[plane], from_even[plane])
        for block in range(blocks):
            values = folded_ref[plane, block]
            if block == 0:
                values += left
            if block == blocks - 1:
                values += right
            up_ref[plane, block] = values[0:rim]
            down_ref[plane, block] = values[rim : 2 * rim]
    odd_ref[...], even_ref[...] = paired("row", up_ref[...], down_ref[...])


def next_kernel(
    pos_ref, old_ref, up_ref, down_ref, left_ref, mid_ref, right_ref,
    from_odd, from_even, row_odd, row_even, amps_ref, probe_ref, tables_ref, field_ref, *rest,
):
    pieces, (grad_ref, *work) = rest[:-5], rest[-5:]
    _, blocks, all_rows, _ = old_ref.shape
    rim = up_ref.shape[2]
    rows = all_rows - 2 * rim
    from_left, from_right = paired("col", from_odd[...], from_even[...])
    for block in range(blocks):
        lane = lane_ids((1, 1, LANES))
        from_up, from_down = paired("row", row_odd[:, block], row_even[:, block])
        inside = lane >= 0
        middle = mid_ref[:, block - 1] if 0 < block < blocks - 1 else None
        if block == 0:
            inside = lane >= pos_ref[2, 1] * (LANES // 2)
            middle = left_ref[...] + from_left
        if block == blocks - 1:
            inside = lane < LANES - pos_ref[2, 2] * (LANES // 2)
            middle = right_ref[...] + from_right
        for lo, hi, values in (
            (0, rim, from_up),
            (rim, 2 * rim, up_ref[:, block]),
            (2 * rim, rows, middle),
            (rows, rows + rim, down_ref[:, block]),
            (rows + rim, all_rows, from_down),
        ):
            updated = old_ref[:, block, lo:hi, :] - values
            field_ref[:, block, lo:hi, :] = jnp.where(inside, updated, 0.0)
    gradients(pos_ref, amps_ref, probe_ref, tables_ref, field_ref, grad_ref, work)
    write_grad(grad_ref, pieces)


def finish_kernel(
    field_ref, edges, left_ref, mid_ref, right_ref,
    mid_odd, mid_even, edge_odd, edge_even, out_ref,
):
    planes, blocks, _, _ = field_ref.shape
    rows = out_ref.shape[1]
    rim = edge_odd.shape[1]
    (first, last), (upper, lower) = segments(rows, rim)
    half = upper.stop - upper.start

    def whole(plane, part, edge):
        size = rim if edge else half
        at = slice(part * size, (part + 1) * size)
        values = [
            edges[plane, block, at, :] if edge
            else left_ref[plane, at, :] if block == 0
            else right_ref[plane, at, :] if block == blocks - 1
            else mid_ref[plane, block - 1, at, :]
            for block in range(blocks)
        ]
        odd, even = (edge_odd, edge_even) if edge else (mid_odd, mid_even)
        extras = paired("col", odd[plane], even[plane])
        if part == 1:
            extras = [swap_halves(extra) for extra in extras]
        values[0] += extras[0]
        values[-1] += extras[1]
        return values

    for plane in range(planes):
        for part, edge, at in ((0, True, first), (0, False, upper), (1, False, lower), (1, True, last)):
            values = whole(plane, part, edge)
            turned = [
                swap_halves(field_ref[plane, block, rim + at.start : rim + at.stop, :] - values[block])
                for block in range(blocks)
            ]
            for block in range(blocks - 1):
                out_ref[plane, at, block * LANES : (block + 1) * LANES] = blend(
                    turned[block], turned[block + 1]
                )


def f32(*shape):
    return pltpu.VMEM(shape, jnp.float32)


def on_chip(*arrays):
    return [pltpu.with_memory_space_constraint(array, pltpu.VMEM) for array in arrays]


def body(object_slices, probe, amplitudes, scan_pos, scan_count):
    layers, _, tile_r, tile_c = object_slices.shape
    planes = layers * 2
    frame = probe.shape[-1]
    rim = frame // 2
    blocks = tile_c // LANES + 1
    slots = amplitudes.shape[2]
    row_id, col_id = lax.axis_index("row"), lax.axis_index("col")
    amps = amplitudes[0, 0]
    flags = jnp.stack(
        [
            scan_count[0, 0],
            (col_id == 0).astype(jnp.int32),
            (col_id == lax.axis_size("col") - 1).astype(jnp.int32),
        ]
    )
    pos = jnp.stack(
        [
            scan_pos[0, 0, 0] - row_id * tile_r,
            scan_pos[1, 0, 0] - col_id * tile_c,
            jnp.pad(flags, (0, slots - 3)),
        ]
    )
    tables = jnp.asarray(transform_tables(frame))
    tile = object_slices.reshape(planes, tile_r, tile_c)

    band = tile_r - 2 * rim

    def call(kernel, outs, mib, scratch=(), scalars=(), raw=()):
        def run(*arrays):
            return pl.pallas_call(
                kernel,
                out_shape=outs,
                in_specs=[smem()] * len(scalars) + [vmem()] * len(arrays)
                + [pl.BlockSpec(memory_space=pltpu.HBM)] * len(raw),
                out_specs=[vmem()] * len(outs),
                scratch_shapes=list(scratch),
                compiler_params=pltpu.CompilerParams(vmem_limit_bytes=mib << 20),
            )(
                *scalars,
                *on_chip(*arrays),
                *[pltpu.with_memory_space_constraint(array, pltpu.HBM) for array in raw],
            )

        return run

    strip = f32(planes, blocks, rim, LANES)
    packed_edge = f32(planes, rim, LANES)
    packed_mid = f32(planes, band // 2, LANES)
    packed_both = [packed_edge] * 2
    turned, odd_edge, even_edge, odd_mid, even_mid = call(
        pack_kernel,
        [f32(planes, blocks - 1, tile_r, LANES)] + packed_both + [packed_mid] * 2,
        4,
    )(tile)
    edge_strips = exchange(odd_edge, even_edge, "col")
    mid_strips = exchange(odd_mid, even_mid, "col")
    up, down, odd, even = call(rows_kernel, [strip] * 4, 4)(turned, *edge_strips)
    (tables,) = call(
        load_kernel,
        [pltpu.VMEM(tables.shape, tables.dtype)],
        4,
        scratch=[pltpu.SemaphoreType.DMA(())],
        raw=[tables],
    )()
    row_strips = exchange(odd, even, "row")

    field_shape = f32(planes, blocks, tile_r + frame, LANES)
    work = [field_shape] + [pltpu.VMEM((GROUP, 2, frame, frame), jnp.float32)] * 4
    edge_rows = f32(planes, blocks, 2 * rim, LANES)
    pieces = [
        strip,
        strip,
        edge_rows,
        f32(planes, band, LANES),
        f32(planes, blocks - 2, band, LANES),
        f32(planes, band, LANES),
    ]
    field, *grads = call(
        first_kernel, [field_shape] + pieces + [f32(planes, band, LANES)] * 2, 20,
        scratch=work, scalars=[pos],
    )(turned, up, down, *mid_strips, *row_strips, amps, probe, tables)

    for iteration in range(1, ITERS):
        odd, even, edges, left, mid, right, band_odd, band_even = grads
        row_strips = exchange(odd, even, "row")
        mid_strips = exchange(band_odd, band_even, "col")
        edges, odd, even = call(
            fold_kernel, [edge_rows] + [f32(planes, 2 * rim, LANES)] * 2, 4
        )(edges, *row_strips)
        edge_strips = exchange(odd, even, "col")
        up, down, odd, even = call(total_kernel, [strip] * 4, 4)(edges, *edge_strips)
        row_strips = exchange(odd, even, "row")
        bands = [f32(planes, band, LANES)] * 2 if iteration < ITERS - 1 else [packed_mid] * 2
        field, *grads = call(
            next_kernel, [field_shape] + pieces + bands, 20, scratch=work, scalars=[pos]
        )(field, up, down, left, mid, right, *mid_strips, *row_strips, amps, probe, tables)

    odd, even, edges, left, mid, right, band_odd, band_even = grads
    row_strips = exchange(odd, even, "row")
    mid_strips = exchange(band_odd, band_even, "col")
    edges, odd, even = call(fold_kernel, [edge_rows] + packed_both, 4)(edges, *row_strips)
    edge_strips = exchange(odd, even, "col")
    (out,) = call(finish_kernel, [jax.ShapeDtypeStruct((planes, tile_r, tile_c), jnp.float32)], 8)(
        field, edges, left, mid, right, *mid_strips, *edge_strips
    )
    return out.reshape(object_slices.shape)


def solution(mesh):
    in_specs = (
        P(None, None, "row", "col"),
        P(),
        P("row", "col", None, None, None),
        P(None, "row", "col", None),
        P("row", "col"),
    )
    out_specs = P(None, None, "row", "col")

    return jax.shard_map(body, mesh=mesh, in_specs=in_specs, out_specs=out_specs, check_vma=False)
```

```python
import math

import jax
import jax.numpy as jnp
import ml_dtypes
import numpy as np
from jax import lax
from jax.experimental import pallas as pl
from jax.experimental.pallas import tpu as pltpu
from jax.sharding import PartitionSpec as P

ITERS = 2
LANES = 128
GROUP = 8

modulus_offset = 0.5
fresnel_scale = 0.9


def split_table(table):
    high = table.astype(np.float32).astype(ml_dtypes.bfloat16)
    low = (table - high.astype(np.float64)).astype(np.float32).astype(ml_dtypes.bfloat16)
    return high, low


def transform_tables(frame_size):
    positions = np.arange(frame_size)
    dft = np.exp(-2j * math.pi * (positions[:, None] * positions[None, :] % frame_size) / frame_size)
    dft = dft / math.sqrt(frame_size)
    frequency = np.where(positions < frame_size // 2, positions, positions - frame_size)
    phase = np.exp(1j * math.pi * fresnel_scale * frequency.astype(np.float64) ** 2 / frame_size)
    hop = (np.conj(dft) * phase[None, :]) @ dft
    tables = []
    for matrix in (dft, hop):
        re, im = matrix.real, matrix.imag
        right = np.block([[re, im], [-im, re]])
        left = np.block([[re, -im], [im, re]])
        for table in (right, left):
            tables.extend(split_table(table))
    return np.stack(tables)


DFT_RIGHT, DFT_LEFT, HOP_RIGHT, HOP_LEFT = 0, 2, 4, 6


def exchange(odd_values, even_values, axis):
    count = lax.axis_size(axis)
    received = []
    for values, first in ((odd_values, 1), (even_values, 0)):
        lower = range(first, count - 1, 2)
        pairs = [(i, i + 1) for i in lower] + [(i + 1, i) for i in lower]
        received.append(lax.ppermute(values, axis, pairs))
    return received


def paired(axis, before, after):
    even = lax.rem(lax.axis_index(axis), 2) == 0
    return jnp.where(even, before, after), jnp.where(even, after, before)


def lane_ids(shape):
    return lax.broadcasted_iota(jnp.int32, shape, len(shape) - 1)


def swap_halves(values):
    return pltpu.roll(values, LANES // 2, values.ndim - 1)


def vmem():
    return pl.BlockSpec(memory_space=pltpu.VMEM)


def smem():
    return pl.BlockSpec(memory_space=pltpu.SMEM)


def split(values):
    high = values.astype(jnp.bfloat16)
    return high, (values - high.astype(jnp.float32)).astype(jnp.bfloat16)


def dot(a, b):
    return jnp.dot(a, b, preferred_element_type=jnp.float32)


def blend(first, second):
    return jnp.where(lane_ids(first.shape) < LANES // 2, first, second)


def segments(rows, rim):
    half = rows // 2
    return ((slice(0, rim), slice(rows - rim, rows)), (slice(rim, half), slice(half, rows - rim)))


def pack_kernel(
    object_ref, turned_ref, odd_edge, even_edge, odd_mid, even_mid, row_odd, row_even
):
    planes, rows, cols = object_ref.shape
    tiles = cols // LANES
    pieces = segments(rows, odd_edge.shape[1])
    for plane in range(planes):
        for (upper, lower), odd_ref, even_ref in zip(
            pieces, (odd_edge, odd_mid), (even_edge, even_mid)
        ):
            left = blend(
                object_ref[plane, lower, 0:LANES], swap_halves(object_ref[plane, upper, 0:LANES])
            )
            right = blend(
                swap_halves(object_ref[plane, upper, cols - LANES : cols]),
                object_ref[plane, lower, cols - LANES : cols],
            )
            odd_ref[plane], even_ref[plane] = paired("col", left, right)
    for plane in range(planes):
        for tile in range(tiles):
            turned = swap_halves(object_ref[plane, :, tile * LANES : (tile + 1) * LANES])
            turned_ref[plane, tile] = turned
            upper, lower = pieces[0]
            row_odd[plane, tile], row_even[plane, tile] = paired("row", turned[upper], turned[lower])


def lay(turned_ref, plane, rows, left, right, field_ref, row_at):
    tiles = turned_ref.shape[1]
    parts = [left] + [turned_ref[plane, tile, rows, :] for tile in range(tiles)] + [right]
    for block in range(tiles + 1):
        field_ref[plane, block, row_at : row_at + rows.stop - rows.start, :] = blend(
            parts[block], parts[block + 1]
        )


def load_kernel(*refs):
    count = len(refs) // 3
    copies = [
        pltpu.make_async_copy(refs[k], refs[count + k], refs[2 * count + k]) for k in range(count)
    ]
    for copy in copies:
        copy.start()
    for copy in copies:
        copy.wait()


def corner_kernel(from_odd, from_even, odd_ref, even_ref):
    for plane in range(odd_ref.shape[0]):
        left, right = paired("col", from_odd[plane], from_even[plane])
        odd_ref[plane], even_ref[plane] = paired(
            "row", blend(left, right), swap_halves(blend(right, left))
        )


def gradients(pos_ref, amps_ref, probe_ref, tables_ref, field_ref, grad_ref, work):
    frame = probe_ref.shape[-1]
    o0, o1, inc, wave = work
    count = pos_ref[2, 0]
    lanes = lane_ids((frame, LANES))

    grad_ref[...] = jnp.zeros_like(grad_ref)

    def right(source, index):
        table_high, table_low = tables_ref[index], tables_ref[index + 1]
        high, low = split(source)
        return dot(high, table_high) + (dot(low, table_high) + dot(high, table_low))

    def left(source, index):
        table_high, table_low = tables_ref[index], tables_ref[index + 1]
        high, low = split(source)
        return dot(table_high, high) + (dot(table_high, low) + dot(table_low, high))

    def two_sided(zs, right_index, left_index):
        outs = [
            right(
                jnp.concatenate([jnp.concatenate(z, axis=1) for z in zs[pair : pair + 2]], axis=0),
                right_index,
            )
            for pair in range(0, len(zs), 2)
        ]
        mixes = [
            left(
                jnp.concatenate(
                    [
                        jnp.concatenate([out[:frame, :frame], out[frame:, :frame]], axis=1),
                        jnp.concatenate([out[:frame, frame:], out[frame:, frame:]], axis=1),
                    ],
                    axis=0,
                ),
                left_index,
            )
            for out in outs
        ]
        result = []
        for mixed in mixes:
            for k in range(2):
                cols = slice(k * frame, (k + 1) * frame)
                result.append((mixed[:frame, cols], mixed[frame:, cols]))
        return result

    def group_step(group, carry):
        base = group * GROUP
        where = []
        for k in range(GROUP):
            row_at, col_at = pos_ref[0, base + k], pos_ref[1, base + k]
            block = lax.shift_right_logical(col_at, 7)
            shift = jnp.bitwise_and(col_at, LANES - 1)
            where.append((pl.ds(row_at, frame), block, shift))
            for plane in range(4):
                near = field_ref[plane, block, pl.ds(row_at, frame), :]
                far = field_ref[plane, block + 1, pl.ds(row_at, frame), :]
                joined = jnp.where(lanes >= shift, near, far)
                target = o0 if plane < 2 else o1
                target[k, plane % 2] = pltpu.roll(
                    joined, jnp.bitwise_and(LANES - shift, LANES - 1), 1
                )
        probe_re, probe_im = probe_ref[0], probe_ref[1]
        zs = []
        for k in range(GROUP):
            a, b = o0[k, 0], o0[k, 1]
            zs.append((probe_re * a - probe_im * b, probe_re * b + probe_im * a))
        for k, (re, im) in enumerate(two_sided(zs, HOP_RIGHT, HOP_LEFT)):
            inc[k, 0] = re
            inc[k, 1] = im
        zs = []
        for k in range(GROUP):
            a, b, c, d = inc[k, 0], inc[k, 1], o1[k, 0], o1[k, 1]
            zs.append((a * c - b * d, a * d + b * c))
        for k, (re, im) in enumerate(two_sided(zs, DFT_RIGHT, DFT_LEFT)):
            live = jnp.where(base + k < count, 1.0, 0.0)
            factor = (1.0 - amps_ref[base + k] * lax.rsqrt(re * re + im * im + modulus_offset)) * live
            wave[k, 0] = re * factor
            wave[k, 1] = im * factor
        zs = [(wave[k, 0], wave[k, 1]) for k in range(GROUP)]

        def place(k, first_plane, values):
            rows, block, shift = where[k]
            for part in range(2):
                moved = pltpu.roll(values[part], shift, 1)
                near = jnp.where(lanes >= shift, moved, 0.0)
                far = jnp.where(lanes >= shift, 0.0, moved)
                grad_ref[first_plane + part, block, rows, :] += near
                grad_ref[first_plane + part, block + 1, rows, :] += far

        for k, (re, im) in enumerate(two_sided(zs, DFT_LEFT, DFT_RIGHT)):
            wave[k, 0] = re
            wave[k, 1] = im
        zs = []
        for k in range(GROUP):
            re, im = wave[k, 0], wave[k, 1]
            a, b, c, d = inc[k, 0], inc[k, 1], o1[k, 0], o1[k, 1]
            place(k, 2, (a * re + b * im, a * im - b * re))
            zs.append((c * re + d * im, c * im - d * re))
        for k, (re, im) in enumerate(two_sided(zs, HOP_LEFT, HOP_RIGHT)):
            place(k, 0, (probe_re * re + probe_im * im, probe_re * im - probe_im * re))
        return carry

    lax.fori_loop(0, (count + GROUP - 1) // GROUP, group_step, 0)


def outer(blocks):
    return (0, blocks - 1)


def inner(blocks):
    return range(1, blocks - 1)


def write_grad(grad_ref, pieces):
    (
        row_odd, row_even, row_mid_odd, row_mid_even, edges, edges_mid, left, mid, right,
        band_odd, band_even,
    ) = pieces
    _, blocks, all_rows, _ = grad_ref.shape
    rim = row_odd.shape[2]
    rows = all_rows - 2 * rim
    for odd, even, edge, group in (
        (row_odd, row_even, edges, outer(blocks)),
        (row_mid_odd, row_mid_even, edges_mid, inner(blocks)),
    ):
        for at, block in enumerate(group):
            odd[:, at], even[:, at] = paired(
                "row", grad_ref[:, block, 0:rim, :], grad_ref[:, block, rim + rows : all_rows, :]
            )
            edge[:, at, 0:rim, :] = grad_ref[:, block, rim : 2 * rim, :]
            edge[:, at, rim : 2 * rim, :] = grad_ref[:, block, rows : rim + rows, :]
    left[...] = grad_ref[:, 0, 2 * rim : rows, :]
    mid[...] = grad_ref[:, 1 : blocks - 1, 2 * rim : rows, :]
    right[...] = grad_ref[:, blocks - 1, 2 * rim : rows, :]
    if band_odd.shape[1] == rows - 2 * rim:
        band_odd[...], band_even[...] = paired("col", left[...], right[...])
    else:
        half = (rows - 2 * rim) // 2
        upper, lower = slice(2 * rim, 2 * rim + half), slice(2 * rim + half, rows)
        pack_bands(grad_ref, (band_odd, band_even), upper, lower)


def pack_bands(ref, packed, upper, lower):
    last = ref.shape[1] - 1
    for plane in range(ref.shape[0]):
        packed[0][plane], packed[1][plane] = paired(
            "col",
            blend(ref[plane, 0, upper, :], swap_halves(ref[plane, 0, lower, :])),
            blend(swap_halves(ref[plane, last, lower, :]), ref[plane, last, upper, :]),
        )


def first_kernel(
    pos_ref, turned_ref, edge_odd, edge_even, mid_odd, mid_even, row_odd, row_even,
    corner_odd, corner_even, amps_ref, probe_ref, tables_ref, field_ref, *rest,
):
    pieces, (grad_ref, *work) = rest[:-5], rest[-5:]
    planes, _, rows, _ = turned_ref.shape
    rim = edge_odd.shape[1]
    for plane in range(planes):
        for (upper, lower), odd, even in zip(
            segments(rows, rim), (edge_odd, mid_odd), (edge_even, mid_even)
        ):
            left, right = paired("col", odd[plane], even[plane])
            lay(turned_ref, plane, upper, left, right, field_ref, rim + upper.start)
            left, right = swap_halves(left), swap_halves(right)
            lay(turned_ref, plane, lower, left, right, field_ref, rim + lower.start)
        corners = paired("row", corner_odd[plane], corner_even[plane])
        rims = paired("row", row_odd[plane], row_even[plane])
        for strip, corner, row_at in zip(rims, corners, (0, rows + rim)):
            parts = [corner, *strip, corner]
            for block in range(len(parts) - 1):
                field_ref[plane, block, row_at : row_at + rim, :] = blend(
                    parts[block], parts[block + 1]
                )
    gradients(pos_ref, amps_ref, probe_ref, tables_ref, field_ref, grad_ref, work)
    write_grad(grad_ref, pieces)


def fold(edges, row_odd, row_even, plane, at):
    rim = row_odd.shape[2]
    from_up, from_down = paired("row", row_odd[plane, at], row_even[plane, at])
    return edges[plane, at, 0:rim, :] + from_up, edges[plane, at, rim : 2 * rim, :] + from_down


def fold_kernel(edges, row_odd, row_even, folded_ref, odd_ref, even_ref):
    planes, count = edges.shape[:2]
    rim = row_odd.shape[2]
    for plane in range(planes):
        for at in range(count):
            upper, lower = fold(edges, row_odd, row_even, plane, at)
            folded_ref[plane, at, 0:rim, :] = upper
            folded_ref[plane, at, rim : 2 * rim, :] = lower
    if odd_ref.shape[1] == 2 * rim:
        odd_ref[...], even_ref[...] = paired("col", folded_ref[:, 0], folded_ref[:, count - 1])
    else:
        pack_bands(folded_ref, (odd_ref, even_ref), slice(0, rim), slice(rim, 2 * rim))


def fold_mid_kernel(edges, row_odd, row_even, up_ref, down_ref, odd_ref, even_ref):
    for plane in range(edges.shape[0]):
        for at in range(edges.shape[1]):
            upper, lower = fold(edges, row_odd, row_even, plane, at)
            up_ref[plane, at], down_ref[plane, at] = upper, lower
            odd_ref[plane, at], even_ref[plane, at] = paired("row", upper, lower)


def total_kernel(folded_ref, from_odd, from_even, up_ref, down_ref, odd_ref, even_ref):
    planes, count, rim, _ = up_ref.shape
    for plane in range(planes):
        sides = paired("col", from_odd[plane], from_even[plane])
        for at in range(count):
            values = folded_ref[plane, at] + sides[at]
            upper, lower = values[0:rim], values[rim : 2 * rim]
            up_ref[plane, at], down_ref[plane, at] = upper, lower
            odd_ref[plane, at], even_ref[plane, at] = paired("row", upper, lower)


def next_kernel(
    pos_ref, old_ref, up_ref, down_ref, up_mid, down_mid, left_ref, mid_ref, right_ref,
    from_odd, from_even, row_odd, row_even, row_mid_odd, row_mid_even,
    amps_ref, probe_ref, tables_ref, field_ref, *rest,
):
    pieces, (grad_ref, *work) = rest[:-5], rest[-5:]
    _, blocks, all_rows, _ = old_ref.shape
    rim = up_ref.shape[2]
    rows = all_rows - 2 * rim
    from_left, from_right = paired("col", from_odd[...], from_even[...])
    for block in range(blocks):
        lane = lane_ids((1, 1, LANES))
        inside = lane >= 0
        if block in inner(blocks):
            at, odd, even, up, down = block - 1, row_mid_odd, row_mid_even, up_mid, down_mid
            middle = mid_ref[:, at]
        elif block == 0:
            at, odd, even, up, down = 0, row_odd, row_even, up_ref, down_ref
            inside = lane >= pos_ref[2, 1] * (LANES // 2)
            middle = left_ref[...] + from_left
        else:
            at, odd, even, up, down = 1, row_odd, row_even, up_ref, down_ref
            inside = lane < LANES - pos_ref[2, 2] * (LANES // 2)
            middle = right_ref[...] + from_right
        from_up, from_down = paired("row", odd[:, at], even[:, at])
        for lo, hi, values in (
            (0, rim, from_up),
            (rim, 2 * rim, up[:, at]),
            (2 * rim, rows, middle),
            (rows, rows + rim, down[:, at]),
            (rows + rim, all_rows, from_down),
        ):
            updated = old_ref[:, block, lo:hi, :] - values
            field_ref[:, block, lo:hi, :] = jnp.where(inside, updated, 0.0)
    gradients(pos_ref, amps_ref, probe_ref, tables_ref, field_ref, grad_ref, work)
    write_grad(grad_ref, pieces)


def finish_kernel(
    field_ref, edges, edges_mid, row_odd, row_even, left_ref, mid_ref, right_ref,
    mid_odd, mid_even, edge_odd, edge_even, out_ref,
):
    planes, blocks, _, _ = field_ref.shape
    rows = out_ref.shape[1]
    rim = edge_odd.shape[1]
    (first, last), (upper, lower) = segments(rows, rim)
    half = upper.stop - upper.start

    def whole(plane, part, edge):
        size = rim if edge else half
        at = slice(part * size, (part + 1) * size)
        if edge:
            values = [edges[plane, 0, at, :], edges[plane, 1, at, :]]
            values[1:1] = [
                fold(edges_mid, row_odd, row_even, plane, k)[part] for k in range(blocks - 2)
            ]
        else:
            values = [left_ref[plane, at, :], right_ref[plane, at, :]]
            values[1:1] = [mid_ref[plane, k, at, :] for k in range(blocks - 2)]
        odd, even = (edge_odd, edge_even) if edge else (mid_odd, mid_even)
        extras = paired("col", odd[plane], even[plane])
        if part == 1:
            extras = [swap_halves(extra) for extra in extras]
        values[0] += extras[0]
        values[-1] += extras[1]
        return values

    for plane in range(planes):
        for part, edge, at in ((0, True, first), (0, False, upper), (1, False, lower), (1, True, last)):
            values = whole(plane, part, edge)
            turned = [
                swap_halves(field_ref[plane, block, rim + at.start : rim + at.stop, :] - values[block])
                for block in range(blocks)
            ]
            for block in range(blocks - 1):
                out_ref[plane, at, block * LANES : (block + 1) * LANES] = blend(
                    turned[block], turned[block + 1]
                )


def f32(*shape):
    return pltpu.VMEM(shape, jnp.float32)


def on_chip(*arrays):
    return [pltpu.with_memory_space_constraint(array, pltpu.VMEM) for array in arrays]


def body(object_slices, probe, amplitudes, scan_pos, scan_count):
    layers, _, tile_r, tile_c = object_slices.shape
    planes = layers * 2
    frame = probe.shape[-1]
    rim = frame // 2
    blocks = tile_c // LANES + 1
    slots = amplitudes.shape[2]
    row_id, col_id = lax.axis_index("row"), lax.axis_index("col")
    amps = amplitudes[0, 0]
    flags = jnp.stack(
        [
            scan_count[0, 0],
            (col_id == 0).astype(jnp.int32),
            (col_id == lax.axis_size("col") - 1).astype(jnp.int32),
        ]
    )
    pos = jnp.stack(
        [
            scan_pos[0, 0, 0] - row_id * tile_r,
            scan_pos[1, 0, 0] - col_id * tile_c,
            jnp.pad(flags, (0, slots - 3)),
        ]
    )
    tables = jnp.asarray(transform_tables(frame))
    tile = object_slices.reshape(planes, tile_r, tile_c)

    band = tile_r - 2 * rim

    def call(kernel, outs, mib, scratch=(), scalars=(), raw=()):
        def run(*arrays):
            return pl.pallas_call(
                kernel,
                out_shape=outs,
                in_specs=[smem()] * len(scalars) + [vmem()] * len(arrays)
                + [pl.BlockSpec(memory_space=pltpu.HBM)] * len(raw),
                out_specs=[vmem()] * len(outs),
                scratch_shapes=list(scratch),
                compiler_params=pltpu.CompilerParams(vmem_limit_bytes=mib << 20),
            )(
                *scalars,
                *on_chip(*arrays),
                *[pltpu.with_memory_space_constraint(array, pltpu.HBM) for array in raw],
            )

        return run

    packed_edge = f32(planes, rim, LANES)
    packed_mid = f32(planes, band // 2, LANES)
    row_strip = f32(planes, blocks - 1, rim, LANES)
    turned, odd_edge, even_edge, odd_mid, even_mid, odd, even = call(
        pack_kernel,
        [f32(planes, blocks - 1, tile_r, LANES)]
        + [packed_edge] * 2 + [packed_mid] * 2 + [row_strip] * 2,
        4,
    )(tile)
    edge_strips = exchange(odd_edge, even_edge, "col")
    row_strips = exchange(odd, even, "row")
    mid_strips = exchange(odd_mid, even_mid, "col")
    constants = (tables, amps, probe)
    tables, amps, probe = call(
        load_kernel,
        [pltpu.VMEM(array.shape, array.dtype) for array in constants],
        4,
        scratch=[pltpu.SemaphoreType.DMA(())] * len(constants),
        raw=constants,
    )()
    odd, even = call(corner_kernel, [packed_edge] * 2, 4)(*edge_strips)
    corner_strips = exchange(odd, even, "row")

    field_shape = f32(planes, blocks, tile_r + frame, LANES)
    work = [field_shape] + [pltpu.VMEM((GROUP, 2, frame, frame), jnp.float32)] * 4
    strip, strip_mid = f32(planes, 2, rim, LANES), f32(planes, blocks - 2, rim, LANES)
    edge_rows = f32(planes, 2, 2 * rim, LANES)
    band_rows = f32(planes, band, LANES)
    pieces = [strip] * 2 + [strip_mid] * 2 + [
        edge_rows,
        f32(planes, blocks - 2, 2 * rim, LANES),
        band_rows,
        f32(planes, blocks - 2, band, LANES),
        band_rows,
    ]
    field, *grads = call(
        first_kernel,
        [field_shape] + pieces + [band_rows] * 2,
        20,
        scratch=work,
        scalars=[pos],
    )(turned, *edge_strips, *mid_strips, *row_strips, *corner_strips, amps, probe, tables)

    for iteration in range(1, ITERS):
        odd, even, odd_in, even_in, edges, edges_mid, left, mid, right, band_odd, band_even = grads
        row_strips = exchange(odd, even, "row")
        mid_strips = exchange(band_odd, band_even, "col")
        inner_strips = exchange(odd_in, even_in, "row")
        edges, odd, even = call(
            fold_kernel, [edge_rows] + [f32(planes, 2 * rim, LANES)] * 2, 4
        )(edges, *row_strips)
        edge_strips = exchange(odd, even, "col")
        up_mid, down_mid, odd_in, even_in = call(fold_mid_kernel, [strip_mid] * 4, 4)(
            edges_mid, *inner_strips
        )
        inner_strips = exchange(odd_in, even_in, "row")
        up, down, odd, even = call(total_kernel, [strip] * 4, 4)(edges, *edge_strips)
        row_strips = exchange(odd, even, "row")
        bands = [band_rows] * 2 if iteration < ITERS - 1 else [packed_mid] * 2
        field, *grads = call(
            next_kernel, [field_shape] + pieces + bands, 20, scratch=work, scalars=[pos]
        )(
            field, up, down, up_mid, down_mid, left, mid, right,
            *mid_strips, *row_strips, *inner_strips, amps, probe, tables,
        )

    odd, even, odd_in, even_in, edges, edges_mid, left, mid, right, band_odd, band_even = grads
    row_strips = exchange(odd, even, "row")
    mid_strips = exchange(band_odd, band_even, "col")
    inner_strips = exchange(odd_in, even_in, "row")
    edges, odd, even = call(fold_kernel, [edge_rows] + [packed_edge] * 2, 4)(edges, *row_strips)
    edge_strips = exchange(odd, even, "col")
    (out,) = call(finish_kernel, [jax.ShapeDtypeStruct((planes, tile_r, tile_c), jnp.float32)], 8)(
        field, edges, edges_mid, *inner_strips, left, mid, right, *mid_strips, *edge_strips
    )
    return out.reshape(object_slices.shape)


def solution(mesh):
    in_specs = (
        P(None, None, "row", "col"),
        P(),
        P("row", "col", None, None, None),
        P(None, "row", "col", None),
        P("row", "col"),
    )
    out_specs = P(None, None, "row", "col")

    return jax.shard_map(body, mesh=mesh, in_specs=in_specs, out_specs=out_specs, check_vma=False)
```

```python
import math

import jax
import jax.numpy as jnp
import ml_dtypes
import numpy as np
from jax import lax
from jax.experimental import pallas as pl
from jax.experimental.pallas import tpu as pltpu
from jax.sharding import PartitionSpec as P

ITERS = 2
LANES = 128
GROUP = 8

modulus_offset = 0.5
fresnel_scale = 0.9


def split_table(table):
    high = table.astype(np.float32).astype(ml_dtypes.bfloat16)
    low = (table - high.astype(np.float64)).astype(np.float32).astype(ml_dtypes.bfloat16)
    return high, low


def transform_tables(frame_size):
    positions = np.arange(frame_size)
    dft = np.exp(-2j * math.pi * (positions[:, None] * positions[None, :] % frame_size) / frame_size)
    dft = dft / math.sqrt(frame_size)
    frequency = np.where(positions < frame_size // 2, positions, positions - frame_size)
    phase = np.exp(1j * math.pi * fresnel_scale * frequency.astype(np.float64) ** 2 / frame_size)
    hop = (np.conj(dft) * phase[None, :]) @ dft
    tables = []
    for matrix in (dft, hop):
        re, im = matrix.real, matrix.imag
        right = np.block([[re, im], [-im, re]])
        left = np.block([[re, -im], [im, re]])
        for table in (right, left):
            tables.extend(split_table(table))
    return np.stack(tables)


DFT_RIGHT, DFT_LEFT, HOP_RIGHT, HOP_LEFT = 0, 2, 4, 6


def exchange(odd_values, even_values, axis):
    count = lax.axis_size(axis)
    received = []
    for values, first in ((odd_values, 1), (even_values, 0)):
        lower = range(first, count - 1, 2)
        pairs = [(i, i + 1) for i in lower] + [(i + 1, i) for i in lower]
        received.append(lax.ppermute(values, axis, pairs))
    return received


def paired(axis, before, after):
    even = lax.rem(lax.axis_index(axis), 2) == 0
    return jnp.where(even, before, after), jnp.where(even, after, before)


def lane_ids(shape):
    return lax.broadcasted_iota(jnp.int32, shape, len(shape) - 1)


def swap_halves(values):
    return pltpu.roll(values, LANES // 2, values.ndim - 1)


def vmem():
    return pl.BlockSpec(memory_space=pltpu.VMEM)


def smem():
    return pl.BlockSpec(memory_space=pltpu.SMEM)


def split(values):
    high = values.astype(jnp.bfloat16)
    return high, (values - high.astype(jnp.float32)).astype(jnp.bfloat16)


def dot(a, b):
    return jnp.dot(a, b, preferred_element_type=jnp.float32)


def blend(first, second):
    return jnp.where(lane_ids(first.shape) < LANES // 2, first, second)


def segments(rows, rim):
    half = rows // 2
    return ((slice(0, rim), slice(rows - rim, rows)), (slice(rim, half), slice(half, rows - rim)))


def pack_kernel(
    object_ref, turned_ref, odd_edge, even_edge, odd_mid, even_mid, row_odd, row_even
):
    planes, rows, cols = object_ref.shape
    tiles = cols // LANES
    pieces = segments(rows, odd_edge.shape[1])
    for plane in range(planes):
        for (upper, lower), odd_ref, even_ref in zip(
            pieces, (odd_edge, odd_mid), (even_edge, even_mid)
        ):
            left = blend(
                object_ref[plane, lower, 0:LANES], swap_halves(object_ref[plane, upper, 0:LANES])
            )
            right = blend(
                swap_halves(object_ref[plane, upper, cols - LANES : cols]),
                object_ref[plane, lower, cols - LANES : cols],
            )
            odd_ref[plane], even_ref[plane] = paired("col", left, right)
    for plane in range(planes):
        for tile in range(tiles):
            turned = swap_halves(object_ref[plane, :, tile * LANES : (tile + 1) * LANES])
            turned_ref[plane, tile] = turned
            upper, lower = pieces[0]
            row_odd[plane, tile], row_even[plane, tile] = paired("row", turned[upper], turned[lower])


def lay(turned_ref, plane, rows, left, right, field_ref, row_at):
    tiles = turned_ref.shape[1]
    parts = [left] + [turned_ref[plane, tile, rows, :] for tile in range(tiles)] + [right]
    for block in range(tiles + 1):
        field_ref[plane, block, row_at : row_at + rows.stop - rows.start, :] = blend(
            parts[block], parts[block + 1]
        )


def load_kernel(*refs):
    count = len(refs) // 3
    copies = [
        pltpu.make_async_copy(refs[k], refs[count + k], refs[2 * count + k]) for k in range(count)
    ]
    for copy in copies:
        copy.start()
    for copy in copies:
        copy.wait()


def corner_kernel(from_odd, from_even, odd_ref, even_ref):
    for plane in range(odd_ref.shape[0]):
        left, right = paired("col", from_odd[plane], from_even[plane])
        odd_ref[plane], even_ref[plane] = paired(
            "row", blend(left, right), swap_halves(blend(right, left))
        )


def gradients(pos_ref, count_ref, amps_ref, probe_ref, tables_ref, field_ref, grad_ref, work):
    frame = probe_ref.shape[-1]
    o0, o1, inc, wave = work
    count = count_ref[0, 0]
    first_row = lax.axis_index("row") * (field_ref.shape[2] - frame)
    first_col = lax.axis_index("col") * ((field_ref.shape[1] - 1) * LANES)
    lanes = lane_ids((frame, LANES))

    grad_ref[...] = jnp.zeros_like(grad_ref)

    def right(source, index):
        table_high, table_low = tables_ref[index], tables_ref[index + 1]
        high, low = split(source)
        return dot(high, table_high) + (dot(low, table_high) + dot(high, table_low))

    def left(source, index):
        table_high, table_low = tables_ref[index], tables_ref[index + 1]
        high, low = split(source)
        return dot(table_high, high) + (dot(table_high, low) + dot(table_low, high))

    def two_sided(zs, right_index, left_index):
        outs = [
            right(
                jnp.concatenate([jnp.concatenate(z, axis=1) for z in zs[pair : pair + 2]], axis=0),
                right_index,
            )
            for pair in range(0, len(zs), 2)
        ]
        mixes = [
            left(
                jnp.concatenate(
                    [
                        jnp.concatenate([out[:frame, :frame], out[frame:, :frame]], axis=1),
                        jnp.concatenate([out[:frame, frame:], out[frame:, frame:]], axis=1),
                    ],
                    axis=0,
                ),
                left_index,
            )
            for out in outs
        ]
        result = []
        for mixed in mixes:
            for k in range(2):
                cols = slice(k * frame, (k + 1) * frame)
                result.append((mixed[:frame, cols], mixed[frame:, cols]))
        return result

    def group_step(group, carry):
        base = group * GROUP
        where = []
        for k in range(GROUP):
            row_at = pos_ref[0, 0, 0, base + k] - first_row
            col_at = pos_ref[1, 0, 0, base + k] - first_col
            block = lax.shift_right_logical(col_at, 7)
            shift = jnp.bitwise_and(col_at, LANES - 1)
            where.append((pl.ds(row_at, frame), block, shift))
            for plane in range(4):
                near = field_ref[plane, block, pl.ds(row_at, frame), :]
                far = field_ref[plane, block + 1, pl.ds(row_at, frame), :]
                joined = jnp.where(lanes >= shift, near, far)
                target = o0 if plane < 2 else o1
                target[k, plane % 2] = pltpu.roll(
                    joined, jnp.bitwise_and(LANES - shift, LANES - 1), 1
                )
        probe_re, probe_im = probe_ref[0], probe_ref[1]
        zs = []
        for k in range(GROUP):
            a, b = o0[k, 0], o0[k, 1]
            zs.append((probe_re * a - probe_im * b, probe_re * b + probe_im * a))
        for k, (re, im) in enumerate(two_sided(zs, HOP_RIGHT, HOP_LEFT)):
            inc[k, 0] = re
            inc[k, 1] = im
        zs = []
        for k in range(GROUP):
            a, b, c, d = inc[k, 0], inc[k, 1], o1[k, 0], o1[k, 1]
            zs.append((a * c - b * d, a * d + b * c))
        for k, (re, im) in enumerate(two_sided(zs, DFT_RIGHT, DFT_LEFT)):
            live = jnp.where(base + k < count, 1.0, 0.0)
            factor = (1.0 - amps_ref[base + k] * lax.rsqrt(re * re + im * im + modulus_offset)) * live
            wave[k, 0] = re * factor
            wave[k, 1] = im * factor
        zs = [(wave[k, 0], wave[k, 1]) for k in range(GROUP)]

        def place(k, first_plane, values):
            rows, block, shift = where[k]
            for part in range(2):
                moved = pltpu.roll(values[part], shift, 1)
                near = jnp.where(lanes >= shift, moved, 0.0)
                far = jnp.where(lanes >= shift, 0.0, moved)
                grad_ref[first_plane + part, block, rows, :] += near
                grad_ref[first_plane + part, block + 1, rows, :] += far

        for k, (re, im) in enumerate(two_sided(zs, DFT_LEFT, DFT_RIGHT)):
            wave[k, 0] = re
            wave[k, 1] = im
        zs = []
        for k in range(GROUP):
            re, im = wave[k, 0], wave[k, 1]
            a, b, c, d = inc[k, 0], inc[k, 1], o1[k, 0], o1[k, 1]
            place(k, 2, (a * re + b * im, a * im - b * re))
            zs.append((c * re + d * im, c * im - d * re))
        for k, (re, im) in enumerate(two_sided(zs, HOP_LEFT, HOP_RIGHT)):
            place(k, 0, (probe_re * re + probe_im * im, probe_re * im - probe_im * re))
        return carry

    lax.fori_loop(0, (count + GROUP - 1) // GROUP, group_step, 0)


def outer(blocks):
    return (0, blocks - 1)


def inner(blocks):
    return range(1, blocks - 1)


def write_grad(grad_ref, pieces):
    (
        row_odd, row_even, row_mid_odd, row_mid_even, edges, edges_mid, left, mid, right,
        band_odd, band_even,
    ) = pieces
    _, blocks, all_rows, _ = grad_ref.shape
    rim = row_odd.shape[-2]
    rows = all_rows - 2 * rim
    closing = len(row_odd.shape) == 3

    def row_pieces(block):
        def rows_of(lo):
            if block is outside:
                return blend(grad_ref[:, 0, lo : lo + rim, :], grad_ref[:, blocks - 1, lo : lo + rim, :])
            if block is rest:
                return blend(grad_ref[:, blocks - 1, lo : lo + rim, :], grad_ref[:, 0, lo : lo + rim, :])
            return grad_ref[:, block, lo : lo + rim, :]

        return [rows_of(lo) for lo in (0, rim, rows, rows + rim)]

    outside, rest = object(), object()
    groups = (outer(blocks), inner(blocks))
    if closing:
        groups = ((outside,), (rest, *inner(blocks)))
    for odd, even, edge, group in (
        (row_odd, row_even, edges, groups[0]),
        (row_mid_odd, row_mid_even, edges_mid, groups[1]),
    ):
        for at, block in enumerate(group):
            top, upper, lower, bottom = row_pieces(block)
            view = (slice(None),) if block is outside else (slice(None), at)
            odd[view], even[view] = paired("row", top, bottom)
            edge[*view, 0:rim, :] = upper
            edge[*view, rim : 2 * rim, :] = lower
    left[...] = grad_ref[:, 0, 2 * rim : rows, :]
    mid[...] = grad_ref[:, 1 : blocks - 1, 2 * rim : rows, :]
    right[...] = grad_ref[:, blocks - 1, 2 * rim : rows, :]
    if band_odd.shape[1] == rows - 2 * rim:
        band_odd[...], band_even[...] = paired("col", left[...], right[...])
    else:
        half = (rows - 2 * rim) // 2
        upper, lower = slice(2 * rim, 2 * rim + half), slice(2 * rim + half, rows)
        pack_bands(grad_ref, (band_odd, band_even), upper, lower)


def pack_bands(ref, packed, upper, lower):
    last = ref.shape[1] - 1
    for plane in range(ref.shape[0]):
        packed[0][plane], packed[1][plane] = paired(
            "col",
            blend(ref[plane, 0, upper, :], swap_halves(ref[plane, 0, lower, :])),
            blend(swap_halves(ref[plane, last, lower, :]), ref[plane, last, upper, :]),
        )


def first_kernel(
    pos_ref, count_ref, turned_ref, edge_odd, edge_even, mid_odd, mid_even, row_odd, row_even,
    corner_odd, corner_even, amps_ref, probe_ref, tables_ref, field_ref, *rest,
):
    pieces, (grad_ref, *work) = rest[:-5], rest[-5:]
    planes, _, rows, _ = turned_ref.shape
    rim = edge_odd.shape[1]
    for plane in range(planes):
        for (upper, lower), odd, even in zip(
            segments(rows, rim), (edge_odd, mid_odd), (edge_even, mid_even)
        ):
            left, right = paired("col", odd[plane], even[plane])
            lay(turned_ref, plane, upper, left, right, field_ref, rim + upper.start)
            left, right = swap_halves(left), swap_halves(right)
            lay(turned_ref, plane, lower, left, right, field_ref, rim + lower.start)
        corners = paired("row", corner_odd[plane], corner_even[plane])
        rims = paired("row", row_odd[plane], row_even[plane])
        for strip, corner, row_at in zip(rims, corners, (0, rows + rim)):
            parts = [corner, *strip, corner]
            for block in range(len(parts) - 1):
                field_ref[plane, block, row_at : row_at + rim, :] = blend(
                    parts[block], parts[block + 1]
                )
    gradients(pos_ref, count_ref, amps_ref, probe_ref, tables_ref, field_ref, grad_ref, work)
    write_grad(grad_ref, pieces)


def fold(edges, row_odd, row_even, plane, at):
    rim = row_odd.shape[2]
    from_up, from_down = paired("row", row_odd[plane, at], row_even[plane, at])
    return edges[plane, at, 0:rim, :] + from_up, edges[plane, at, rim : 2 * rim, :] + from_down


def fold_kernel(edges, row_odd, row_even, folded_ref, odd_ref, even_ref):
    planes, count = edges.shape[:2]
    rim = row_odd.shape[2]
    for plane in range(planes):
        for at in range(count):
            upper, lower = fold(edges, row_odd, row_even, plane, at)
            folded_ref[plane, at, 0:rim, :] = upper
            folded_ref[plane, at, rim : 2 * rim, :] = lower
    odd_ref[...], even_ref[...] = paired("col", folded_ref[:, 0], folded_ref[:, count - 1])


def last_fold_kernel(edges, row_odd, row_even, odd_ref, even_ref):
    rim = row_odd.shape[1]
    for plane in range(edges.shape[0]):
        from_up, from_down = paired("row", row_odd[plane], row_even[plane])
        upper = edges[plane, 0:rim, :] + from_up
        lower = swap_halves(edges[plane, rim : 2 * rim, :] + from_down)
        odd_ref[plane], even_ref[plane] = paired("col", blend(upper, lower), blend(lower, upper))


def fold_mid_kernel(edges, row_odd, row_even, up_ref, down_ref, odd_ref, even_ref):
    for plane in range(edges.shape[0]):
        for at in range(edges.shape[1]):
            upper, lower = fold(edges, row_odd, row_even, plane, at)
            up_ref[plane, at], down_ref[plane, at] = upper, lower
            odd_ref[plane, at], even_ref[plane, at] = paired("row", upper, lower)


def total_kernel(folded_ref, from_odd, from_even, up_ref, down_ref, odd_ref, even_ref):
    planes, count, rim, _ = up_ref.shape
    for plane in range(planes):
        sides = paired("col", from_odd[plane], from_even[plane])
        for at in range(count):
            values = folded_ref[plane, at] + sides[at]
            upper, lower = values[0:rim], values[rim : 2 * rim]
            up_ref[plane, at], down_ref[plane, at] = upper, lower
            odd_ref[plane, at], even_ref[plane, at] = paired("row", upper, lower)


def next_kernel(
    pos_ref, count_ref, old_ref, up_ref, down_ref, up_mid, down_mid, left_ref, mid_ref, right_ref,
    from_odd, from_even, row_odd, row_even, row_mid_odd, row_mid_even,
    amps_ref, probe_ref, tables_ref, field_ref, *rest,
):
    pieces, (grad_ref, *work) = rest[:-5], rest[-5:]
    _, blocks, all_rows, _ = old_ref.shape
    rim = up_ref.shape[2]
    rows = all_rows - 2 * rim
    from_left, from_right = paired("col", from_odd[...], from_even[...])
    for block in range(blocks):
        lane = lane_ids((1, 1, LANES))
        inside = lane >= 0
        if block in inner(blocks):
            at, odd, even, up, down = block - 1, row_mid_odd, row_mid_even, up_mid, down_mid
            middle = mid_ref[:, at]
        elif block == 0:
            at, odd, even, up, down = 0, row_odd, row_even, up_ref, down_ref
            inside = lane >= jnp.where(lax.axis_index("col") == 0, LANES // 2, 0)
            middle = left_ref[...] + from_left
        else:
            at, odd, even, up, down = 1, row_odd, row_even, up_ref, down_ref
            at_end = lax.axis_index("col") == lax.axis_size("col") - 1
            inside = lane < jnp.where(at_end, LANES // 2, LANES)
            middle = right_ref[...] + from_right
        from_up, from_down = paired("row", odd[:, at], even[:, at])
        for lo, hi, values in (
            (0, rim, from_up),
            (rim, 2 * rim, up[:, at]),
            (2 * rim, rows, middle),
            (rows, rows + rim, down[:, at]),
            (rows + rim, all_rows, from_down),
        ):
            updated = old_ref[:, block, lo:hi, :] - values
            field_ref[:, block, lo:hi, :] = jnp.where(inside, updated, 0.0)
    gradients(pos_ref, count_ref, amps_ref, probe_ref, tables_ref, field_ref, grad_ref, work)
    write_grad(grad_ref, pieces)


def put_rows(field_ref, plane, row_at, values, sides, part, target_ref, put_at):
    size = values[0].shape[0]
    if part == 1:
        sides = [swap_halves(side) for side in sides]
    values = [values[0] + sides[0], *values[1:-1], values[-1] + sides[1]]
    turned = [
        swap_halves(field_ref[plane, block, row_at : row_at + size, :] - block_values)
        for block, block_values in enumerate(values)
    ]
    for block in range(len(turned) - 1):
        target_ref[plane, put_at : put_at + size, block * LANES : (block + 1) * LANES] = blend(
            turned[block], turned[block + 1]
        )


def finish_mid_kernel(
    field_ref, left_ref, mid_ref, right_ref, from_odd, from_even, out_hbm, result, sem
):
    planes, blocks, all_rows, _ = field_ref.shape
    band = result.shape[1]
    rim = (all_rows - band) // 4
    half = band // 2
    for plane in range(planes):
        sides = paired("col", from_odd[plane], from_even[plane])
        for part in range(2):
            at = slice(part * half, (part + 1) * half)
            values = [left_ref[plane, at, :], right_ref[plane, at, :]]
            values[1:1] = [mid_ref[plane, k, at, :] for k in range(blocks - 2)]
            put_rows(
                field_ref, plane, 2 * rim + part * half, values, sides, part, result, part * half
            )
    copy = pltpu.make_async_copy(result, out_hbm.at[:, rim : rim + band, :], sem)
    copy.start()
    copy.wait()


def finish_edge_kernel(
    field_ref, edges_mid, row_odd, row_even, from_odd, from_even, _, out_hbm, result, *sems
):
    planes, blocks, all_rows, _ = field_ref.shape
    rim = from_odd.shape[1]
    rows = all_rows - 2 * rim
    copies = []
    for part in range(2):
        for plane in range(planes):
            sides = paired("col", from_odd[plane], from_even[plane])
            folded = [fold(edges_mid, row_odd, row_even, plane, k)[part] for k in range(blocks - 1)]
            values = [*folded, folded[0]]
            put_rows(
                field_ref, plane, rim + part * (rows - rim), values, sides, part, result, part * rim
            )
        at = part * (rows - rim)
        copies.append(
            pltpu.make_async_copy(
                result.at[:, part * rim : (part + 1) * rim, :],
                out_hbm.at[:, at : at + rim, :],
                sems[part],
            )
        )
        copies[-1].start()
    for copy in copies:
        copy.wait()


def f32(*shape):
    return pltpu.VMEM(shape, jnp.float32)


def on_chip(*arrays):
    return [pltpu.with_memory_space_constraint(array, pltpu.VMEM) for array in arrays]


def body(object_slices, probe, amplitudes, scan_pos, scan_count):
    layers, _, tile_r, tile_c = object_slices.shape
    planes = layers * 2
    frame = probe.shape[-1]
    rim = frame // 2
    blocks = tile_c // LANES + 1
    slots = amplitudes.shape[2]
    assert slots % GROUP == 0
    amps = amplitudes[0, 0]
    scalars = [scan_pos, scan_count]
    tables = jnp.asarray(transform_tables(frame))
    tile = object_slices.reshape(planes, tile_r, tile_c)

    band = tile_r - 2 * rim

    def call(kernel, outs, mib, scratch=(), scalars=(), raw=(), in_hbm=False, alias=None):
        def run(*arrays):
            return pl.pallas_call(
                kernel,
                out_shape=outs,
                input_output_aliases=alias or {},
                in_specs=[smem()] * len(scalars) + [vmem()] * len(arrays)
                + [pl.BlockSpec(memory_space=pltpu.HBM)] * len(raw),
                out_specs=[pl.BlockSpec(memory_space=pltpu.HBM) if in_hbm else vmem()] * len(outs),
                scratch_shapes=list(scratch),
                compiler_params=pltpu.CompilerParams(vmem_limit_bytes=mib << 20),
            )(
                *scalars,
                *on_chip(*arrays),
                *[pltpu.with_memory_space_constraint(array, pltpu.HBM) for array in raw],
            )

        return run

    packed_edge = f32(planes, rim, LANES)
    packed_mid = f32(planes, band // 2, LANES)
    row_strip = f32(planes, blocks - 1, rim, LANES)
    turned, odd_edge, even_edge, odd_mid, even_mid, odd, even = call(
        pack_kernel,
        [f32(planes, blocks - 1, tile_r, LANES)]
        + [packed_edge] * 2 + [packed_mid] * 2 + [row_strip] * 2,
        4,
    )(tile)
    edge_strips = exchange(odd_edge, even_edge, "col")
    row_strips = exchange(odd, even, "row")
    mid_strips = exchange(odd_mid, even_mid, "col")
    constants = (tables, amps, probe)
    tables, amps, probe = call(
        load_kernel,
        [pltpu.VMEM(array.shape, array.dtype) for array in constants],
        4,
        scratch=[pltpu.SemaphoreType.DMA(())] * len(constants),
        raw=constants,
    )()
    odd, even = call(corner_kernel, [packed_edge] * 2, 4)(*edge_strips)
    corner_strips = exchange(odd, even, "row")

    field_shape = f32(planes, blocks, tile_r + frame, LANES)
    work = [field_shape] + [pltpu.VMEM((GROUP, 2, frame, frame), jnp.float32)] * 4
    strip, strip_mid = f32(planes, 2, rim, LANES), f32(planes, blocks - 2, rim, LANES)
    edge_rows = f32(planes, 2, 2 * rim, LANES)
    band_rows = f32(planes, band, LANES)
    pieces = [strip] * 2 + [strip_mid] * 2 + [
        edge_rows,
        f32(planes, blocks - 2, 2 * rim, LANES),
        band_rows,
        f32(planes, blocks - 2, band, LANES),
        band_rows,
    ]
    field, *grads = call(
        first_kernel,
        [field_shape] + pieces + [band_rows] * 2,
        20,
        scratch=work,
        scalars=scalars,
    )(turned, *edge_strips, *mid_strips, *row_strips, *corner_strips, amps, probe, tables)

    for iteration in range(1, ITERS):
        odd, even, odd_in, even_in, edges, edges_mid, left, mid, right, band_odd, band_even = grads
        row_strips = exchange(odd, even, "row")
        mid_strips = exchange(band_odd, band_even, "col")
        inner_strips = exchange(odd_in, even_in, "row")
        edges, odd, even = call(
            fold_kernel, [edge_rows] + [f32(planes, 2 * rim, LANES)] * 2, 4
        )(edges, *row_strips)
        edge_strips = exchange(odd, even, "col")
        up_mid, down_mid, odd_in, even_in = call(fold_mid_kernel, [strip_mid] * 4, 4)(
            edges_mid, *inner_strips
        )
        inner_strips = exchange(odd_in, even_in, "row")
        up, down, odd, even = call(total_kernel, [strip] * 4, 4)(edges, *edge_strips)
        row_strips = exchange(odd, even, "row")
        if iteration < ITERS - 1:
            outs = pieces + [band_rows] * 2
        else:
            rest = f32(planes, blocks - 1, rim, LANES)
            outs = [packed_edge] * 2 + [rest] * 2 + [
                f32(planes, 2 * rim, LANES),
                f32(planes, blocks - 1, 2 * rim, LANES),
                *pieces[6:],
                packed_mid,
                packed_mid,
            ]
        field, *grads = call(
            next_kernel, [field_shape] + outs, 20, scratch=work, scalars=scalars
        )(
            field, up, down, up_mid, down_mid, left, mid, right,
            *mid_strips, *row_strips, *inner_strips, amps, probe, tables,
        )

    odd, even, odd_in, even_in, edges, edges_mid, left, mid, right, band_odd, band_even = grads
    row_strips = exchange(odd, even, "row")
    mid_strips = exchange(band_odd, band_even, "col")
    inner_strips = exchange(odd_in, even_in, "row")
    odd, even = call(last_fold_kernel, [packed_edge] * 2, 4)(edges, *row_strips)
    edge_strips = exchange(odd, even, "col")
    whole = pltpu.HBM((planes, tile_r, tile_c), jnp.float32)
    (out,) = call(
        finish_mid_kernel,
        [whole],
        4,
        scratch=[f32(planes, band, tile_c), pltpu.SemaphoreType.DMA(())],
        in_hbm=True,
    )(field, left, mid, right, *mid_strips)
    (out,) = call(
        finish_edge_kernel,
        [whole],
        4,
        scratch=[f32(planes, 2 * rim, tile_c)] + [pltpu.SemaphoreType.DMA(())] * 2,
        raw=[out],
        in_hbm=True,
        alias={6: 0},
    )(field, edges_mid, *inner_strips, *edge_strips)
    return out.reshape(object_slices.shape)


def solution(mesh):
    in_specs = (
        P(None, None, "row", "col"),
        P(),
        P("row", "col", None, None, None),
        P(None, "row", "col", None),
        P("row", "col"),
    )
    out_specs = P(None, None, "row", "col")

    return jax.shard_map(body, mesh=mesh, in_specs=in_specs, out_specs=out_specs, check_vma=False)
```

```python
import math

import jax
import jax.numpy as jnp
import ml_dtypes
import numpy as np
from jax import lax
from jax.experimental import pallas as pl
from jax.experimental.pallas import tpu as pltpu
from jax.sharding import PartitionSpec as P

ITERS = 2
LANES = 128
GROUP = 8

modulus_offset = 0.5
fresnel_scale = 0.9


def split_table(table):
    high = table.astype(np.float32).astype(ml_dtypes.bfloat16)
    low = (table - high.astype(np.float64)).astype(np.float32).astype(ml_dtypes.bfloat16)
    return high, low


def transform_tables(frame_size):
    positions = np.arange(frame_size)
    dft = np.exp(-2j * math.pi * (positions[:, None] * positions[None, :] % frame_size) / frame_size)
    dft = dft / math.sqrt(frame_size)
    frequency = np.where(positions < frame_size // 2, positions, positions - frame_size)
    phase = np.exp(1j * math.pi * fresnel_scale * frequency.astype(np.float64) ** 2 / frame_size)
    hop = (np.conj(dft) * phase[None, :]) @ dft
    half = frame_size // 2
    hop_parts = ((hop[:half, :half] + hop[:half, half:]) / 2, (hop[:half, :half] - hop[:half, half:]) / 2)
    into = (dft[0::2, :half], dft[1::2, :half])
    out_of = (np.conj(dft[:half, 0::2]), np.conj(dft[:half, 1::2]))
    rights, lefts = [], []
    for matrix in (dft, np.conj(dft), hop, np.conj(hop)):
        rights.extend(
            split_table(np.block([[matrix.real, matrix.imag], [-matrix.imag, matrix.real]]))
        )
    for parts in (into, out_of, hop_parts, np.conj(hop_parts)):
        for part in parts:
            lefts.append(
                np.concatenate(
                    split_table(np.block([[part.real, -part.imag], [part.imag, part.real]]))
                )
            )
    return np.stack(rights), np.stack(lefts)


DFT, INVERSE, HOP, HOP_BACK = 0, 1, 2, 3


def exchange(odd_values, even_values, axis):
    count = lax.axis_size(axis)
    received = []
    for values, first in ((odd_values, 1), (even_values, 0)):
        lower = range(first, count - 1, 2)
        pairs = [(i, i + 1) for i in lower] + [(i + 1, i) for i in lower]
        received.append(lax.ppermute(values, axis, pairs))
    return received


def paired(axis, before, after):
    even = lax.rem(lax.axis_index(axis), 2) == 0
    return jnp.where(even, before, after), jnp.where(even, after, before)


def lane_ids(shape):
    return lax.broadcasted_iota(jnp.int32, shape, len(shape) - 1)


def swap_halves(values):
    return pltpu.roll(values, LANES // 2, values.ndim - 1)


def vmem():
    return pl.BlockSpec(memory_space=pltpu.VMEM)


def smem():
    return pl.BlockSpec(memory_space=pltpu.SMEM)


def split(values):
    high = values.astype(jnp.bfloat16)
    return high, (values - high.astype(jnp.float32)).astype(jnp.bfloat16)


def dot(a, b):
    return jnp.dot(a, b, preferred_element_type=jnp.float32)


def blend(first, second):
    return jnp.where(lane_ids(first.shape) < LANES // 2, first, second)


def segments(rows, rim):
    half = rows // 2
    return ((slice(0, rim), slice(rows - rim, rows)), (slice(rim, half), slice(half, rows - rim)))


def pack_kernel(*refs):
    count = (len(refs) - 8) // 3
    sources, outs, targets = refs[: count + 1], refs[count + 1 : count + 8], refs[count + 8 : -count - 2]
    turned_ref, odd_edge, even_edge, odd_mid, even_mid, row_odd, row_even = outs
    object_ref, sems = refs[-count - 2], refs[-count - 1 :]
    copies = [
        pltpu.make_async_copy(source, target, sem)
        for source, target, sem in zip(sources, (object_ref, *targets), sems)
    ]
    for copy in copies:
        copy.start()
    copies[0].wait()
    planes, rows, cols = object_ref.shape
    tiles = cols // LANES
    pieces = segments(rows, odd_edge.shape[1])
    for plane in range(planes):
        for (upper, lower), odd_ref, even_ref in zip(
            pieces, (odd_edge, odd_mid), (even_edge, even_mid)
        ):
            left = blend(
                object_ref[plane, lower, 0:LANES], swap_halves(object_ref[plane, upper, 0:LANES])
            )
            right = blend(
                swap_halves(object_ref[plane, upper, cols - LANES : cols]),
                object_ref[plane, lower, cols - LANES : cols],
            )
            odd_ref[plane], even_ref[plane] = paired("col", left, right)
    for plane in range(planes):
        for tile in range(tiles):
            turned = swap_halves(object_ref[plane, :, tile * LANES : (tile + 1) * LANES])
            turned_ref[plane, tile] = turned
            upper, lower = pieces[0]
            row_odd[plane, tile], row_even[plane, tile] = paired("row", turned[upper], turned[lower])
    for copy in copies[1:]:
        copy.wait()


def lay(turned_ref, plane, rows, left, right, field_ref, row_at):
    tiles = turned_ref.shape[1]
    parts = [left] + [turned_ref[plane, tile, rows, :] for tile in range(tiles)] + [right]
    for block in range(tiles + 1):
        field_ref[plane, block, row_at : row_at + rows.stop - rows.start, :] = blend(
            parts[block], parts[block + 1]
        )


def corner_kernel(from_odd, from_even, odd_ref, even_ref):
    for plane in range(odd_ref.shape[0]):
        left, right = paired("col", from_odd[plane], from_even[plane])
        odd_ref[plane], even_ref[plane] = paired(
            "row", blend(left, right), swap_halves(blend(right, left))
        )


def gradients(pos_ref, count_ref, amps_ref, probe_ref, rights_ref, lefts_ref, field_ref, grad_ref, work):
    frame = probe_ref.shape[-1]
    o0, o1, inc, wave = work
    count = count_ref[0, 0]
    first_row = lax.axis_index("row") * (field_ref.shape[2] - frame)
    first_col = lax.axis_index("col") * ((field_ref.shape[1] - 1) * LANES)
    lanes = lane_ids((frame, LANES))

    grad_ref[...] = jnp.zeros_like(grad_ref)

    half = frame // 2

    def right(source, kind):
        table_high, table_low = rights_ref[2 * kind], rights_ref[2 * kind + 1]
        high, low = split(source)
        return dot(high, table_high) + (dot(low, table_high) + dot(high, table_low))

    def left(re, im, kind):
        upper, lower = (re[:half], im[:half]), (re[half:], im[half:])
        if kind != INVERSE:
            upper, lower = (
                [a + b for a, b in zip(upper, lower)], [a - b for a, b in zip(upper, lower)]
            )
        sides = []
        for side, (side_re, side_im) in enumerate((upper, lower)):
            table = lefts_ref[2 * kind + side]
            high, low = split(jnp.concatenate([side_re, side_im], axis=0))
            out = dot(
                jnp.concatenate([table, table], axis=1), jnp.concatenate([high, low], axis=0)
            )
            out = out[:frame] + out[frame:]
            sides.append((out[:half], out[half:]))
        upper, lower = sides
        if kind != DFT:
            upper, lower = (
                [a + b for a, b in zip(upper, lower)], [a - b for a, b in zip(upper, lower)]
            )
        return [jnp.concatenate([a, b], axis=0) for a, b in zip(upper, lower)]

    def two_sided(zs, kind):
        outs = [
            right(
                jnp.concatenate([jnp.concatenate(z, axis=1) for z in zs[pair : pair + 2]], axis=0),
                kind,
            )
            for pair in range(0, len(zs), 2)
        ]
        mixes = [
            left(
                jnp.concatenate([out[:frame, :frame], out[frame:, :frame]], axis=1),
                jnp.concatenate([out[:frame, frame:], out[frame:, frame:]], axis=1),
                kind,
            )
            for out in outs
        ]
        return [
            (re[:, k * frame : (k + 1) * frame], im[:, k * frame : (k + 1) * frame])
            for re, im in mixes
            for k in range(2)
        ]

    def group_step(group, carry):
        base = group * GROUP
        where = []
        for k in range(GROUP):
            row_at = pos_ref[0, 0, 0, base + k] - first_row
            col_at = pos_ref[1, 0, 0, base + k] - first_col
            block = lax.shift_right_logical(col_at, 7)
            shift = jnp.bitwise_and(col_at, LANES - 1)
            where.append((pl.ds(row_at, frame), block, shift))
            for plane in range(4):
                near = field_ref[plane, block, pl.ds(row_at, frame), :]
                far = field_ref[plane, block + 1, pl.ds(row_at, frame), :]
                joined = jnp.where(lanes >= shift, near, far)
                target = o0 if plane < 2 else o1
                target[k, plane % 2] = pltpu.roll(
                    joined, jnp.bitwise_and(LANES - shift, LANES - 1), 1
                )
        probe_re, probe_im = probe_ref[0], probe_ref[1]
        zs = []
        for k in range(GROUP):
            a, b = o0[k, 0], o0[k, 1]
            zs.append((probe_re * a - probe_im * b, probe_re * b + probe_im * a))
        for k, (re, im) in enumerate(two_sided(zs, HOP)):
            inc[k, 0] = re
            inc[k, 1] = im
        zs = []
        for k in range(GROUP):
            a, b, c, d = inc[k, 0], inc[k, 1], o1[k, 0], o1[k, 1]
            zs.append((a * c - b * d, a * d + b * c))
        for k, (re, im) in enumerate(two_sided(zs, DFT)):
            live = jnp.where(base + k < count, 1.0, 0.0)
            amps = jnp.concatenate(
                [amps_ref[base + k, pl.ds(odd, half, stride=2), :] for odd in range(2)], axis=0
            )
            factor = (1.0 - amps * lax.rsqrt(re * re + im * im + modulus_offset)) * live
            wave[k, 0] = re * factor
            wave[k, 1] = im * factor
        zs = [(wave[k, 0], wave[k, 1]) for k in range(GROUP)]

        def place(k, first_plane, values):
            rows, block, shift = where[k]
            for part in range(2):
                moved = pltpu.roll(values[part], shift, 1)
                near = jnp.where(lanes >= shift, moved, 0.0)
                far = jnp.where(lanes >= shift, 0.0, moved)
                grad_ref[first_plane + part, block, rows, :] += near
                grad_ref[first_plane + part, block + 1, rows, :] += far

        for k, (re, im) in enumerate(two_sided(zs, INVERSE)):
            wave[k, 0] = re
            wave[k, 1] = im
        zs = []
        for k in range(GROUP):
            re, im = wave[k, 0], wave[k, 1]
            a, b, c, d = inc[k, 0], inc[k, 1], o1[k, 0], o1[k, 1]
            place(k, 2, (a * re + b * im, a * im - b * re))
            zs.append((c * re + d * im, c * im - d * re))
        for k, (re, im) in enumerate(two_sided(zs, HOP_BACK)):
            place(k, 0, (probe_re * re + probe_im * im, probe_re * im - probe_im * re))
        return carry

    lax.fori_loop(0, (count + GROUP - 1) // GROUP, group_step, 0)


def outer(blocks):
    return (0, blocks - 1)


def inner(blocks):
    return range(1, blocks - 1)


def write_grad(grad_ref, pieces):
    left, mid, right, band_odd, band_even = pieces[-5:]
    _, blocks, all_rows, _ = grad_ref.shape
    rim = pieces[0].shape[-2]
    rows = all_rows - 2 * rim
    if len(pieces) == 8:
        row_odd, row_even, edges = pieces[:3]
        groups = [(row_odd, row_even, edges, [(0, blocks - 1), (blocks - 1, 0), *inner(blocks)])]
    else:
        row_odd, row_even, row_mid_odd, row_mid_even, edges, edges_mid = pieces[:6]
        groups = [
            (row_odd, row_even, edges, outer(blocks)),
            (row_mid_odd, row_mid_even, edges_mid, inner(blocks)),
        ]

    def rows_of(block, lo):
        if isinstance(block, tuple):
            return blend(*[grad_ref[:, part, lo : lo + rim, :] for part in block])
        return grad_ref[:, block, lo : lo + rim, :]

    for odd, even, edge, group in groups:
        for at, block in enumerate(group):
            odd[:, at], even[:, at] = paired("row", rows_of(block, 0), rows_of(block, rows + rim))
            edge[:, at, 0:rim, :] = rows_of(block, rim)
            edge[:, at, rim : 2 * rim, :] = rows_of(block, rows)
    left[...] = grad_ref[:, 0, 2 * rim : rows, :]
    mid[...] = grad_ref[:, 1 : blocks - 1, 2 * rim : rows, :]
    right[...] = grad_ref[:, blocks - 1, 2 * rim : rows, :]
    if band_odd.shape[1] == rows - 2 * rim:
        band_odd[...], band_even[...] = paired("col", left[...], right[...])
    else:
        half = (rows - 2 * rim) // 2
        upper, lower = slice(2 * rim, 2 * rim + half), slice(2 * rim + half, rows)
        pack_bands(grad_ref, (band_odd, band_even), upper, lower)


def pack_bands(ref, packed, upper, lower):
    last = ref.shape[1] - 1
    for plane in range(ref.shape[0]):
        packed[0][plane], packed[1][plane] = paired(
            "col",
            blend(ref[plane, 0, upper, :], swap_halves(ref[plane, 0, lower, :])),
            blend(swap_halves(ref[plane, last, lower, :]), ref[plane, last, upper, :]),
        )


def first_kernel(
    pos_ref, count_ref, turned_ref, edge_odd, edge_even, mid_odd, mid_even, row_odd, row_even,
    corner_odd, corner_even, amps_ref, probe_ref, rights_ref, lefts_ref, field_ref, *rest,
):
    pieces, (grad_ref, *work) = rest[:-5], rest[-5:]
    planes, _, rows, _ = turned_ref.shape
    rim = edge_odd.shape[1]
    for plane in range(planes):
        for (upper, lower), odd, even in zip(
            segments(rows, rim), (edge_odd, mid_odd), (edge_even, mid_even)
        ):
            left, right = paired("col", odd[plane], even[plane])
            lay(turned_ref, plane, upper, left, right, field_ref, rim + upper.start)
            left, right = swap_halves(left), swap_halves(right)
            lay(turned_ref, plane, lower, left, right, field_ref, rim + lower.start)
        corners = paired("row", corner_odd[plane], corner_even[plane])
        rims = paired("row", row_odd[plane], row_even[plane])
        for strip, corner, row_at in zip(rims, corners, (0, rows + rim)):
            parts = [corner, *strip, corner]
            for block in range(len(parts) - 1):
                field_ref[plane, block, row_at : row_at + rim, :] = blend(
                    parts[block], parts[block + 1]
                )
    gradients(pos_ref, count_ref, amps_ref, probe_ref, rights_ref, lefts_ref, field_ref, grad_ref, work)
    write_grad(grad_ref, pieces)


def fold(edges, row_odd, row_even, plane, at):
    rim = row_odd.shape[2]
    from_up, from_down = paired("row", row_odd[plane, at], row_even[plane, at])
    return edges[plane, at, 0:rim, :] + from_up, edges[plane, at, rim : 2 * rim, :] + from_down


def fold_kernel(edges, row_odd, row_even, folded_ref, odd_ref, even_ref):
    planes, count = edges.shape[:2]
    rim = row_odd.shape[2]
    for plane in range(planes):
        for at in range(count):
            upper, lower = fold(edges, row_odd, row_even, plane, at)
            folded_ref[plane, at, 0:rim, :] = upper
            folded_ref[plane, at, rim : 2 * rim, :] = lower
    odd_ref[...], even_ref[...] = paired("col", folded_ref[:, 0], folded_ref[:, count - 1])


def last_fold_kernel(edges, row_odd, row_even, odd_ref, even_ref):
    for plane in range(edges.shape[0]):
        upper, lower = fold(edges, row_odd, row_even, plane, 0)
        lower = swap_halves(lower)
        odd_ref[plane], even_ref[plane] = paired("col", blend(upper, lower), blend(lower, upper))


def fold_mid_kernel(edges, row_odd, row_even, up_ref, down_ref, odd_ref, even_ref):
    for plane in range(edges.shape[0]):
        for at in range(edges.shape[1]):
            upper, lower = fold(edges, row_odd, row_even, plane, at)
            up_ref[plane, at], down_ref[plane, at] = upper, lower
            odd_ref[plane, at], even_ref[plane, at] = paired("row", upper, lower)


def total_kernel(folded_ref, from_odd, from_even, up_ref, down_ref, odd_ref, even_ref):
    planes, count, rim, _ = up_ref.shape
    for plane in range(planes):
        sides = paired("col", from_odd[plane], from_even[plane])
        for at in range(count):
            values = folded_ref[plane, at] + sides[at]
            upper, lower = values[0:rim], values[rim : 2 * rim]
            up_ref[plane, at], down_ref[plane, at] = upper, lower
            odd_ref[plane, at], even_ref[plane, at] = paired("row", upper, lower)


def next_kernel(
    pos_ref, count_ref, old_ref, up_ref, down_ref, up_mid, down_mid, left_ref, mid_ref, right_ref,
    from_odd, from_even, row_odd, row_even, row_mid_odd, row_mid_even,
    amps_ref, probe_ref, rights_ref, lefts_ref, field_ref, *rest,
):
    pieces, (grad_ref, *work) = rest[:-5], rest[-5:]
    _, blocks, all_rows, _ = old_ref.shape
    rim = up_ref.shape[2]
    rows = all_rows - 2 * rim
    from_left, from_right = paired("col", from_odd[...], from_even[...])
    for block in range(blocks):
        lane = lane_ids((1, 1, LANES))
        inside = lane >= 0
        if block in inner(blocks):
            at, odd, even, up, down = block - 1, row_mid_odd, row_mid_even, up_mid, down_mid
            middle = mid_ref[:, at]
        elif block == 0:
            at, odd, even, up, down = 0, row_odd, row_even, up_ref, down_ref
            inside = lane >= jnp.where(lax.axis_index("col") == 0, LANES // 2, 0)
            middle = left_ref[...] + from_left
        else:
            at, odd, even, up, down = 1, row_odd, row_even, up_ref, down_ref
            at_end = lax.axis_index("col") == lax.axis_size("col") - 1
            inside = lane < jnp.where(at_end, LANES // 2, LANES)
            middle = right_ref[...] + from_right
        from_up, from_down = paired("row", odd[:, at], even[:, at])
        for lo, hi, values in (
            (0, rim, from_up),
            (rim, 2 * rim, up[:, at]),
            (2 * rim, rows, middle),
            (rows, rows + rim, down[:, at]),
            (rows + rim, all_rows, from_down),
        ):
            updated = old_ref[:, block, lo:hi, :] - values
            field_ref[:, block, lo:hi, :] = jnp.where(inside, updated, 0.0)
    gradients(pos_ref, count_ref, amps_ref, probe_ref, rights_ref, lefts_ref, field_ref, grad_ref, work)
    write_grad(grad_ref, pieces)


def put_rows(field_ref, plane, row_at, values, sides, part, target_ref, put_at):
    size = values[0].shape[0]
    if part == 1:
        sides = [swap_halves(side) for side in sides]
    values = [values[0] + sides[0], *values[1:-1], values[-1] + sides[1]]
    turned = [
        swap_halves(field_ref[plane, block, row_at : row_at + size, :] - block_values)
        for block, block_values in enumerate(values)
    ]
    for block in range(len(turned) - 1):
        target_ref[plane, put_at : put_at + size, block * LANES : (block + 1) * LANES] = blend(
            turned[block], turned[block + 1]
        )


def finish_mid_kernel(
    field_ref, left_ref, mid_ref, right_ref, from_odd, from_even, out_hbm, result, sem
):
    planes, blocks, all_rows, _ = field_ref.shape
    band = result.shape[1]
    rim = (all_rows - band) // 4
    half = band // 2
    for plane in range(planes):
        sides = paired("col", from_odd[plane], from_even[plane])
        for part in range(2):
            at = slice(part * half, (part + 1) * half)
            values = [left_ref[plane, at, :], right_ref[plane, at, :]]
            values[1:1] = [mid_ref[plane, k, at, :] for k in range(blocks - 2)]
            put_rows(
                field_ref, plane, 2 * rim + part * half, values, sides, part, result, part * half
            )
    copy = pltpu.make_async_copy(result, out_hbm.at[:, rim : rim + band, :], sem)
    copy.start()
    copy.wait()


def finish_edge_kernel(
    field_ref, edges, row_odd, row_even, from_odd, from_even, _, out_hbm, result, *sems
):
    planes, blocks, all_rows, _ = field_ref.shape
    rim = from_odd.shape[1]
    rows = all_rows - 2 * rim
    copies = []
    for part in range(2):
        for plane in range(planes):
            sides = paired("col", from_odd[plane], from_even[plane])
            folded = [fold(edges, row_odd, row_even, plane, k)[part] for k in range(1, blocks)]
            values = [*folded, folded[0]]
            put_rows(
                field_ref, plane, rim + part * (rows - rim), values, sides, part, result, part * rim
            )
        at = part * (rows - rim)
        copies.append(
            pltpu.make_async_copy(
                result.at[:, part * rim : (part + 1) * rim, :],
                out_hbm.at[:, at : at + rim, :],
                sems[part],
            )
        )
        copies[-1].start()
    for copy in copies:
        copy.wait()


def f32(*shape):
    return pltpu.VMEM(shape, jnp.float32)


def on_chip(*arrays):
    return [pltpu.with_memory_space_constraint(array, pltpu.VMEM) for array in arrays]


def body(object_slices, probe, amplitudes, scan_pos, scan_count):
    layers, _, tile_r, tile_c = object_slices.shape
    planes = layers * 2
    frame = probe.shape[-1]
    rim = frame // 2
    blocks = tile_c // LANES + 1
    slots = amplitudes.shape[2]
    assert slots % GROUP == 0
    amps = amplitudes[0, 0]
    scalars = [scan_pos, scan_count]
    tables = [jnp.asarray(table) for table in transform_tables(frame)]
    tile = object_slices.reshape(planes, tile_r, tile_c)

    band = tile_r - 2 * rim

    def call(kernel, outs, mib, scratch=(), scalars=(), raw=(), in_hbm=False, alias=None):
        def run(*arrays):
            return pl.pallas_call(
                kernel,
                out_shape=outs,
                input_output_aliases=alias or {},
                in_specs=[smem()] * len(scalars) + [vmem()] * len(arrays)
                + [pl.BlockSpec(memory_space=pltpu.HBM)] * len(raw),
                out_specs=[pl.BlockSpec(memory_space=pltpu.HBM) if in_hbm else vmem()] * len(outs),
                scratch_shapes=list(scratch),
                compiler_params=pltpu.CompilerParams(vmem_limit_bytes=mib << 20),
            )(
                *scalars,
                *on_chip(*arrays),
                *[pltpu.with_memory_space_constraint(array, pltpu.HBM) for array in raw],
            )

        return run

    packed_edge = f32(planes, rim, LANES)
    packed_mid = f32(planes, band // 2, LANES)
    row_strip = f32(planes, blocks - 1, rim, LANES)
    constants = (amps, probe, *tables)
    turned, odd_edge, even_edge, odd_mid, even_mid, odd, even, amps, probe, *tables = call(
        pack_kernel,
        [f32(planes, blocks - 1, tile_r, LANES)]
        + [packed_edge] * 2 + [packed_mid] * 2 + [row_strip] * 2
        + [pltpu.VMEM(array.shape, array.dtype) for array in constants],
        8,
        scratch=[f32(planes, tile_r, tile_c)]
        + [pltpu.SemaphoreType.DMA(())] * (len(constants) + 1),
        raw=[tile, *constants],
    )()
    edge_strips = exchange(odd_edge, even_edge, "col")
    row_strips = exchange(odd, even, "row")
    mid_strips = exchange(odd_mid, even_mid, "col")
    odd, even = call(corner_kernel, [packed_edge] * 2, 4)(*edge_strips)
    corner_strips = exchange(odd, even, "row")

    field_shape = f32(planes, blocks, tile_r + frame, LANES)
    work = [field_shape] + [pltpu.VMEM((GROUP, 2, frame, frame), jnp.float32)] * 4
    strip, strip_mid = f32(planes, 2, rim, LANES), f32(planes, blocks - 2, rim, LANES)
    edge_rows = f32(planes, 2, 2 * rim, LANES)
    band_rows = f32(planes, band, LANES)
    pieces = [strip] * 2 + [strip_mid] * 2 + [
        edge_rows,
        f32(planes, blocks - 2, 2 * rim, LANES),
        band_rows,
        f32(planes, blocks - 2, band, LANES),
        band_rows,
    ]
    field, *grads = call(
        first_kernel,
        [field_shape] + pieces + [band_rows] * 2,
        20,
        scratch=work,
        scalars=scalars,
    )(turned, *edge_strips, *mid_strips, *row_strips, *corner_strips, amps, probe, *tables)

    for iteration in range(1, ITERS):
        odd, even, odd_in, even_in, edges, edges_mid, left, mid, right, band_odd, band_even = grads
        row_strips = exchange(odd, even, "row")
        mid_strips = exchange(band_odd, band_even, "col")
        inner_strips = exchange(odd_in, even_in, "row")
        edges, odd, even = call(
            fold_kernel, [edge_rows] + [f32(planes, 2 * rim, LANES)] * 2, 4
        )(edges, *row_strips)
        edge_strips = exchange(odd, even, "col")
        up_mid, down_mid, odd_in, even_in = call(fold_mid_kernel, [strip_mid] * 4, 4)(
            edges_mid, *inner_strips
        )
        inner_strips = exchange(odd_in, even_in, "row")
        up, down, odd, even = call(total_kernel, [strip] * 4, 4)(edges, *edge_strips)
        row_strips = exchange(odd, even, "row")
        if iteration < ITERS - 1:
            outs = pieces + [band_rows] * 2
        else:
            outs = [f32(planes, blocks, rim, LANES)] * 2 + [
                f32(planes, blocks, 2 * rim, LANES),
                *pieces[6:],
                packed_mid,
                packed_mid,
            ]
        field, *grads = call(
            next_kernel, [field_shape] + outs, 20, scratch=work, scalars=scalars
        )(
            field, up, down, up_mid, down_mid, left, mid, right,
            *mid_strips, *row_strips, *inner_strips, amps, probe, *tables,
        )

    odd, even, edges, left, mid, right, band_odd, band_even = grads
    row_strips = exchange(odd, even, "row")
    mid_strips = exchange(band_odd, band_even, "col")
    odd, even = call(last_fold_kernel, [packed_edge] * 2, 4)(edges, *row_strips)
    edge_strips = exchange(odd, even, "col")
    whole = pltpu.HBM((planes, tile_r, tile_c), jnp.float32)
    (out,) = call(
        finish_mid_kernel,
        [whole],
        4,
        scratch=[f32(planes, band, tile_c), pltpu.SemaphoreType.DMA(())],
        in_hbm=True,
    )(field, left, mid, right, *mid_strips)
    (out,) = call(
        finish_edge_kernel,
        [whole],
        4,
        scratch=[f32(planes, 2 * rim, tile_c)] + [pltpu.SemaphoreType.DMA(())] * 2,
        raw=[out],
        in_hbm=True,
        alias={6: 0},
    )(field, edges, *row_strips, *edge_strips)
    return out.reshape(object_slices.shape)


def solution(mesh):
    in_specs = (
        P(None, None, "row", "col"),
        P(),
        P("row", "col", None, None, None),
        P(None, "row", "col", None),
        P("row", "col"),
    )
    out_specs = P(None, None, "row", "col")

    return jax.shard_map(body, mesh=mesh, in_specs=in_specs, out_specs=out_specs, check_vma=False)
```

```python
import math

import jax
import jax.numpy as jnp
import ml_dtypes
import numpy as np
from jax import lax
from jax.experimental import pallas as pl
from jax.experimental.pallas import tpu as pltpu
from jax.sharding import PartitionSpec as P

ITERS = 2
LANES = 128
GROUP = 8
BATCH = 4

modulus_offset = 0.5
fresnel_scale = 0.9


def split_table(table):
    high = table.astype(np.float32).astype(ml_dtypes.bfloat16)
    low = (table - high.astype(np.float64)).astype(np.float32).astype(ml_dtypes.bfloat16)
    return high, low


def transform_tables(frame_size):
    positions = np.arange(frame_size)
    dft = np.exp(-2j * math.pi * (positions[:, None] * positions[None, :] % frame_size) / frame_size)
    dft = dft / math.sqrt(frame_size)
    frequency = np.where(positions < frame_size // 2, positions, positions - frame_size)
    phase = np.exp(1j * math.pi * fresnel_scale * frequency.astype(np.float64) ** 2 / frame_size)
    hop = (np.conj(dft) * phase[None, :]) @ dft
    half = frame_size // 2
    hop_parts = ((hop[:half, :half] + hop[:half, half:]) / 2, (hop[:half, :half] - hop[:half, half:]) / 2)
    into = (dft[0::2, :half], dft[1::2, :half])
    out_of = (np.conj(dft[:half, 0::2]), np.conj(dft[:half, 1::2]))
    rights, lefts = [], []
    for matrix in (dft, np.conj(dft), hop, np.conj(hop)):
        rights.extend(
            split_table(np.block([[matrix.real, matrix.imag], [-matrix.imag, matrix.real]]))
        )
    for parts in (into, out_of, hop_parts, np.conj(hop_parts)):
        for part in parts:
            lefts.append(
                np.concatenate(
                    split_table(np.block([[part.real, -part.imag], [part.imag, part.real]]))
                )
            )
    return np.stack(rights), np.stack(lefts)


DFT, INVERSE, HOP, HOP_BACK = 0, 1, 2, 3


def exchange(odd_values, even_values, axis):
    count = lax.axis_size(axis)
    received = []
    for values, first in ((odd_values, 1), (even_values, 0)):
        lower = range(first, count - 1, 2)
        pairs = [(i, i + 1) for i in lower] + [(i + 1, i) for i in lower]
        received.append(lax.ppermute(values, axis, pairs))
    return received


def paired(axis, before, after):
    even = lax.rem(lax.axis_index(axis), 2) == 0
    return jnp.where(even, before, after), jnp.where(even, after, before)


def lane_ids(shape):
    return lax.broadcasted_iota(jnp.int32, shape, len(shape) - 1)


def swap_halves(values):
    return pltpu.roll(values, LANES // 2, values.ndim - 1)


def vmem():
    return pl.BlockSpec(memory_space=pltpu.VMEM)


def smem():
    return pl.BlockSpec(memory_space=pltpu.SMEM)


def split(values):
    high = values.astype(jnp.bfloat16)
    return high, (values - high.astype(jnp.float32)).astype(jnp.bfloat16)


def dot(a, b):
    return jnp.dot(a, b, preferred_element_type=jnp.float32)


def blend(first, second):
    return jnp.where(lane_ids(first.shape) < LANES // 2, first, second)


def segments(rows, rim):
    half = rows // 2
    return ((slice(0, rim), slice(rows - rim, rows)), (slice(rim, half), slice(half, rows - rim)))


def pack_kernel(*refs):
    count = (len(refs) - 8) // 3
    sources, outs, targets = refs[: count + 1], refs[count + 1 : count + 8], refs[count + 8 : -count - 2]
    turned_ref, odd_edge, even_edge, odd_mid, even_mid, row_odd, row_even = outs
    object_ref, sems = refs[-count - 2], refs[-count - 1 :]
    copies = [
        pltpu.make_async_copy(source, target, sem)
        for source, target, sem in zip(sources, (object_ref, *targets), sems)
    ]
    for copy in copies:
        copy.start()
    copies[0].wait()
    planes, rows, cols = object_ref.shape
    tiles = cols // LANES
    pieces = segments(rows, odd_edge.shape[1])
    for plane in range(planes):
        for (upper, lower), odd_ref, even_ref in zip(
            pieces, (odd_edge, odd_mid), (even_edge, even_mid)
        ):
            left = blend(
                object_ref[plane, lower, 0:LANES], swap_halves(object_ref[plane, upper, 0:LANES])
            )
            right = blend(
                swap_halves(object_ref[plane, upper, cols - LANES : cols]),
                object_ref[plane, lower, cols - LANES : cols],
            )
            odd_ref[plane], even_ref[plane] = paired("col", left, right)
    for plane in range(planes):
        for tile in range(tiles):
            turned = swap_halves(object_ref[plane, :, tile * LANES : (tile + 1) * LANES])
            turned_ref[plane, tile] = turned
            upper, lower = pieces[0]
            row_odd[plane, tile], row_even[plane, tile] = paired("row", turned[upper], turned[lower])
    for copy in copies[1:]:
        copy.wait()


def lay(turned_ref, plane, rows, left, right, field_ref, row_at):
    tiles = turned_ref.shape[1]
    parts = [left] + [turned_ref[plane, tile, rows, :] for tile in range(tiles)] + [right]
    for block in range(tiles + 1):
        field_ref[plane, block, row_at : row_at + rows.stop - rows.start, :] = blend(
            parts[block], parts[block + 1]
        )


def corner_kernel(from_odd, from_even, odd_ref, even_ref):
    for plane in range(odd_ref.shape[0]):
        left, right = paired("col", from_odd[plane], from_even[plane])
        odd_ref[plane], even_ref[plane] = paired(
            "row", blend(left, right), swap_halves(blend(right, left))
        )


def gradients(pos_ref, count_ref, amps_ref, probe_ref, rights_ref, lefts_ref, field_ref, grad_ref, work):
    frame = probe_ref.shape[-1]
    o0, o1, inc, wave = work
    count = count_ref[0, 0]
    first_row = lax.axis_index("row") * (field_ref.shape[2] - frame)
    first_col = lax.axis_index("col") * ((field_ref.shape[1] - 1) * LANES)
    lanes = lane_ids((frame, LANES))

    grad_ref[...] = jnp.zeros_like(grad_ref)

    half = frame // 2

    def right(source, kind):
        table_high, table_low = rights_ref[2 * kind], rights_ref[2 * kind + 1]
        high, low = split(source)
        out = dot(jnp.concatenate([high, low], axis=0), table_high)
        return out[: high.shape[0]] + out[high.shape[0] :] + dot(high, table_low)

    def left(re, im, kind):
        upper, lower = (re[:half], im[:half]), (re[half:], im[half:])
        if kind != INVERSE:
            upper, lower = (
                [a + b for a, b in zip(upper, lower)], [a - b for a, b in zip(upper, lower)]
            )
        sides = []
        for side, (side_re, side_im) in enumerate((upper, lower)):
            table = lefts_ref[2 * kind + side]
            high, low = split(jnp.concatenate([side_re, side_im], axis=0))
            out = dot(
                jnp.concatenate([table, table], axis=1), jnp.concatenate([high, low], axis=0)
            )
            out = out[:frame] + out[frame:]
            sides.append((out[:half], out[half:]))
        upper, lower = sides
        if kind != DFT:
            upper, lower = (
                [a + b for a, b in zip(upper, lower)], [a - b for a, b in zip(upper, lower)]
            )
        return [jnp.concatenate([a, b], axis=0) for a, b in zip(upper, lower)]

    def two_sided(zs, kind):
        outs = []
        for first in range(0, len(zs), BATCH):
            rows = [jnp.concatenate(z, axis=1) for z in zs[first : first + BATCH]]
            out = right(jnp.concatenate(rows, axis=0), kind)
            outs.extend(out[at : at + 2 * frame] for at in range(0, BATCH * frame, 2 * frame))
        mixes = [
            left(
                jnp.concatenate([out[:frame, :frame], out[frame:, :frame]], axis=1),
                jnp.concatenate([out[:frame, frame:], out[frame:, frame:]], axis=1),
                kind,
            )
            for out in outs
        ]
        return [
            (re[:, k * frame : (k + 1) * frame], im[:, k * frame : (k + 1) * frame])
            for re, im in mixes
            for k in range(2)
        ]

    def group_step(group, carry):
        base = group * GROUP
        where = []
        for k in range(GROUP):
            row_at = pos_ref[0, 0, 0, base + k] - first_row
            col_at = pos_ref[1, 0, 0, base + k] - first_col
            block = lax.shift_right_logical(col_at, 7)
            shift = jnp.bitwise_and(col_at, LANES - 1)
            where.append((pl.ds(row_at, frame), block, shift))
            for plane in range(4):
                near = field_ref[plane, block, pl.ds(row_at, frame), :]
                far = field_ref[plane, block + 1, pl.ds(row_at, frame), :]
                joined = jnp.where(lanes >= shift, near, far)
                target = o0 if plane < 2 else o1
                target[k, plane % 2] = pltpu.roll(
                    joined, jnp.bitwise_and(LANES - shift, LANES - 1), 1
                )
        probe_re, probe_im = probe_ref[0], probe_ref[1]
        zs = []
        for k in range(GROUP):
            a, b = o0[k, 0], o0[k, 1]
            zs.append((probe_re * a - probe_im * b, probe_re * b + probe_im * a))
        for k, (re, im) in enumerate(two_sided(zs, HOP)):
            inc[k, 0] = re
            inc[k, 1] = im
        zs = []
        for k in range(GROUP):
            a, b, c, d = inc[k, 0], inc[k, 1], o1[k, 0], o1[k, 1]
            zs.append((a * c - b * d, a * d + b * c))
        for k, (re, im) in enumerate(two_sided(zs, DFT)):
            live = jnp.where(base + k < count, 1.0, 0.0)
            amps = jnp.concatenate(
                [amps_ref[base + k, pl.ds(odd, half, stride=2), :] for odd in range(2)], axis=0
            )
            factor = (1.0 - amps * lax.rsqrt(re * re + im * im + modulus_offset)) * live
            wave[k, 0] = re * factor
            wave[k, 1] = im * factor
        zs = [(wave[k, 0], wave[k, 1]) for k in range(GROUP)]

        def place(k, first_plane, values):
            rows, block, shift = where[k]
            for part in range(2):
                moved = pltpu.roll(values[part], shift, 1)
                near = jnp.where(lanes >= shift, moved, 0.0)
                far = jnp.where(lanes >= shift, 0.0, moved)
                grad_ref[first_plane + part, block, rows, :] += near
                grad_ref[first_plane + part, block + 1, rows, :] += far

        for k, (re, im) in enumerate(two_sided(zs, INVERSE)):
            wave[k, 0] = re
            wave[k, 1] = im
        zs = []
        for k in range(GROUP):
            re, im = wave[k, 0], wave[k, 1]
            a, b, c, d = inc[k, 0], inc[k, 1], o1[k, 0], o1[k, 1]
            place(k, 2, (a * re + b * im, a * im - b * re))
            zs.append((c * re + d * im, c * im - d * re))
        for k, (re, im) in enumerate(two_sided(zs, HOP_BACK)):
            place(k, 0, (probe_re * re + probe_im * im, probe_re * im - probe_im * re))
        return carry

    lax.fori_loop(0, (count + GROUP - 1) // GROUP, group_step, 0)


def outer(blocks):
    return (0, blocks - 1)


def inner(blocks):
    return range(1, blocks - 1)


def write_grad(grad_ref, pieces):
    left, mid, right, band_odd, band_even = pieces[-5:]
    _, blocks, all_rows, _ = grad_ref.shape
    rim = pieces[0].shape[-2]
    rows = all_rows - 2 * rim
    if len(pieces) == 8:
        row_odd, row_even, edges = pieces[:3]
        groups = [(row_odd, row_even, edges, [(0, blocks - 1), (blocks - 1, 0), *inner(blocks)])]
    else:
        row_odd, row_even, row_mid_odd, row_mid_even, edges, edges_mid = pieces[:6]
        groups = [
            (row_odd, row_even, edges, outer(blocks)),
            (row_mid_odd, row_mid_even, edges_mid, inner(blocks)),
        ]

    def rows_of(block, lo):
        if isinstance(block, tuple):
            return blend(*[grad_ref[:, part, lo : lo + rim, :] for part in block])
        return grad_ref[:, block, lo : lo + rim, :]

    for odd, even, edge, group in groups:
        for at, block in enumerate(group):
            odd[:, at], even[:, at] = paired("row", rows_of(block, 0), rows_of(block, rows + rim))
            edge[:, at, 0:rim, :] = rows_of(block, rim)
            edge[:, at, rim : 2 * rim, :] = rows_of(block, rows)
    left[...] = grad_ref[:, 0, 2 * rim : rows, :]
    mid[...] = grad_ref[:, 1 : blocks - 1, 2 * rim : rows, :]
    right[...] = grad_ref[:, blocks - 1, 2 * rim : rows, :]
    if band_odd.shape[1] == rows - 2 * rim:
        band_odd[...], band_even[...] = paired("col", left[...], right[...])
    else:
        half = (rows - 2 * rim) // 2
        upper, lower = slice(2 * rim, 2 * rim + half), slice(2 * rim + half, rows)
        pack_bands(grad_ref, (band_odd, band_even), upper, lower)


def pack_bands(ref, packed, upper, lower):
    last = ref.shape[1] - 1
    for plane in range(ref.shape[0]):
        packed[0][plane], packed[1][plane] = paired(
            "col",
            blend(ref[plane, 0, upper, :], swap_halves(ref[plane, 0, lower, :])),
            blend(swap_halves(ref[plane, last, lower, :]), ref[plane, last, upper, :]),
        )


def first_kernel(
    pos_ref, count_ref, turned_ref, edge_odd, edge_even, mid_odd, mid_even, row_odd, row_even,
    corner_odd, corner_even, amps_ref, probe_ref, rights_ref, lefts_ref, field_ref, *rest,
):
    pieces, (grad_ref, *work) = rest[:-5], rest[-5:]
    planes, _, rows, _ = turned_ref.shape
    rim = edge_odd.shape[1]
    for plane in range(planes):
        for (upper, lower), odd, even in zip(
            segments(rows, rim), (edge_odd, mid_odd), (edge_even, mid_even)
        ):
            left, right = paired("col", odd[plane], even[plane])
            lay(turned_ref, plane, upper, left, right, field_ref, rim + upper.start)
            left, right = swap_halves(left), swap_halves(right)
            lay(turned_ref, plane, lower, left, right, field_ref, rim + lower.start)
        corners = paired("row", corner_odd[plane], corner_even[plane])
        rims = paired("row", row_odd[plane], row_even[plane])
        for strip, corner, row_at in zip(rims, corners, (0, rows + rim)):
            parts = [corner, *strip, corner]
            for block in range(len(parts) - 1):
                field_ref[plane, block, row_at : row_at + rim, :] = blend(
                    parts[block], parts[block + 1]
                )
    gradients(pos_ref, count_ref, amps_ref, probe_ref, rights_ref, lefts_ref, field_ref, grad_ref, work)
    write_grad(grad_ref, pieces)


def fold(edges, row_odd, row_even, plane, at):
    rim = row_odd.shape[2]
    from_up, from_down = paired("row", row_odd[plane, at], row_even[plane, at])
    return edges[plane, at, 0:rim, :] + from_up, edges[plane, at, rim : 2 * rim, :] + from_down


def fold_kernel(edges, row_odd, row_even, folded_ref, odd_ref, even_ref):
    planes, count = edges.shape[:2]
    rim = row_odd.shape[2]
    for plane in range(planes):
        for at in range(count):
            upper, lower = fold(edges, row_odd, row_even, plane, at)
            folded_ref[plane, at, 0:rim, :] = upper
            folded_ref[plane, at, rim : 2 * rim, :] = lower
    odd_ref[...], even_ref[...] = paired("col", folded_ref[:, 0], folded_ref[:, count - 1])


def last_fold_kernel(edges, row_odd, row_even, odd_ref, even_ref):
    for plane in range(edges.shape[0]):
        upper, lower = fold(edges, row_odd, row_even, plane, 0)
        lower = swap_halves(lower)
        odd_ref[plane], even_ref[plane] = paired("col", blend(upper, lower), blend(lower, upper))


def fold_mid_kernel(edges, row_odd, row_even, up_ref, down_ref, odd_ref, even_ref):
    for plane in range(edges.shape[0]):
        for at in range(edges.shape[1]):
            upper, lower = fold(edges, row_odd, row_even, plane, at)
            up_ref[plane, at], down_ref[plane, at] = upper, lower
            odd_ref[plane, at], even_ref[plane, at] = paired("row", upper, lower)


def total_kernel(folded_ref, from_odd, from_even, up_ref, down_ref, odd_ref, even_ref):
    planes, count, rim, _ = up_ref.shape
    for plane in range(planes):
        sides = paired("col", from_odd[plane], from_even[plane])
        for at in range(count):
            values = folded_ref[plane, at] + sides[at]
            upper, lower = values[0:rim], values[rim : 2 * rim]
            up_ref[plane, at], down_ref[plane, at] = upper, lower
            odd_ref[plane, at], even_ref[plane, at] = paired("row", upper, lower)


def next_kernel(
    pos_ref, count_ref, old_ref, up_ref, down_ref, up_mid, down_mid, left_ref, mid_ref, right_ref,
    from_odd, from_even, row_odd, row_even, row_mid_odd, row_mid_even,
    amps_ref, probe_ref, rights_ref, lefts_ref, field_ref, *rest,
):
    pieces, (grad_ref, *work) = rest[:-5], rest[-5:]
    _, blocks, all_rows, _ = old_ref.shape
    rim = up_ref.shape[2]
    rows = all_rows - 2 * rim
    from_left, from_right = paired("col", from_odd[...], from_even[...])
    for block in range(blocks):
        lane = lane_ids((1, 1, LANES))
        inside = lane >= 0
        if block in inner(blocks):
            at, odd, even, up, down = block - 1, row_mid_odd, row_mid_even, up_mid, down_mid
            middle = mid_ref[:, at]
        elif block == 0:
            at, odd, even, up, down = 0, row_odd, row_even, up_ref, down_ref
            inside = lane >= jnp.where(lax.axis_index("col") == 0, LANES // 2, 0)
            middle = left_ref[...] + from_left
        else:
            at, odd, even, up, down = 1, row_odd, row_even, up_ref, down_ref
            at_end = lax.axis_index("col") == lax.axis_size("col") - 1
            inside = lane < jnp.where(at_end, LANES // 2, LANES)
            middle = right_ref[...] + from_right
        from_up, from_down = paired("row", odd[:, at], even[:, at])
        for lo, hi, values in (
            (0, rim, from_up),
            (rim, 2 * rim, up[:, at]),
            (2 * rim, rows, middle),
            (rows, rows + rim, down[:, at]),
            (rows + rim, all_rows, from_down),
        ):
            updated = old_ref[:, block, lo:hi, :] - values
            field_ref[:, block, lo:hi, :] = jnp.where(inside, updated, 0.0)
    gradients(pos_ref, count_ref, amps_ref, probe_ref, rights_ref, lefts_ref, field_ref, grad_ref, work)
    write_grad(grad_ref, pieces)


def put_rows(field_ref, plane, row_at, values, sides, part, target_ref, put_at):
    size = values[0].shape[0]
    if part == 1:
        sides = [swap_halves(side) for side in sides]
    values = [values[0] + sides[0], *values[1:-1], values[-1] + sides[1]]
    turned = [
        swap_halves(field_ref[plane, block, row_at : row_at + size, :] - block_values)
        for block, block_values in enumerate(values)
    ]
    for block in range(len(turned) - 1):
        target_ref[plane, put_at : put_at + size, block * LANES : (block + 1) * LANES] = blend(
            turned[block], turned[block + 1]
        )


def finish_mid_kernel(
    field_ref, left_ref, mid_ref, right_ref, from_odd, from_even, out_hbm, result, sem
):
    planes, blocks, all_rows, _ = field_ref.shape
    band = result.shape[1]
    rim = (all_rows - band) // 4
    half = band // 2
    for plane in range(planes):
        sides = paired("col", from_odd[plane], from_even[plane])
        for part in range(2):
            at = slice(part * half, (part + 1) * half)
            values = [left_ref[plane, at, :], right_ref[plane, at, :]]
            values[1:1] = [mid_ref[plane, k, at, :] for k in range(blocks - 2)]
            put_rows(
                field_ref, plane, 2 * rim + part * half, values, sides, part, result, part * half
            )
    copy = pltpu.make_async_copy(result, out_hbm.at[:, rim : rim + band, :], sem)
    copy.start()
    copy.wait()


def finish_edge_kernel(
    field_ref, edges, row_odd, row_even, from_odd, from_even, _, out_hbm, result, *sems
):
    planes, blocks, all_rows, _ = field_ref.shape
    rim = from_odd.shape[1]
    rows = all_rows - 2 * rim
    copies = []
    for part in range(2):
        for plane in range(planes):
            sides = paired("col", from_odd[plane], from_even[plane])
            folded = [fold(edges, row_odd, row_even, plane, k)[part] for k in range(1, blocks)]
            values = [*folded, folded[0]]
            put_rows(
                field_ref, plane, rim + part * (rows - rim), values, sides, part, result, part * rim
            )
        at = part * (rows - rim)
        copies.append(
            pltpu.make_async_copy(
                result.at[:, part * rim : (part + 1) * rim, :],
                out_hbm.at[:, at : at + rim, :],
                sems[part],
            )
        )
        copies[-1].start()
    for copy in copies:
        copy.wait()


def f32(*shape):
    return pltpu.VMEM(shape, jnp.float32)


def on_chip(*arrays):
    return [pltpu.with_memory_space_constraint(array, pltpu.VMEM) for array in arrays]


def body(object_slices, probe, amplitudes, scan_pos, scan_count):
    layers, _, tile_r, tile_c = object_slices.shape
    planes = layers * 2
    frame = probe.shape[-1]
    rim = frame // 2
    blocks = tile_c // LANES + 1
    slots = amplitudes.shape[2]
    assert slots % GROUP == 0
    amps = amplitudes[0, 0]
    scalars = [scan_pos, scan_count]
    tables = [jnp.asarray(table) for table in transform_tables(frame)]
    tile = object_slices.reshape(planes, tile_r, tile_c)

    band = tile_r - 2 * rim

    def call(kernel, outs, mib, scratch=(), scalars=(), raw=(), in_hbm=False, alias=None):
        def run(*arrays):
            return pl.pallas_call(
                kernel,
                out_shape=outs,
                input_output_aliases=alias or {},
                in_specs=[smem()] * len(scalars) + [vmem()] * len(arrays)
                + [pl.BlockSpec(memory_space=pltpu.HBM)] * len(raw),
                out_specs=[pl.BlockSpec(memory_space=pltpu.HBM) if in_hbm else vmem()] * len(outs),
                scratch_shapes=list(scratch),
                compiler_params=pltpu.CompilerParams(vmem_limit_bytes=mib << 20),
            )(
                *scalars,
                *on_chip(*arrays),
                *[pltpu.with_memory_space_constraint(array, pltpu.HBM) for array in raw],
            )

        return run

    packed_edge = f32(planes, rim, LANES)
    packed_mid = f32(planes, band // 2, LANES)
    row_strip = f32(planes, blocks - 1, rim, LANES)
    constants = (amps, probe, *tables)
    turned, odd_edge, even_edge, odd_mid, even_mid, odd, even, amps, probe, *tables = call(
        pack_kernel,
        [f32(planes, blocks - 1, tile_r, LANES)]
        + [packed_edge] * 2 + [packed_mid] * 2 + [row_strip] * 2
        + [pltpu.VMEM(array.shape, array.dtype) for array in constants],
        8,
        scratch=[f32(planes, tile_r, tile_c)]
        + [pltpu.SemaphoreType.DMA(())] * (len(constants) + 1),
        raw=[tile, *constants],
    )()
    edge_strips = exchange(odd_edge, even_edge, "col")
    row_strips = exchange(odd, even, "row")
    mid_strips = exchange(odd_mid, even_mid, "col")
    odd, even = call(corner_kernel, [packed_edge] * 2, 4)(*edge_strips)
    corner_strips = exchange(odd, even, "row")

    field_shape = f32(planes, blocks, tile_r + frame, LANES)
    work = [field_shape] + [pltpu.VMEM((GROUP, 2, frame, frame), jnp.float32)] * 4
    strip, strip_mid = f32(planes, 2, rim, LANES), f32(planes, blocks - 2, rim, LANES)
    edge_rows = f32(planes, 2, 2 * rim, LANES)
    band_rows = f32(planes, band, LANES)
    pieces = [strip] * 2 + [strip_mid] * 2 + [
        edge_rows,
        f32(planes, blocks - 2, 2 * rim, LANES),
        band_rows,
        f32(planes, blocks - 2, band, LANES),
        band_rows,
    ]
    field, *grads = call(
        first_kernel,
        [field_shape] + pieces + [band_rows] * 2,
        20,
        scratch=work,
        scalars=scalars,
    )(turned, *edge_strips, *mid_strips, *row_strips, *corner_strips, amps, probe, *tables)

    for iteration in range(1, ITERS):
        odd, even, odd_in, even_in, edges, edges_mid, left, mid, right, band_odd, band_even = grads
        row_strips = exchange(odd, even, "row")
        mid_strips = exchange(band_odd, band_even, "col")
        inner_strips = exchange(odd_in, even_in, "row")
        edges, odd, even = call(
            fold_kernel, [edge_rows] + [f32(planes, 2 * rim, LANES)] * 2, 4
        )(edges, *row_strips)
        edge_strips = exchange(odd, even, "col")
        up_mid, down_mid, odd_in, even_in = call(fold_mid_kernel, [strip_mid] * 4, 4)(
            edges_mid, *inner_strips
        )
        inner_strips = exchange(odd_in, even_in, "row")
        up, down, odd, even = call(total_kernel, [strip] * 4, 4)(edges, *edge_strips)
        row_strips = exchange(odd, even, "row")
        if iteration < ITERS - 1:
            outs = pieces + [band_rows] * 2
        else:
            outs = [f32(planes, blocks, rim, LANES)] * 2 + [
                f32(planes, blocks, 2 * rim, LANES),
                *pieces[6:],
                packed_mid,
                packed_mid,
            ]
        field, *grads = call(
            next_kernel, [field_shape] + outs, 20, scratch=work, scalars=scalars
        )(
            field, up, down, up_mid, down_mid, left, mid, right,
            *mid_strips, *row_strips, *inner_strips, amps, probe, *tables,
        )

    odd, even, edges, left, mid, right, band_odd, band_even = grads
    row_strips = exchange(odd, even, "row")
    mid_strips = exchange(band_odd, band_even, "col")
    odd, even = call(last_fold_kernel, [packed_edge] * 2, 4)(edges, *row_strips)
    edge_strips = exchange(odd, even, "col")
    whole = pltpu.HBM((planes, tile_r, tile_c), jnp.float32)
    (out,) = call(
        finish_mid_kernel,
        [whole],
        4,
        scratch=[f32(planes, band, tile_c), pltpu.SemaphoreType.DMA(())],
        in_hbm=True,
    )(field, left, mid, right, *mid_strips)
    (out,) = call(
        finish_edge_kernel,
        [whole],
        4,
        scratch=[f32(planes, 2 * rim, tile_c)] + [pltpu.SemaphoreType.DMA(())] * 2,
        raw=[out],
        in_hbm=True,
        alias={6: 0},
    )(field, edges, *row_strips, *edge_strips)
    return out.reshape(object_slices.shape)


def solution(mesh):
    in_specs = (
        P(None, None, "row", "col"),
        P(),
        P("row", "col", None, None, None),
        P(None, "row", "col", None),
        P("row", "col"),
    )
    out_specs = P(None, None, "row", "col")

    return jax.shard_map(body, mesh=mesh, in_specs=in_specs, out_specs=out_specs, check_vma=False)
```

```python
import math

import jax
import jax.numpy as jnp
import ml_dtypes
import numpy as np
from jax import lax
from jax.experimental import pallas as pl
from jax.experimental.pallas import tpu as pltpu
from jax.sharding import PartitionSpec as P

ITERS = 2
LANES = 128
GROUP = 8
BATCH = 4

modulus_offset = 0.5
fresnel_scale = 0.9


def split_table(table):
    high = table.astype(np.float32).astype(ml_dtypes.bfloat16)
    low = (table - high.astype(np.float64)).astype(np.float32).astype(ml_dtypes.bfloat16)
    return high, low


def transform_tables(frame_size):
    positions = np.arange(frame_size)
    dft = np.exp(-2j * math.pi * (positions[:, None] * positions[None, :] % frame_size) / frame_size)
    dft = dft / math.sqrt(frame_size)
    frequency = np.where(positions < frame_size // 2, positions, positions - frame_size)
    phase = np.exp(1j * math.pi * fresnel_scale * frequency.astype(np.float64) ** 2 / frame_size)
    hop = (np.conj(dft) * phase[None, :]) @ dft
    half = frame_size // 2
    hop_parts = ((hop[:half, :half] + hop[:half, half:]) / 2, (hop[:half, :half] - hop[:half, half:]) / 2)
    into = (dft[0::2, :half], dft[1::2, :half])
    out_of = (np.conj(dft[:half, 0::2]), np.conj(dft[:half, 1::2]))
    rights, lefts = [], []
    for matrix in (dft, np.conj(dft), hop, np.conj(hop)):
        rights.extend(
            split_table(np.block([[matrix.real, matrix.imag], [-matrix.imag, matrix.real]]))
        )
    for parts in (into, out_of, hop_parts, np.conj(hop_parts)):
        for part in parts:
            lefts.append(
                np.concatenate(
                    split_table(np.block([[part.real, -part.imag], [part.imag, part.real]]))
                )
            )
    return np.stack(rights), np.stack(lefts)


DFT, INVERSE, HOP, HOP_BACK = 0, 1, 2, 3


def exchange(odd_values, even_values, axis):
    count = lax.axis_size(axis)
    received = []
    for values, first in ((odd_values, 1), (even_values, 0)):
        lower = range(first, count - 1, 2)
        pairs = [(i, i + 1) for i in lower] + [(i + 1, i) for i in lower]
        received.append(lax.ppermute(values, axis, pairs))
    return received


def paired(axis, before, after):
    even = lax.rem(lax.axis_index(axis), 2) == 0
    return jnp.where(even, before, after), jnp.where(even, after, before)


def lane_ids(shape):
    return lax.broadcasted_iota(jnp.int32, shape, len(shape) - 1)


def swap_halves(values):
    return pltpu.roll(values, LANES // 2, values.ndim - 1)


def vmem():
    return pl.BlockSpec(memory_space=pltpu.VMEM)


def smem():
    return pl.BlockSpec(memory_space=pltpu.SMEM)


def split(values):
    high = values.astype(jnp.bfloat16)
    return high, (values - high.astype(jnp.float32)).astype(jnp.bfloat16)


def dot(a, b):
    return jnp.dot(a, b, preferred_element_type=jnp.float32)


def blend(first, second):
    return jnp.where(lane_ids(first.shape) < LANES // 2, first, second)


def segments(rows, rim):
    half = rows // 2
    return ((slice(0, rim), slice(rows - rim, rows)), (slice(rim, half), slice(half, rows - rim)))


def pack_kernel(*refs):
    count = (len(refs) - 11) // 2
    sources, outs, targets = refs[: count + 1], refs[count + 1 : count + 8], refs[count + 8 : -3]
    turned_ref, odd_edge, even_edge, odd_mid, even_mid, row_odd, row_even = outs
    object_ref, plane_sems, sems = refs[-3:]
    planes, rows, cols = object_ref.shape
    plane_copies = [
        pltpu.make_async_copy(sources[0].at[plane], object_ref.at[plane], plane_sems.at[plane])
        for plane in range(planes)
    ]
    copies = [
        pltpu.make_async_copy(source, target, sems.at[at])
        for at, (source, target) in enumerate(zip(sources[1:], targets))
    ]
    for copy in plane_copies + copies:
        copy.start()
    tiles = cols // LANES
    pieces = segments(rows, odd_edge.shape[1])
    for plane in range(planes):
        plane_copies[plane].wait()
        for (upper, lower), odd_ref, even_ref in zip(
            pieces, (odd_edge, odd_mid), (even_edge, even_mid)
        ):
            left = blend(
                object_ref[plane, lower, 0:LANES], swap_halves(object_ref[plane, upper, 0:LANES])
            )
            right = blend(
                swap_halves(object_ref[plane, upper, cols - LANES : cols]),
                object_ref[plane, lower, cols - LANES : cols],
            )
            odd_ref[plane], even_ref[plane] = paired("col", left, right)
        for tile in range(tiles):
            turned = swap_halves(object_ref[plane, :, tile * LANES : (tile + 1) * LANES])
            turned_ref[plane, tile] = turned
            upper, lower = pieces[0]
            row_odd[plane, tile], row_even[plane, tile] = paired("row", turned[upper], turned[lower])
    for copy in copies:
        copy.wait()


def lay(turned_ref, plane, rows, left, right, field_ref, row_at):
    tiles = turned_ref.shape[1]
    parts = [left] + [turned_ref[plane, tile, rows, :] for tile in range(tiles)] + [right]
    for block in range(tiles + 1):
        field_ref[plane, block, row_at : row_at + rows.stop - rows.start, :] = blend(
            parts[block], parts[block + 1]
        )


def corner_kernel(from_odd, from_even, odd_ref, even_ref):
    for plane in range(odd_ref.shape[0]):
        left, right = paired("col", from_odd[plane], from_even[plane])
        odd_ref[plane], even_ref[plane] = paired(
            "row", blend(left, right), swap_halves(blend(right, left))
        )


def gradients(pos_ref, count_ref, amps_ref, probe_ref, rights_ref, lefts_ref, field_ref, grad_ref, work):
    frame = probe_ref.shape[-1]
    o0, o1, inc, wave = work
    count = count_ref[0, 0]
    first_row = lax.axis_index("row") * (field_ref.shape[2] - frame)
    first_col = lax.axis_index("col") * ((field_ref.shape[1] - 1) * LANES)
    lanes = lane_ids((frame, LANES))

    grad_ref[...] = jnp.zeros_like(grad_ref)

    half = frame // 2

    def right(source, kind):
        table_high, table_low = rights_ref[2 * kind], rights_ref[2 * kind + 1]
        high, low = split(source)
        out = dot(jnp.concatenate([high, low], axis=0), table_high)
        return out[: high.shape[0]] + out[high.shape[0] :] + dot(high, table_low)

    def left(re, im, kind):
        upper, lower = (re[:half], im[:half]), (re[half:], im[half:])
        if kind != INVERSE:
            upper, lower = (
                [a + b for a, b in zip(upper, lower)], [a - b for a, b in zip(upper, lower)]
            )
        sides = []
        for side, (side_re, side_im) in enumerate((upper, lower)):
            table = lefts_ref[2 * kind + side]
            high, low = split(jnp.concatenate([side_re, side_im], axis=0))
            out = dot(
                jnp.concatenate([table, table], axis=1), jnp.concatenate([high, low], axis=0)
            )
            out = out[:frame] + out[frame:]
            sides.append((out[:half], out[half:]))
        upper, lower = sides
        if kind != DFT:
            upper, lower = (
                [a + b for a, b in zip(upper, lower)], [a - b for a, b in zip(upper, lower)]
            )
        return [jnp.concatenate([a, b], axis=0) for a, b in zip(upper, lower)]

    def two_sided(zs, kind):
        outs = []
        for first in range(0, len(zs), BATCH):
            rows = [jnp.concatenate(z, axis=1) for z in zs[first : first + BATCH]]
            out = right(jnp.concatenate(rows, axis=0), kind)
            outs.extend(out[at : at + 2 * frame] for at in range(0, BATCH * frame, 2 * frame))
        mixes = [
            left(
                jnp.concatenate([out[:frame, :frame], out[frame:, :frame]], axis=1),
                jnp.concatenate([out[:frame, frame:], out[frame:, frame:]], axis=1),
                kind,
            )
            for out in outs
        ]
        return [
            (re[:, k * frame : (k + 1) * frame], im[:, k * frame : (k + 1) * frame])
            for re, im in mixes
            for k in range(2)
        ]

    def group_step(group, carry):
        base = group * GROUP
        where = []
        for k in range(GROUP):
            row_at = pos_ref[0, 0, 0, base + k] - first_row
            col_at = pos_ref[1, 0, 0, base + k] - first_col
            block = lax.shift_right_logical(col_at, 7)
            shift = jnp.bitwise_and(col_at, LANES - 1)
            where.append((pl.ds(row_at, frame), block, shift))
            for plane in range(4):
                near = field_ref[plane, block, pl.ds(row_at, frame), :]
                far = field_ref[plane, block + 1, pl.ds(row_at, frame), :]
                joined = jnp.where(lanes >= shift, near, far)
                target = o0 if plane < 2 else o1
                target[k, plane % 2] = pltpu.roll(
                    joined, jnp.bitwise_and(LANES - shift, LANES - 1), 1
                )
        probe_re, probe_im = probe_ref[0], probe_ref[1]
        zs = []
        for k in range(GROUP):
            a, b = o0[k, 0], o0[k, 1]
            zs.append((probe_re * a - probe_im * b, probe_re * b + probe_im * a))
        for k, (re, im) in enumerate(two_sided(zs, HOP)):
            inc[k, 0] = re
            inc[k, 1] = im
        zs = []
        for k in range(GROUP):
            a, b, c, d = inc[k, 0], inc[k, 1], o1[k, 0], o1[k, 1]
            zs.append((a * c - b * d, a * d + b * c))
        for k, (re, im) in enumerate(two_sided(zs, DFT)):
            live = jnp.where(base + k < count, 1.0, 0.0)
            amps = jnp.concatenate(
                [amps_ref[base + k, pl.ds(odd, half, stride=2), :] for odd in range(2)], axis=0
            )
            factor = (1.0 - amps * lax.rsqrt(re * re + im * im + modulus_offset)) * live
            wave[k, 0] = re * factor
            wave[k, 1] = im * factor
        zs = [(wave[k, 0], wave[k, 1]) for k in range(GROUP)]

        def place(k, first_plane, values):
            rows, block, shift = where[k]
            for part in range(2):
                moved = pltpu.roll(values[part], shift, 1)
                near = jnp.where(lanes >= shift, moved, 0.0)
                far = jnp.where(lanes >= shift, 0.0, moved)
                grad_ref[first_plane + part, block, rows, :] += near
                grad_ref[first_plane + part, block + 1, rows, :] += far

        for k, (re, im) in enumerate(two_sided(zs, INVERSE)):
            wave[k, 0] = re
            wave[k, 1] = im
        zs = []
        for k in range(GROUP):
            re, im = wave[k, 0], wave[k, 1]
            a, b, c, d = inc[k, 0], inc[k, 1], o1[k, 0], o1[k, 1]
            place(k, 2, (a * re + b * im, a * im - b * re))
            zs.append((c * re + d * im, c * im - d * re))
        for k, (re, im) in enumerate(two_sided(zs, HOP_BACK)):
            place(k, 0, (probe_re * re + probe_im * im, probe_re * im - probe_im * re))
        return carry

    lax.fori_loop(0, (count + GROUP - 1) // GROUP, group_step, 0)


def outer(blocks):
    return (0, blocks - 1)


def inner(blocks):
    return range(1, blocks - 1)


def write_grad(grad_ref, pieces):
    left, mid, right, band_odd, band_even = pieces[-5:]
    _, blocks, all_rows, _ = grad_ref.shape
    rim = pieces[0].shape[-2]
    rows = all_rows - 2 * rim
    if len(pieces) == 8:
        row_odd, row_even, edges = pieces[:3]
        groups = [(row_odd, row_even, edges, [(0, blocks - 1), (blocks - 1, 0), *inner(blocks)])]
    else:
        row_odd, row_even, row_mid_odd, row_mid_even, edges, edges_mid = pieces[:6]
        groups = [
            (row_odd, row_even, edges, outer(blocks)),
            (row_mid_odd, row_mid_even, edges_mid, inner(blocks)),
        ]

    def rows_of(block, lo):
        if isinstance(block, tuple):
            return blend(*[grad_ref[:, part, lo : lo + rim, :] for part in block])
        return grad_ref[:, block, lo : lo + rim, :]

    for odd, even, edge, group in groups:
        for at, block in enumerate(group):
            odd[:, at], even[:, at] = paired("row", rows_of(block, 0), rows_of(block, rows + rim))
            edge[:, at, 0:rim, :] = rows_of(block, rim)
            edge[:, at, rim : 2 * rim, :] = rows_of(block, rows)
    left[...] = grad_ref[:, 0, 2 * rim : rows, :]
    mid[...] = grad_ref[:, 1 : blocks - 1, 2 * rim : rows, :]
    right[...] = grad_ref[:, blocks - 1, 2 * rim : rows, :]
    if band_odd.shape[1] == rows - 2 * rim:
        band_odd[...], band_even[...] = paired("col", left[...], right[...])
    else:
        half = (rows - 2 * rim) // 2
        upper, lower = slice(2 * rim, 2 * rim + half), slice(2 * rim + half, rows)
        pack_bands(grad_ref, (band_odd, band_even), upper, lower)


def pack_bands(ref, packed, upper, lower):
    last = ref.shape[1] - 1
    for plane in range(ref.shape[0]):
        packed[0][plane], packed[1][plane] = paired(
            "col",
            blend(ref[plane, 0, upper, :], swap_halves(ref[plane, 0, lower, :])),
            blend(swap_halves(ref[plane, last, lower, :]), ref[plane, last, upper, :]),
        )


def first_kernel(
    pos_ref, count_ref, turned_ref, edge_odd, edge_even, mid_odd, mid_even, row_odd, row_even,
    corner_odd, corner_even, amps_ref, probe_ref, rights_ref, lefts_ref, field_ref, *rest,
):
    pieces, (grad_ref, *work) = rest[:-5], rest[-5:]
    planes, _, rows, _ = turned_ref.shape
    rim = edge_odd.shape[1]
    for plane in range(planes):
        for (upper, lower), odd, even in zip(
            segments(rows, rim), (edge_odd, mid_odd), (edge_even, mid_even)
        ):
            left, right = paired("col", odd[plane], even[plane])
            lay(turned_ref, plane, upper, left, right, field_ref, rim + upper.start)
            left, right = swap_halves(left), swap_halves(right)
            lay(turned_ref, plane, lower, left, right, field_ref, rim + lower.start)
        corners = paired("row", corner_odd[plane], corner_even[plane])
        rims = paired("row", row_odd[plane], row_even[plane])
        for strip, corner, row_at in zip(rims, corners, (0, rows + rim)):
            parts = [corner, *strip, corner]
            for block in range(len(parts) - 1):
                field_ref[plane, block, row_at : row_at + rim, :] = blend(
                    parts[block], parts[block + 1]
                )
    gradients(pos_ref, count_ref, amps_ref, probe_ref, rights_ref, lefts_ref, field_ref, grad_ref, work)
    write_grad(grad_ref, pieces)


def fold(edges, row_odd, row_even, plane, at):
    rim = row_odd.shape[2]
    from_up, from_down = paired("row", row_odd[plane, at], row_even[plane, at])
    return edges[plane, at, 0:rim, :] + from_up, edges[plane, at, rim : 2 * rim, :] + from_down


def fold_kernel(edges, row_odd, row_even, folded_ref, odd_ref, even_ref):
    planes, count = edges.shape[:2]
    rim = row_odd.shape[2]
    for plane in range(planes):
        for at in range(count):
            upper, lower = fold(edges, row_odd, row_even, plane, at)
            folded_ref[plane, at, 0:rim, :] = upper
            folded_ref[plane, at, rim : 2 * rim, :] = lower
    odd_ref[...], even_ref[...] = paired("col", folded_ref[:, 0], folded_ref[:, count - 1])


def last_fold_kernel(edges, row_odd, row_even, odd_ref, even_ref):
    for plane in range(edges.shape[0]):
        upper, lower = fold(edges, row_odd, row_even, plane, 0)
        lower = swap_halves(lower)
        odd_ref[plane], even_ref[plane] = paired("col", blend(upper, lower), blend(lower, upper))


def fold_mid_kernel(edges, row_odd, row_even, up_ref, down_ref, odd_ref, even_ref):
    for plane in range(edges.shape[0]):
        for at in range(edges.shape[1]):
            upper, lower = fold(edges, row_odd, row_even, plane, at)
            up_ref[plane, at], down_ref[plane, at] = upper, lower
            odd_ref[plane, at], even_ref[plane, at] = paired("row", upper, lower)


def total_kernel(folded_ref, from_odd, from_even, up_ref, down_ref, odd_ref, even_ref):
    planes, count, rim, _ = up_ref.shape
    for plane in range(planes):
        sides = paired("col", from_odd[plane], from_even[plane])
        for at in range(count):
            values = folded_ref[plane, at] + sides[at]
            upper, lower = values[0:rim], values[rim : 2 * rim]
            up_ref[plane, at], down_ref[plane, at] = upper, lower
            odd_ref[plane, at], even_ref[plane, at] = paired("row", upper, lower)


def next_kernel(
    pos_ref, count_ref, old_ref, up_ref, down_ref, up_mid, down_mid, left_ref, mid_ref, right_ref,
    from_odd, from_even, row_odd, row_even, row_mid_odd, row_mid_even,
    amps_ref, probe_ref, rights_ref, lefts_ref, field_ref, *rest,
):
    pieces, (grad_ref, *work) = rest[:-5], rest[-5:]
    _, blocks, all_rows, _ = old_ref.shape
    rim = up_ref.shape[2]
    rows = all_rows - 2 * rim
    from_left, from_right = paired("col", from_odd[...], from_even[...])
    for block in range(blocks):
        lane = lane_ids((1, 1, LANES))
        inside = lane >= 0
        if block in inner(blocks):
            at, odd, even, up, down = block - 1, row_mid_odd, row_mid_even, up_mid, down_mid
            middle = mid_ref[:, at]
        elif block == 0:
            at, odd, even, up, down = 0, row_odd, row_even, up_ref, down_ref
            inside = lane >= jnp.where(lax.axis_index("col") == 0, LANES // 2, 0)
            middle = left_ref[...] + from_left
        else:
            at, odd, even, up, down = 1, row_odd, row_even, up_ref, down_ref
            at_end = lax.axis_index("col") == lax.axis_size("col") - 1
            inside = lane < jnp.where(at_end, LANES // 2, LANES)
            middle = right_ref[...] + from_right
        from_up, from_down = paired("row", odd[:, at], even[:, at])
        for lo, hi, values in (
            (0, rim, from_up),
            (rim, 2 * rim, up[:, at]),
            (2 * rim, rows, middle),
            (rows, rows + rim, down[:, at]),
            (rows + rim, all_rows, from_down),
        ):
            updated = old_ref[:, block, lo:hi, :] - values
            field_ref[:, block, lo:hi, :] = jnp.where(inside, updated, 0.0)
    gradients(pos_ref, count_ref, amps_ref, probe_ref, rights_ref, lefts_ref, field_ref, grad_ref, work)
    write_grad(grad_ref, pieces)


def put_rows(field_ref, plane, row_at, values, sides, part, target_ref, put_at):
    size = values[0].shape[0]
    if part == 1:
        sides = [swap_halves(side) for side in sides]
    values = [values[0] + sides[0], *values[1:-1], values[-1] + sides[1]]
    turned = [
        swap_halves(field_ref[plane, block, row_at : row_at + size, :] - block_values)
        for block, block_values in enumerate(values)
    ]
    for block in range(len(turned) - 1):
        target_ref[plane, put_at : put_at + size, block * LANES : (block + 1) * LANES] = blend(
            turned[block], turned[block + 1]
        )


def finish_mid_kernel(
    field_ref, left_ref, mid_ref, right_ref, from_odd, from_even, out_hbm, result, sem
):
    planes, blocks, all_rows, _ = field_ref.shape
    band = result.shape[1]
    rim = (all_rows - band) // 4
    half = band // 2
    for plane in range(planes):
        sides = paired("col", from_odd[plane], from_even[plane])
        for part in range(2):
            at = slice(part * half, (part + 1) * half)
            values = [left_ref[plane, at, :], right_ref[plane, at, :]]
            values[1:1] = [mid_ref[plane, k, at, :] for k in range(blocks - 2)]
            put_rows(
                field_ref, plane, 2 * rim + part * half, values, sides, part, result, part * half
            )
    copy = pltpu.make_async_copy(result, out_hbm.at[:, rim : rim + band, :], sem)
    copy.start()
    copy.wait()


def finish_edge_kernel(
    field_ref, edges, row_odd, row_even, from_odd, from_even, _, out_hbm, result, *sems
):
    planes, blocks, all_rows, _ = field_ref.shape
    rim = from_odd.shape[1]
    rows = all_rows - 2 * rim
    copies = []
    for part in range(2):
        for plane in range(planes):
            sides = paired("col", from_odd[plane], from_even[plane])
            folded = [fold(edges, row_odd, row_even, plane, k)[part] for k in range(1, blocks)]
            values = [*folded, folded[0]]
            put_rows(
                field_ref, plane, rim + part * (rows - rim), values, sides, part, result, part * rim
            )
        at = part * (rows - rim)
        copies.append(
            pltpu.make_async_copy(
                result.at[:, part * rim : (part + 1) * rim, :],
                out_hbm.at[:, at : at + rim, :],
                sems[part],
            )
        )
        copies[-1].start()
    for copy in copies:
        copy.wait()


def f32(*shape):
    return pltpu.VMEM(shape, jnp.float32)


def on_chip(*arrays):
    return [pltpu.with_memory_space_constraint(array, pltpu.VMEM) for array in arrays]


def body(object_slices, probe, amplitudes, scan_pos, scan_count):
    layers, _, tile_r, tile_c = object_slices.shape
    planes = layers * 2
    frame = probe.shape[-1]
    rim = frame // 2
    blocks = tile_c // LANES + 1
    slots = amplitudes.shape[2]
    assert slots % GROUP == 0
    amps = amplitudes[0, 0]
    scalars = [scan_pos, scan_count]
    tables = [jnp.asarray(table) for table in transform_tables(frame)]
    tile = object_slices.reshape(planes, tile_r, tile_c)

    band = tile_r - 2 * rim

    def call(kernel, outs, mib, scratch=(), scalars=(), raw=(), in_hbm=False, alias=None):
        def run(*arrays):
            return pl.pallas_call(
                kernel,
                out_shape=outs,
                input_output_aliases=alias or {},
                in_specs=[smem()] * len(scalars) + [vmem()] * len(arrays)
                + [pl.BlockSpec(memory_space=pltpu.HBM)] * len(raw),
                out_specs=[pl.BlockSpec(memory_space=pltpu.HBM) if in_hbm else vmem()] * len(outs),
                scratch_shapes=list(scratch),
                compiler_params=pltpu.CompilerParams(vmem_limit_bytes=mib << 20),
            )(
                *scalars,
                *on_chip(*arrays),
                *[pltpu.with_memory_space_constraint(array, pltpu.HBM) for array in raw],
            )

        return run

    packed_edge = f32(planes, rim, LANES)
    packed_mid = f32(planes, band // 2, LANES)
    row_strip = f32(planes, blocks - 1, rim, LANES)
    constants = (amps, probe, *tables)
    turned, odd_edge, even_edge, odd_mid, even_mid, odd, even, amps, probe, *tables = call(
        pack_kernel,
        [f32(planes, blocks - 1, tile_r, LANES)]
        + [packed_edge] * 2 + [packed_mid] * 2 + [row_strip] * 2
        + [pltpu.VMEM(array.shape, array.dtype) for array in constants],
        8,
        scratch=[
            f32(planes, tile_r, tile_c),
            pltpu.SemaphoreType.DMA((planes,)),
            pltpu.SemaphoreType.DMA((len(constants),)),
        ],
        raw=[tile, *constants],
    )()
    edge_strips = exchange(odd_edge, even_edge, "col")
    row_strips = exchange(odd, even, "row")
    mid_strips = exchange(odd_mid, even_mid, "col")
    odd, even = call(corner_kernel, [packed_edge] * 2, 4)(*edge_strips)
    corner_strips = exchange(odd, even, "row")

    field_shape = f32(planes, blocks, tile_r + frame, LANES)
    work = [field_shape] + [pltpu.VMEM((GROUP, 2, frame, frame), jnp.float32)] * 4
    strip, strip_mid = f32(planes, 2, rim, LANES), f32(planes, blocks - 2, rim, LANES)
    edge_rows = f32(planes, 2, 2 * rim, LANES)
    band_rows = f32(planes, band, LANES)
    pieces = [strip] * 2 + [strip_mid] * 2 + [
        edge_rows,
        f32(planes, blocks - 2, 2 * rim, LANES),
        band_rows,
        f32(planes, blocks - 2, band, LANES),
        band_rows,
    ]
    field, *grads = call(
        first_kernel,
        [field_shape] + pieces + [band_rows] * 2,
        20,
        scratch=work,
        scalars=scalars,
    )(turned, *edge_strips, *mid_strips, *row_strips, *corner_strips, amps, probe, *tables)

    for iteration in range(1, ITERS):
        odd, even, odd_in, even_in, edges, edges_mid, left, mid, right, band_odd, band_even = grads
        row_strips = exchange(odd, even, "row")
        mid_strips = exchange(band_odd, band_even, "col")
        inner_strips = exchange(odd_in, even_in, "row")
        edges, odd, even = call(
            fold_kernel, [edge_rows] + [f32(planes, 2 * rim, LANES)] * 2, 4
        )(edges, *row_strips)
        edge_strips = exchange(odd, even, "col")
        up_mid, down_mid, odd_in, even_in = call(fold_mid_kernel, [strip_mid] * 4, 4)(
            edges_mid, *inner_strips
        )
        inner_strips = exchange(odd_in, even_in, "row")
        up, down, odd, even = call(total_kernel, [strip] * 4, 4)(edges, *edge_strips)
        row_strips = exchange(odd, even, "row")
        if iteration < ITERS - 1:
            outs = pieces + [band_rows] * 2
        else:
            outs = [f32(planes, blocks, rim, LANES)] * 2 + [
                f32(planes, blocks, 2 * rim, LANES),
                *pieces[6:],
                packed_mid,
                packed_mid,
            ]
        field, *grads = call(
            next_kernel, [field_shape] + outs, 20, scratch=work, scalars=scalars
        )(
            field, up, down, up_mid, down_mid, left, mid, right,
            *mid_strips, *row_strips, *inner_strips, amps, probe, *tables,
        )

    odd, even, edges, left, mid, right, band_odd, band_even = grads
    row_strips = exchange(odd, even, "row")
    mid_strips = exchange(band_odd, band_even, "col")
    odd, even = call(last_fold_kernel, [packed_edge] * 2, 4)(edges, *row_strips)
    edge_strips = exchange(odd, even, "col")
    whole = pltpu.HBM((planes, tile_r, tile_c), jnp.float32)
    (out,) = call(
        finish_mid_kernel,
        [whole],
        4,
        scratch=[f32(planes, band, tile_c), pltpu.SemaphoreType.DMA(())],
        in_hbm=True,
    )(field, left, mid, right, *mid_strips)
    (out,) = call(
        finish_edge_kernel,
        [whole],
        4,
        scratch=[f32(planes, 2 * rim, tile_c)] + [pltpu.SemaphoreType.DMA(())] * 2,
        raw=[out],
        in_hbm=True,
        alias={6: 0},
    )(field, edges, *row_strips, *edge_strips)
    return out.reshape(object_slices.shape)


def solution(mesh):
    in_specs = (
        P(None, None, "row", "col"),
        P(),
        P("row", "col", None, None, None),
        P(None, "row", "col", None),
        P("row", "col"),
    )
    out_specs = P(None, None, "row", "col")

    return jax.shard_map(body, mesh=mesh, in_specs=in_specs, out_specs=out_specs, check_vma=False)
```
